32 devices in a mesh: member: 4 (over z), region: 4 (over y, x), fine: 2 (over core).
Axes of the slice: x: 2, y: 2, z: 4, core: 2. Of those that a mesh axis runs over, the one named last changes fastest.
Arguments:
- sample_surface_elevation: float32 [256, 4, 512], P('member', 'region', 'fine'), may hold values from -6 to 6
- sample_zonal_current: float32 [256, 4, 512], P('member', 'region', 'fine'), may hold values from -6 to 6
- sample_meridional_current: float32 [256, 4, 512], P('member', 'region', 'fine'), may hold values from -6 to 6
- zonal_edge_layer_courant: float32 [4, 512], P('region', 'fine'), may hold values from 0.1 to 0.45
- meridional_edge_layer_courant: float32 [4, 512], P('region', 'fine'), may hold values from 0.1 to 0.45
- obs_index: int32 [64, 512, 4], P(('member', 'region', 'fine')), may hold values from 0 to 95
- obs_weight: float32 [64, 512, 4], P(('member', 'region', 'fine')), may hold values from 0.1 to 1
- obs_value: float32 [64, 512], P(('member', 'region', 'fine')), may hold values from -12 to 12
- obs_var: float32 [64, 512], P(('member', 'region', 'fine')), may hold values from 0.25 to 4
- obs_count: int32 [64], P(('member', 'region', 'fine')), may hold values from 64 to 512, as said below
- fine_ctrl: float32 [3, 8, 2, 512], P(None, 'region', 'fine', 'member'), may hold values from -6 to 6
Outputs:
- ana_h: float32 [256, 4, 512], P('member', 'region', 'fine')
- ana_u: float32 [256, 4, 512], P('member', 'region', 'fine')
- ana_v: float32 [256, 4, 512], P('member', 'region', 'fine')
- fine_out: float32 [3, 8, 2, 512], P(None, 'region', 'fine', 'member')
The draws below stay inside these ranges and needn't reach their ends.
Inputs may be any that keep to these rules, and one draw needn't show every extreme that they name: `obs_count`: each region's count is 512 // 8 times 1, 2, 4 or 8; some region has 512 and some 512 // 8 in every draw; the live observations of a region are its first count slots.
All inputs are finite; a program needn't handle non-finite values.
Results may differ from the reference program's by a relative error of at most 0.0003.
Values sent between devices are 32-bit elements; how exact they have to be, the bound alone decides.
No kernel may reach another device: no remote copies, remote signals or barrier semaphores. Data moves between devices by JAX's collectives and lax.ppermute only.
A program may use at most 64 MiB of HBM per device.

```python
import math
import jax
import jax.numpy as jnp
from jax import lax

K = 256
ROWS_DEV = 1
RCOLS = 16
REG_DEV = 2
NOBS = 512
STEPS = 4
NEWTON = 8
NY = 4
NX = 512
CELLS_REG = 32
NREG = 64
FNY = 8
FNX = 1024
N_MEMBER = 4
N_REGION = 4
N_FINE = 2


def draw_obs_count(key, part):
    key_pick = jax.random.fold_in(key, 11)
    key_order = jax.random.fold_in(key, 23)
    pick = jax.random.randint(key_pick, (NREG,), 0, 4)
    table = jnp.array([1, 2, 4, 8], dtype=jnp.int32)
    counts = NOBS // 8 * jnp.take(table, pick)
    order = jax.random.permutation(key_order, NREG)
    counts = counts.at[order[0]].set(NOBS)
    counts = counts.at[order[1]].set(NOBS // 8)
    return counts.astype(jnp.int32)


def touch_ends(drawn, stream_key, least, largest):
    place = [jax.random.randint(jax.random.fold_in(stream_key, axis), (), 0, length) for axis, length in enumerate(drawn.shape)]
    main_axis = drawn.shape.index(max(drawn.shape))
    next_to = place[:main_axis] + [(place[main_axis] + 1) % drawn.shape[main_axis]] + place[main_axis + 1:]
    return drawn.at[tuple(place)].set(least).at[tuple(next_to)].set(largest)


def block_scale(own_key, shape, cuts, least, largest):
    level, own = 1.0, jax.random.fold_in(own_key, 6)
    for dim, blocks in cuts:
        draws = jnp.exp(jax.random.uniform(jax.random.fold_in(own, dim), (blocks,), jnp.float32, least / len(cuts), largest / len(cuts)))
        level = level * jnp.repeat(draws, shape[dim] // blocks).reshape([-1 if axis == dim else 1 for axis in range(len(shape))])
    return level


def scatter_about(key, extent, deviation, limit, shards=(), kind=jnp.bfloat16):
    level = block_scale(key, extent, shards, -0.22, 0.18) if shards else 1.0
    values = jax.random.normal(key, extent, jnp.float32) * deviation * level
    return jnp.minimum(jnp.maximum(values, -limit), limit).astype(kind)


def setup_inputs(seed: int = 0) -> dict:
    arg_keys = jax.random.split(jax.random.key(seed), 12)
    sample_surface_elevation = scatter_about(arg_keys[0], (K, NY, NX), 1.0, 6.0, ((0, 4), (1, 4), (2, 2)), jnp.float32)
    sample_zonal_current = scatter_about(arg_keys[1], (K, NY, NX), 1.0, 6.0, ((0, 4), (1, 4), (2, 2)), jnp.float32)
    sample_meridional_current = scatter_about(arg_keys[2], (K, NY, NX), 1.0, 6.0, ((0, 4), (1, 4), (2, 2)), jnp.float32)
    zonal_edge_layer_courant = jnp.clip(jnp.exp(math.log(0.45) - 1.50407736 * jax.random.uniform(arg_keys[3], (NY, NX), jnp.float32) ** block_scale(arg_keys[3], (NY, NX), ((0, 4), (1, 2)), -0.2, 0.2)), 0.1, 0.45)
    meridional_edge_layer_courant = jnp.clip(jnp.exp(math.log(0.45) - 1.50407736 * jax.random.uniform(arg_keys[4], (NY, NX), jnp.float32) ** block_scale(arg_keys[4], (NY, NX), ((0, 4), (1, 2)), -0.2, 0.2)), 0.1, 0.45)
    obs_index = touch_ends(jax.random.randint(arg_keys[5], (NREG, NOBS, 4), 0, 3 * CELLS_REG), jax.random.fold_in(arg_keys[5], 1), 0, (3 * CELLS_REG) - 1).astype(jnp.int32)
    obs_weight = jnp.clip(jnp.exp(math.log(1.0) - 2.3025851 * jax.random.uniform(arg_keys[6], (NREG, NOBS, 4), jnp.float32) ** block_scale(arg_keys[6], (NREG, NOBS, 4), ((0, 32),), -0.2, 0.2)), 0.1, 1.0)
    obs_value = scatter_about(arg_keys[7], (NREG, NOBS), 2.0, 12.0, ((0, 32),), jnp.float32)
    obs_var = jnp.clip(jnp.exp(math.log(4.0) - 2.7725887 * jax.random.uniform(arg_keys[8], (NREG, NOBS), jnp.float32) ** block_scale(arg_keys[8], (NREG, NOBS), ((0, 32),), -0.2, 0.2)), 0.25, 4.0)
    obs_count = draw_obs_count(jax.random.fold_in(arg_keys[11], 71), 0)
    fine_ctrl = scatter_about(arg_keys[10], (3, FNY, N_FINE, FNX // N_FINE), 1.0, 6.0, ((1, 4), (2, 2), (3, 4)), jnp.float32)
    return dict(sample_surface_elevation=sample_surface_elevation, sample_zonal_current=sample_zonal_current, sample_meridional_current=sample_meridional_current, zonal_edge_layer_courant=zonal_edge_layer_courant, meridional_edge_layer_courant=meridional_edge_layer_courant, obs_index=obs_index, obs_weight=obs_weight, obs_value=obs_value, obs_var=obs_var, obs_count=obs_count, fine_ctrl=fine_ctrl)


HIGHEST = lax.Precision.HIGHEST

def propagate_trajectories(sample_surface_elevation, sample_zonal_current, sample_meridional_current, zonal_edge_layer_courant, meridional_edge_layer_courant):
    for pass_no in range(STEPS):
        flux_u = zonal_edge_layer_courant * sample_zonal_current
        flux_v = meridional_edge_layer_courant * sample_meridional_current
        south_flux = jnp.concatenate([jnp.zeros_like(flux_v[:, :1]), flux_v[:, :-1]], axis=1)
        sample_surface_elevation = sample_surface_elevation - (flux_u - jnp.roll(flux_u, 1, axis=2) + flux_v - south_flux)
        north_rows = jnp.concatenate([sample_surface_elevation[:, 1:], jnp.zeros_like(sample_surface_elevation[:, :1])], axis=1)
        sample_zonal_current = sample_zonal_current - (jnp.roll(sample_surface_elevation, -1, axis=2) - sample_surface_elevation)
        sample_meridional_current = sample_meridional_current - (north_rows - sample_surface_elevation)
    return (sample_surface_elevation, sample_zonal_current, sample_meridional_current)

def to_regions(field):
    shaped = field.reshape(K, REG_DEV, N_REGION // REG_DEV, ROWS_DEV, N_FINE, N_MEMBER, N_REGION, RCOLS)
    shaped = shaped.transpose(5, 6, 4, 1, 0, 2, 3, 7)
    return shaped.reshape(NREG, K, CELLS_REG)

def from_regions(blocks):
    shaped = blocks.reshape(N_MEMBER, N_REGION, N_FINE, REG_DEV, K, N_REGION // REG_DEV, ROWS_DEV, RCOLS)
    shaped = shaped.transpose(4, 3, 5, 6, 2, 0, 1, 7)
    return shaped.reshape(K, NY, NX)

def increment_grid(blocks):
    shaped = blocks.reshape(N_MEMBER, N_REGION, N_FINE, REG_DEV, N_REGION // REG_DEV, ROWS_DEV, RCOLS)
    shaped = shaped.transpose(3, 4, 5, 2, 0, 1, 6)
    return shaped.reshape(NY, NX)

def analyse(packed):
    ensemble, region_index, region_weight, region_value, region_var, region_count = packed
    mean_state = lax.optimization_barrier(jnp.mean(ensemble, axis=0))
    spread = ensemble - mean_state
    picked = ensemble[:, region_index]
    predicted = lax.optimization_barrier(jnp.sum(picked * region_weight, axis=2))
    mean_obs = lax.optimization_barrier(jnp.mean(predicted, axis=0))
    obs_spread = predicted - mean_obs
    active_obs = (jnp.arange(NOBS) < region_count).astype(jnp.float32)
    weighted = obs_spread * (active_obs / region_var)
    gram_sum = jnp.dot(weighted, obs_spread.T, precision=HIGHEST)
    identity = jnp.eye(K, dtype=jnp.float32)
    scaled = identity + gram_sum / (K - 1)
    frobenius = jnp.sqrt(jnp.sum(scaled * scaled))
    iterate = scaled / frobenius
    inverse_root = identity
    for sweep in range(NEWTON):
        factor = 1.5 * identity - 0.5 * jnp.dot(inverse_root, iterate, precision=HIGHEST)
        iterate = jnp.dot(iterate, factor, precision=HIGHEST)
        inverse_root = jnp.dot(factor, inverse_root, precision=HIGHEST)
    transform = inverse_root / jnp.sqrt(frobenius)
    innovation = jnp.dot(region_value - mean_obs, weighted.T, precision=HIGHEST)
    halfway = jnp.dot(transform, innovation, precision=HIGHEST)
    mean_weights = jnp.dot(transform, halfway, precision=HIGHEST) / (K - 1)
    increment = jnp.dot(mean_weights, spread, precision=HIGHEST)
    members = (mean_state + increment)[None, :] + jnp.dot(transform.T, spread, precision=HIGHEST)
    return (members, increment)

def reference(sample_surface_elevation, sample_zonal_current, sample_meridional_current, zonal_edge_layer_courant, meridional_edge_layer_courant, obs_index, obs_weight, obs_value, obs_var, obs_count, fine_ctrl):
    prognostic_quantities = propagate_trajectories(sample_surface_elevation, sample_zonal_current, sample_meridional_current, zonal_edge_layer_courant, meridional_edge_layer_courant)
    ensemble = jnp.concatenate([to_regions(field) for field in prognostic_quantities], axis=2)
    members, increment = lax.map(analyse, (ensemble, obs_index, obs_weight, obs_value, obs_var, obs_count))
    outputs = [from_regions(members[:, :, vari * CELLS_REG:(vari + 1) * CELLS_REG]) for vari in range(3)]
    grids = jnp.stack([increment_grid(increment[:, vari * CELLS_REG:(vari + 1) * CELLS_REG]) for vari in range(3)])
    widened = jnp.repeat(jnp.repeat(grids, 2, axis=1), 2, axis=2)
    fine_out = fine_ctrl + widened.reshape(fine_ctrl.shape)
    return (outputs[0], outputs[1], outputs[2], fine_out)
```

```python
import functools

import jax
import jax.numpy as jnp
from jax import lax
from jax.experimental import pallas as pl
from jax.experimental.pallas import tpu as pltpu
from jax.sharding import PartitionSpec as P

REG_DEV = 2
STEPS = 4
NEWTON = 8
LANES = 128
TILE = 8
HALF = LANES // 2

HIGHEST = lax.Precision.HIGHEST
NT = (((1,), (1,)), ((), ()))
NN = (((1,), (0,)), ((), ()))
VMEM = pl.BlockSpec(memory_space=pltpu.VMEM)
SMEM = pl.BlockSpec(memory_space=pltpu.SMEM)


def passed_along(block, axis, distance):
    count = lax.axis_size(axis)
    route = [((i - distance) % count, i) for i in range(count)]
    return lax.ppermute(block, axis, route)


def lane_of(shape):
    return lax.broadcasted_iota(jnp.int32, shape, 1)


def row_of(shape):
    return lax.broadcasted_iota(jnp.int32, shape, 0)


def swapped(tile):
    return pltpu.roll(tile, HALF, 1)


def low_pair(even, odd):
    return jnp.where(lane_of(even.shape) < HALF, even, swapped(odd))


def high_pair(even, odd):
    return jnp.where(lane_of(even.shape) < HALF, swapped(even), odd)


def split(value):
    high = value.astype(jnp.bfloat16)
    return high, (value - high.astype(jnp.float32)).astype(jnp.bfloat16)


def product(left, right, dims=NN):
    left_high, left_low = split(left)
    right_high, right_low = split(right)
    dot = functools.partial(
        lax.dot_general, dimension_numbers=dims, preferred_element_type=jnp.float32
    )
    return dot(left_high, right_high) + (dot(left_high, right_low) + dot(left_low, right_high))


OUT_ROWS = 5 * TILE
BACK_ROWS = 4 * TILE


def turn_kernel(mem, h_ref, u_ref, v_ref, zonal_ref, merid_ref, pair_ref, single_ref, edge_ref):
    tiles = h_ref.shape[0] // mem
    columns = tiles * LANES
    zero = jnp.zeros((TILE, LANES), jnp.float32)
    for ref in (pair_ref, single_ref):
        ref[0:TILE, :] = zero
        ref[columns : columns + TILE, :] = zero
    for t in range(tiles):
        rows = pl.ds(t, mem, stride=tiles)
        lanes = slice(t * LANES, (t + 1) * LANES)
        pair = jnp.concatenate([h_ref[rows, :], u_ref[rows, :]], axis=0)
        zonal = jnp.broadcast_to(zonal_ref[:, lanes], (mem // 2, LANES))
        merid = jnp.broadcast_to(merid_ref[:, lanes], (mem // 2, LANES))
        single = jnp.concatenate([v_ref[rows, :], zonal, merid], axis=0)
        place = slice(STEPS + t * LANES, STEPS + (t + 1) * LANES)
        pair_ref[place, :] = pair.T
        single_ref[place, :] = single.T
    early = row_of((TILE, LANES)) < STEPS
    for i, ref in enumerate((pair_ref, single_ref)):
        edge_ref[i] = jnp.where(early, ref[columns : columns + TILE, :], ref[0:TILE, :])


def blocks_kernel(width, pair_ref, single_ref, west_ref, east_ref, send_ref):
    count = send_ref.shape[0]
    shape = (TILE, LANES)
    early = row_of(shape) < STEPS
    lane = lane_of(shape)
    low = lane < HALF
    part = lane % (HALF // 2)
    for d in range(count):
        pair = [pair_ref[width * d + TILE * j : width * d + TILE * (j + 1), :] for j in range(3)]
        single = [
            single_ref[width * d + TILE * j : width * d + TILE * (j + 1), :] for j in range(3)
        ]
        if d == 0:
            pair[0] = jnp.where(early, west_ref[0], pair[0])
            single[0] = jnp.where(early, west_ref[1], single[0])
        if d == count - 1:
            pair[2] = jnp.where(early, pair[2], east_ref[0])
            single[2] = jnp.where(early, single[2], east_ref[1])
        for j in range(3):
            send_ref[d, TILE * j : TILE * (j + 1), :] = pair[j]
        courant = jnp.where(part == 0, single[0], jnp.where(part == 1, single[1], single[2]))
        send_ref[d, 3 * TILE : 4 * TILE, :] = jnp.where(low, single[0], swapped(single[1]))
        send_ref[d, 4 * TILE : 5 * TILE, :] = jnp.where(low, single[2], courant)


def forecast(groups, strips, width, got_ref, x_ref):
    span = width + 2 * STEPS
    per_region = strips // REG_DEV
    cells = per_region * width

    def tiles_of(group, strip):
        block = group * strips + strip
        return [got_ref[block, TILE * j : TILE * (j + 1), :] for j in range(5)]

    zonal, merid = [], []
    for r in range(strips):
        mixed = got_ref[r, 4 * TILE : 5 * TILE, :]

        def column(first):
            parts = [
                jnp.broadcast_to(mixed[:, first + j : first + j + 1], (TILE, LANES))
                for j in range(3)
            ]
            return jnp.concatenate(parts, axis=0)

        zonal.append(column(HALF))
        merid.append(column(HALF + HALF // 2))
    for lane_tile in range(groups // 2):
        h, u, v = [], [], []
        for r in range(strips):
            even, odd = tiles_of(2 * lane_tile, r), tiles_of(2 * lane_tile + 1, r)
            h.append(jnp.concatenate([low_pair(even[j], odd[j]) for j in range(3)], axis=0))
            u.append(jnp.concatenate([high_pair(even[j], odd[j]) for j in range(3)], axis=0))
            v.append(
                jnp.concatenate(
                    [
                        low_pair(even[3], odd[3]),
                        high_pair(even[3], odd[3]),
                        low_pair(even[4], odd[4]),
                    ],
                    axis=0,
                )
            )
        for _ in range(STEPS):
            flux_v = [merid[r] * v[r] for r in range(strips)]
            for r in range(strips):
                flux_u = zonal[r] * u[r]
                south = flux_v[r - 1] if r else jnp.zeros_like(flux_u)
                h[r] = h[r] - (flux_u - pltpu.roll(flux_u, 1, 0) + flux_v[r] - south)
            for r in range(strips):
                north = h[r + 1] if r + 1 < strips else jnp.zeros_like(h[r])
                u[r] = u[r] - (pltpu.roll(h[r], span - 1, 0) - h[r])
                v[r] = v[r] - (north - h[r])
        lanes = slice(lane_tile * LANES, (lane_tile + 1) * LANES)
        for i, field in enumerate((h, u, v)):
            for r in range(strips):
                q, s = divmod(r, per_region)
                place = slice(i * cells + s * width, i * cells + (s + 1) * width)
                x_ref[q, place, lanes] = pltpu.roll(field[r], span - STEPS, 0)[:width]


def observe_kernel(index_ref, weight_ref, value_ref, var_ref, count_ref, info_ref, pull_ref):
    states = info_ref.shape[1]
    obs = index_ref.shape[2]
    for q in range(REG_DEV):
        state = row_of((states, obs))
        operator = jnp.zeros((states, obs), jnp.float32)
        for j in range(index_ref.shape[1]):
            hit = state == index_ref[q, j : j + 1, :]
            operator = operator + jnp.where(hit, weight_ref[q, j : j + 1, :], 0.0)
        live = lane_of((1, obs)) < count_ref[q]
        inverse = jnp.where(live, 1.0 / var_ref[q : q + 1, :], 0.0)
        scaled = operator * inverse
        info_ref[q] = lax.dot_general(
            scaled, operator, NT, precision=HIGHEST, preferred_element_type=jnp.float32
        )
        pulled = jnp.sum(scaled * value_ref[q : q + 1, :], axis=1, keepdims=True)
        pull_ref[q] = jnp.broadcast_to(pulled, (states, LANES))


def analyse(members, x_ref, info_ref, pull_ref, out_ref):
    states = x_ref.shape[1]
    square = (states, states)
    diagonal = row_of(square) == lane_of(square)
    identity = jnp.where(diagonal, 1.0, 0.0)
    regions = range(REG_DEV)
    scale = 1.0 / (members - 1)
    means, spreads, covs, inverses, iterates, norms = [], [], [], [], [], []
    for q in regions:
        x = x_ref[q]
        mean = jnp.sum(x, axis=1, keepdims=True) / members
        spread = x - mean
        means.append(mean)
        spreads.append(spread)
        covs.append(product(spread, spread, NT))
    for q in regions:
        info = info_ref[q]
        gain = product(covs[q], info) * scale
        gain_t = product(info, covs[q]) * scale
        total = jnp.sum(gain * gain_t + jnp.where(diagonal, 2.0 * gain, 0.0), keepdims=True)
        frobenius = jnp.sqrt(total + members)
        norms.append(frobenius)
        iterates.append((identity + gain) / frobenius)
    factors = [1.5 * identity - 0.5 * iterates[q] for q in regions]
    iterates = [product(iterates[q], factors[q]) for q in regions]
    inverses = factors
    for sweep in range(1, NEWTON):
        factors = [1.5 * identity - 0.5 * product(inverses[q], iterates[q]) for q in regions]
        if sweep < NEWTON - 1:
            iterates = [product(iterates[q], factors[q]) for q in regions]
        inverses = [product(factors[q], inverses[q]) for q in regions]
    increments = []
    for q in regions:
        root = inverses[q] / jnp.sqrt(norms[q])
        mean_row = jnp.sum(jnp.where(diagonal, means[q], 0.0), axis=0, keepdims=True)
        pulled = pull_ref[q][:, 0:1] - jnp.sum(info_ref[q] * mean_row, axis=1, keepdims=True)
        pulled = jnp.sum(covs[q] * pulled, axis=0, keepdims=True)
        shift = jnp.sum(root * pulled, axis=1, keepdims=True) * scale
        out_ref[q] = product(root, spreads[q] + shift) + means[q]
        shift_row = jnp.sum(jnp.where(diagonal, shift, 0.0), axis=0, keepdims=True)
        increments.append(jnp.sum(root * shift_row, axis=1, keepdims=True))
    return increments


def pack(groups, strips, width, ana_ref, increments, send_ref):
    per_region = strips // REG_DEV
    cells = per_region * width
    states = increments[0].shape[0]
    state = row_of((states, LANES))
    lane = lane_of((states, LANES))
    for r in range(strips):
        q, s = divmod(r, per_region)
        wanted = (lane // width) * cells + s * width + lane % width
        hit = (state == wanted) & (lane < 3 * width)
        row = jnp.sum(jnp.where(hit, increments[q], 0.0), axis=0, keepdims=True)
        row = jnp.broadcast_to(row, (TILE, LANES))
        for group in range(groups):
            block = group * strips + r
            lanes = slice((group // 2) * LANES, (group // 2 + 1) * LANES)
            pair = high_pair if group % 2 else low_pair
            for i in range(3):
                first = i * cells + s * width
                tile = pair(
                    ana_ref[q, first : first + TILE, lanes],
                    ana_ref[q, first + TILE : first + 2 * TILE, lanes],
                )
                send_ref[block, TILE * i : TILE * (i + 1), :] = tile
            send_ref[block, 3 * TILE : 4 * TILE, :] = row


def region_kernel(groups, strips, width, got_ref, info_ref, pull_ref, send_ref, x_ref, ana_ref):
    states = 3 * width * strips // REG_DEV
    if states < x_ref.shape[1]:
        x_ref[:, states:, :] = jnp.zeros_like(x_ref[:, states:, :])
    forecast(groups, strips, width, got_ref, x_ref)
    members = x_ref.shape[2]
    increments = analyse(members, x_ref, info_ref, pull_ref, ana_ref)
    pack(groups, strips, width, ana_ref, increments, send_ref)


def home_kernel(mem, strips, width, group_ref, got_ref, ctrl_ref, h_ref, u_ref, v_ref, fine_ref):
    blocks = got_ref.shape[0]
    tiles = blocks * width // LANES
    per_tile = LANES // width
    for i, out_ref in enumerate((h_ref, u_ref, v_ref)):
        for t in range(0, tiles, 2):
            rows = []
            for k in range(per_tile):
                even = got_ref[t * per_tile + k, TILE * i : TILE * (i + 1), :]
                odd = got_ref[(t + 1) * per_tile + k, TILE * i : TILE * (i + 1), :]
                rows += [low_pair(even, odd), high_pair(even, odd)]
            turned = jnp.concatenate(rows, axis=0).T
            out_ref[pl.ds(t, mem, stride=tiles), :] = turned[:mem]
            out_ref[pl.ds(t + 1, mem, stride=tiles), :] = turned[mem:]
    mine = group_ref[0] * strips
    per_fine = LANES // (2 * width)
    row = row_of((width, LANES))
    lane = lane_of((width, LANES))
    for t in range(ctrl_ref.shape[3] // LANES):
        rows = [got_ref[mine + t * per_fine + b, 3 * TILE : 4 * TILE, :] for b in range(per_fine)]
        columns = [jnp.concatenate([r] * (LANES // TILE), axis=0).T[:, 0:1] for r in rows]
        for i in range(3):
            total = jnp.zeros((1, LANES), jnp.float32)
            for b in range(per_fine):
                hit = ((lane // 2) % width == row) & (lane // (2 * width) == b)
                part = jnp.where(hit, columns[b][i * width : (i + 1) * width], 0.0)
                total = total + jnp.sum(part, axis=0, keepdims=True)
            lanes = slice(t * LANES, (t + 1) * LANES)
            for e in range(2):
                fine_ref[i, e, :, lanes] = ctrl_ref[i, e, :, lanes] + total


def forecast_kernel(groups, strips, width, got_ref, x_ref):
    forecast(groups, strips, width, got_ref, x_ref)


def pack_kernel(groups, strips, width, ana_ref, inc_ref, send_ref):
    pack(groups, strips, width, ana_ref, [inc_ref[q] for q in range(REG_DEV)], send_ref)


def analyse_in_members(x, obs_index, obs_weight, obs_value, obs_var, obs_count):
    states, members = x.shape[1:]
    mean_state = jnp.mean(x, axis=2, keepdims=True)
    spread = x - mean_state
    picks = (obs_index[:, :, :, None] == jnp.arange(states)).astype(jnp.float32)
    operator = jnp.sum(picks * obs_weight[:, :, :, None], axis=2)
    predicted = jnp.einsum("ros,rsk->rko", operator, x, precision=HIGHEST)
    mean_obs = jnp.mean(predicted, axis=1, keepdims=True)
    obs_spread = predicted - mean_obs
    active_obs = jnp.arange(obs_value.shape[1])[None, :] < obs_count[:, None]
    weighted = obs_spread * (active_obs.astype(jnp.float32) / obs_var)[:, None, :]
    gram_sum = jnp.einsum("rko,rjo->rkj", weighted, obs_spread, precision=HIGHEST)
    identity = jnp.eye(members, dtype=jnp.float32)
    scaled = identity + gram_sum / (members - 1)
    frobenius = jnp.sqrt(jnp.sum(scaled * scaled, axis=(1, 2), keepdims=True))
    iterate = scaled / frobenius
    inverse_root = jnp.broadcast_to(identity, scaled.shape)
    dot = functools.partial(jnp.einsum, "rij,rjk->rik", precision=HIGHEST)
    for _ in range(NEWTON):
        factor = 1.5 * identity - 0.5 * dot(inverse_root, iterate)
        iterate = dot(iterate, factor)
        inverse_root = dot(factor, inverse_root)
    transform = inverse_root / jnp.sqrt(frobenius)
    innovation = jnp.einsum(
        "rko,ro->rk", weighted, obs_value - mean_obs[:, 0], precision=HIGHEST
    )
    halfway = jnp.einsum("rkj,rj->rk", transform, innovation, precision=HIGHEST)
    mean_weights = jnp.einsum("rkj,rj->rk", transform, halfway, precision=HIGHEST) / (members - 1)
    increment = jnp.einsum("rk,rsk->rs", mean_weights, spread, precision=HIGHEST)[:, :, None]
    moved = jnp.einsum("rjk,rsj->rsk", transform, spread, precision=HIGHEST)
    return mean_state + increment + moved, increment


def call(kernel, out_shape, specs, scratch=(), cost=None, name=None):
    return pl.pallas_call(
        kernel,
        out_shape=out_shape,
        in_specs=specs,
        out_specs=jax.tree.map(lambda _: VMEM, out_shape),
        scratch_shapes=scratch,
        cost_estimate=cost,
        name=name,
    )


def f32(*shape):
    return jax.ShapeDtypeStruct(shape, jnp.float32)


def shards(
    sample_surface_elevation,
    sample_zonal_current,
    sample_meridional_current,
    zonal_edge_layer_courant,
    meridional_edge_layer_courant,
    obs_index,
    obs_weight,
    obs_value,
    obs_var,
    obs_count,
    fine_ctrl,
):
    groups = lax.axis_size("member")
    strips = lax.axis_size("region")
    owners = ("member", "region")
    mem, rows, columns = sample_surface_elevation.shape
    count = groups * strips
    width = columns // count
    members = groups * mem
    assert rows == 1 and 2 * mem == LANES and width == 2 * TILE and STEPS * 2 == TILE
    assert columns % (2 * LANES) == 0 and groups % 2 == 0 and strips % REG_DEV == 0
    flat = (mem * columns // LANES, LANES)
    pair, single, edge = call(
        functools.partial(turn_kernel, mem),
        (f32(columns + TILE, LANES), f32(columns + TILE, LANES), f32(2, TILE, LANES)),
        [VMEM] * 5,
        name="turn",
    )(
        sample_surface_elevation.reshape(flat),
        sample_zonal_current.reshape(flat),
        sample_meridional_current.reshape(flat),
        zonal_edge_layer_courant,
        meridional_edge_layer_courant,
    )
    from_west = passed_along(edge, "fine", 1)
    from_east = from_west if lax.axis_size("fine") == 2 else passed_along(edge, "fine", -1)
    out = call(
        functools.partial(blocks_kernel, width),
        f32(count, OUT_ROWS, LANES),
        [VMEM] * 4,
        name="blocks",
    )(pair, single, from_west, from_east)
    got = lax.all_to_all(out, owners, split_axis=0, concat_axis=0, tiled=True)
    states = 3 * width * strips // REG_DEV
    back_shape = f32(count, BACK_ROWS, LANES)
    layout = (groups, strips, width)
    if states <= members:
        padded = -(-states // LANES) * LANES
        obs = obs_value.shape[1]
        info, pull = call(
            observe_kernel,
            (f32(REG_DEV, padded, padded), f32(REG_DEV, padded, LANES)),
            [VMEM] * 4 + [SMEM],
            cost=pl.CostEstimate(
                flops=12 * REG_DEV * padded * padded * obs, bytes_accessed=1 << 20, transcendentals=0
            ),
            name="observe",
        )(
            obs_index.transpose(0, 2, 1),
            obs_weight.transpose(0, 2, 1),
            obs_value,
            obs_var,
            obs_count,
        )
        back = call(
            functools.partial(region_kernel, *layout),
            back_shape,
            [VMEM] * 3,
            scratch=[
                pltpu.VMEM((REG_DEV, padded, members), jnp.float32),
                pltpu.VMEM((REG_DEV, padded, members), jnp.float32),
            ],
            name="region",
        )(got, info, pull)
    else:
        x = call(
            functools.partial(forecast_kernel, *layout),
            f32(REG_DEV, states, members),
            [VMEM],
            name="forecast",
        )(got)
        analysis, increment = analyse_in_members(
            x, obs_index, obs_weight, obs_value, obs_var, obs_count
        )
        back = call(
            functools.partial(pack_kernel, *layout), back_shape, [VMEM] * 2, name="pack"
        )(analysis, increment)
    home = lax.all_to_all(back, owners, split_axis=0, concat_axis=0, tiled=True)
    mine = lax.axis_index("member").astype(jnp.int32).reshape(1)
    ana_h, ana_u, ana_v, fine_out = call(
        functools.partial(home_kernel, mem, strips, width),
        (f32(*flat), f32(*flat), f32(*flat), f32(*fine_ctrl.shape)),
        [SMEM, VMEM, VMEM],
        name="home",
    )(mine, home, fine_ctrl)
    shape = (mem, rows, columns)
    return (ana_h.reshape(shape), ana_u.reshape(shape), ana_v.reshape(shape), fine_out)


def solution(mesh):
    strip = P("member", "region", "fine")
    owner = ("member", "region", "fine")
    fine = P(None, "region", "fine", "member")
    return jax.shard_map(
        shards,
        mesh=mesh,
        in_specs=(
            strip,
            strip,
            strip,
            P("region", "fine"),
            P("region", "fine"),
            P(owner, None, None),
            P(owner, None, None),
            P(owner, None),
            P(owner, None),
            P(owner),
            fine,
        ),
        out_specs=(strip, strip, strip, fine),
        check_vma=False,
    )
```

```python
import functools

import jax
import jax.numpy as jnp
from jax import lax
from jax.experimental import pallas as pl
from jax.experimental.pallas import tpu as pltpu
from jax.sharding import PartitionSpec as P

REG_DEV = 2
STEPS = 4
NEWTON = 8
LANES = 128
TILE = 8
HALF = LANES // 2
GRANT = 32 << 20

HIGHEST = lax.Precision.HIGHEST
NT = (((1,), (1,)), ((), ()))
NN = (((1,), (0,)), ((), ()))
VMEM = pl.BlockSpec(memory_space=pltpu.VMEM)
SMEM = pl.BlockSpec(memory_space=pltpu.SMEM)


def passed_along(block, axis, distance):
    count = lax.axis_size(axis)
    route = [((i - distance) % count, i) for i in range(count)]
    return lax.ppermute(block, axis, route)


def lane_of(shape):
    return lax.broadcasted_iota(jnp.int32, shape, 1)


def row_of(shape):
    return lax.broadcasted_iota(jnp.int32, shape, 0)


def swapped(tile):
    return pltpu.roll(tile, HALF, 1)


def low_pair(even, odd):
    return jnp.where(lane_of(even.shape) < HALF, even, swapped(odd))


def high_pair(even, odd):
    return jnp.where(lane_of(even.shape) < HALF, swapped(even), odd)


def split(value):
    high = value.astype(jnp.bfloat16)
    return high, (value - high.astype(jnp.float32)).astype(jnp.bfloat16)


def product(left, right, dims=NN):
    left_high, left_low = split(left)
    right_high, right_low = split(right)
    dot = functools.partial(
        lax.dot_general, dimension_numbers=dims, preferred_element_type=jnp.float32
    )
    return dot(left_high, right_high) + (dot(left_high, right_low) + dot(left_low, right_high))


OUT_ROWS = 5 * TILE
BACK_ROWS = 4 * TILE


def turn_kernel(mem, h_ref, u_ref, v_ref, zonal_ref, merid_ref, pair_ref, single_ref, edge_ref):
    tiles = h_ref.shape[0] // mem
    columns = tiles * LANES
    zero = jnp.zeros((TILE, LANES), jnp.float32)
    for ref in (pair_ref, single_ref):
        ref[0:TILE, :] = zero
        ref[columns : columns + TILE, :] = zero
    for t in range(tiles):
        rows = pl.ds(t, mem, stride=tiles)
        lanes = slice(t * LANES, (t + 1) * LANES)
        pair = jnp.concatenate([h_ref[rows, :], u_ref[rows, :]], axis=0)
        zonal = jnp.broadcast_to(zonal_ref[:, lanes], (mem // 2, LANES))
        merid = jnp.broadcast_to(merid_ref[:, lanes], (mem // 2, LANES))
        single = jnp.concatenate([v_ref[rows, :], zonal, merid], axis=0)
        place = slice(STEPS + t * LANES, STEPS + (t + 1) * LANES)
        pair_ref[place, :] = pair.T
        single_ref[place, :] = single.T
    early = row_of((TILE, LANES)) < STEPS
    for i, ref in enumerate((pair_ref, single_ref)):
        edge_ref[i] = jnp.where(early, ref[columns : columns + TILE, :], ref[0:TILE, :])


def blocks_kernel(width, pair_ref, single_ref, west_ref, east_ref, send_ref):
    count = send_ref.shape[0]
    shape = (TILE, LANES)
    early = row_of(shape) < STEPS
    lane = lane_of(shape)
    low = lane < HALF
    part = lane % (HALF // 2)
    for d in range(count):
        pair = [pair_ref[width * d + TILE * j : width * d + TILE * (j + 1), :] for j in range(3)]
        single = [
            single_ref[width * d + TILE * j : width * d + TILE * (j + 1), :] for j in range(3)
        ]
        if d == 0:
            pair[0] = jnp.where(early, west_ref[0], pair[0])
            single[0] = jnp.where(early, west_ref[1], single[0])
        if d == count - 1:
            pair[2] = jnp.where(early, pair[2], east_ref[0])
            single[2] = jnp.where(early, single[2], east_ref[1])
        for j in range(3):
            send_ref[d, TILE * j : TILE * (j + 1), :] = pair[j]
        courant = jnp.where(part == 0, single[0], jnp.where(part == 1, single[1], single[2]))
        send_ref[d, 3 * TILE : 4 * TILE, :] = jnp.where(low, single[0], swapped(single[1]))
        send_ref[d, 4 * TILE : 5 * TILE, :] = jnp.where(low, single[2], courant)


def forecast(groups, strips, width, got_ref, x_ref):
    span = width + 2 * STEPS
    per_region = strips // REG_DEV
    cells = per_region * width

    def tiles_of(group, strip):
        block = group * strips + strip
        return [got_ref[block, TILE * j : TILE * (j + 1), :] for j in range(5)]

    zonal, merid = [], []
    for r in range(strips):
        mixed = got_ref[r, 4 * TILE : 5 * TILE, :]

        def column(first):
            parts = [
                jnp.broadcast_to(mixed[:, first + j : first + j + 1], (TILE, LANES))
                for j in range(3)
            ]
            return jnp.concatenate(parts, axis=0)

        zonal.append(column(HALF))
        merid.append(column(HALF + HALF // 2))
    for lane_tile in range(groups // 2):
        h, u, v = [], [], []
        for r in range(strips):
            even, odd = tiles_of(2 * lane_tile, r), tiles_of(2 * lane_tile + 1, r)
            h.append(jnp.concatenate([low_pair(even[j], odd[j]) for j in range(3)], axis=0))
            u.append(jnp.concatenate([high_pair(even[j], odd[j]) for j in range(3)], axis=0))
            v.append(
                jnp.concatenate(
                    [
                        low_pair(even[3], odd[3]),
                        high_pair(even[3], odd[3]),
                        low_pair(even[4], odd[4]),
                    ],
                    axis=0,
                )
            )
        for _ in range(STEPS):
            flux_v = [merid[r] * v[r] for r in range(strips)]
            for r in range(strips):
                flux_u = zonal[r] * u[r]
                south = flux_v[r - 1] if r else jnp.zeros_like(flux_u)
                h[r] = h[r] - (flux_u - pltpu.roll(flux_u, 1, 0) + flux_v[r] - south)
            for r in range(strips):
                north = h[r + 1] if r + 1 < strips else jnp.zeros_like(h[r])
                u[r] = u[r] - (pltpu.roll(h[r], span - 1, 0) - h[r])
                v[r] = v[r] - (north - h[r])
        lanes = slice(lane_tile * LANES, (lane_tile + 1) * LANES)
        for i, field in enumerate((h, u, v)):
            for r in range(strips):
                q, s = divmod(r, per_region)
                place = slice(i * cells + s * width, i * cells + (s + 1) * width)
                x_ref[q, place, lanes] = pltpu.roll(field[r], span - STEPS, 0)[:width]


def observe_kernel(index_ref, weight_ref, value_ref, var_ref, count_ref, info_ref, pull_ref):
    states = info_ref.shape[1]
    obs = index_ref.shape[2]
    for q in range(REG_DEV):
        state = row_of((states, obs))
        operator = jnp.zeros((states, obs), jnp.float32)
        for j in range(index_ref.shape[1]):
            hit = state == index_ref[q, j : j + 1, :]
            operator = operator + jnp.where(hit, weight_ref[q, j : j + 1, :], 0.0)
        live = lane_of((1, obs)) < count_ref[q]
        inverse = jnp.where(live, 1.0 / var_ref[q : q + 1, :], 0.0)
        scaled = operator * inverse
        info_ref[q] = lax.dot_general(
            scaled, operator, NT, precision=HIGHEST, preferred_element_type=jnp.float32
        )
        pulled = jnp.sum(scaled * value_ref[q : q + 1, :], axis=1, keepdims=True)
        pull_ref[q] = jnp.broadcast_to(pulled, (states, LANES))


def analyse(members, x_ref, info_ref, pull_ref, out_ref):
    states = x_ref.shape[1]
    square = (states, states)
    diagonal = row_of(square) == lane_of(square)
    identity = jnp.where(diagonal, 1.0, 0.0)
    regions = range(REG_DEV)
    scale = 1.0 / (members - 1)
    means, spreads, covs, inverses, iterates, norms = [], [], [], [], [], []
    for q in regions:
        x = x_ref[q]
        mean = jnp.sum(x, axis=1, keepdims=True) / members
        spread = x - mean
        means.append(mean)
        spreads.append(spread)
        covs.append(product(spread, spread, NT))
    for q in regions:
        info = info_ref[q]
        gain = product(covs[q], info) * scale
        gain_t = product(info, covs[q]) * scale
        total = jnp.sum(gain * gain_t + jnp.where(diagonal, 2.0 * gain, 0.0), keepdims=True)
        frobenius = jnp.sqrt(total + members)
        norms.append(frobenius)
        iterates.append((identity + gain) / frobenius)
    factors = [1.5 * identity - 0.5 * iterates[q] for q in regions]
    iterates = [product(iterates[q], factors[q]) for q in regions]
    inverses = factors
    for sweep in range(1, NEWTON):
        factors = [1.5 * identity - 0.5 * product(inverses[q], iterates[q]) for q in regions]
        if sweep < NEWTON - 1:
            iterates = [product(iterates[q], factors[q]) for q in regions]
        inverses = [product(factors[q], inverses[q]) for q in regions]
    increments = []
    for q in regions:
        root = inverses[q] / jnp.sqrt(norms[q])
        mean_row = jnp.sum(jnp.where(diagonal, means[q], 0.0), axis=0, keepdims=True)
        pulled = pull_ref[q][:, 0:1] - jnp.sum(info_ref[q] * mean_row, axis=1, keepdims=True)
        pulled = jnp.sum(covs[q] * pulled, axis=0, keepdims=True)
        shift = jnp.sum(root * pulled, axis=1, keepdims=True) * scale
        out_ref[q] = product(root, spreads[q] + shift) + means[q]
        shift_row = jnp.sum(jnp.where(diagonal, shift, 0.0), axis=0, keepdims=True)
        increments.append(jnp.sum(root * shift_row, axis=1, keepdims=True))
    return increments


def pack(groups, strips, width, ana_ref, increments, send_ref):
    per_region = strips // REG_DEV
    cells = per_region * width
    states = increments[0].shape[0]
    state = row_of((states, LANES))
    lane = lane_of((states, LANES))
    for r in range(strips):
        q, s = divmod(r, per_region)
        wanted = (lane // width) * cells + s * width + lane % width
        hit = (state == wanted) & (lane < 3 * width)
        row = jnp.sum(jnp.where(hit, increments[q], 0.0), axis=0, keepdims=True)
        row = jnp.broadcast_to(row, (TILE, LANES))
        for group in range(groups):
            block = group * strips + r
            lanes = slice((group // 2) * LANES, (group // 2 + 1) * LANES)
            pair = high_pair if group % 2 else low_pair
            for i in range(3):
                first = i * cells + s * width
                tile = pair(
                    ana_ref[q, first : first + TILE, lanes],
                    ana_ref[q, first + TILE : first + 2 * TILE, lanes],
                )
                send_ref[block, TILE * i : TILE * (i + 1), :] = tile
            send_ref[block, 3 * TILE : 4 * TILE, :] = row


def region_kernel(groups, strips, width, got_ref, info_ref, pull_ref, send_ref, x_ref, ana_ref):
    states = 3 * width * strips // REG_DEV
    if states < x_ref.shape[1]:
        x_ref[:, states:, :] = jnp.zeros_like(x_ref[:, states:, :])
    forecast(groups, strips, width, got_ref, x_ref)
    members = x_ref.shape[2]
    increments = analyse(members, x_ref, info_ref, pull_ref, ana_ref)
    pack(groups, strips, width, ana_ref, increments, send_ref)


def home_kernel(mem, strips, width, group_ref, got_ref, ctrl_ref, h_ref, u_ref, v_ref, fine_ref):
    blocks = got_ref.shape[0]
    tiles = blocks * width // LANES
    per_tile = LANES // width
    for i, out_ref in enumerate((h_ref, u_ref, v_ref)):
        for t in range(0, tiles, 2):
            rows = []
            for k in range(per_tile):
                even = got_ref[t * per_tile + k, TILE * i : TILE * (i + 1), :]
                odd = got_ref[(t + 1) * per_tile + k, TILE * i : TILE * (i + 1), :]
                rows += [low_pair(even, odd), high_pair(even, odd)]
            turned = jnp.concatenate(rows, axis=0).T
            out_ref[pl.ds(t, mem, stride=tiles), :] = turned[:mem]
            out_ref[pl.ds(t + 1, mem, stride=tiles), :] = turned[mem:]
    mine = group_ref[0] * strips
    per_fine = LANES // (2 * width)
    row = row_of((width, LANES))
    lane = lane_of((width, LANES))
    for t in range(ctrl_ref.shape[3] // LANES):
        rows = [got_ref[mine + t * per_fine + b, 3 * TILE : 4 * TILE, :] for b in range(per_fine)]
        columns = [jnp.concatenate([r] * (LANES // TILE), axis=0).T[:, 0:1] for r in rows]
        for i in range(3):
            total = jnp.zeros((1, LANES), jnp.float32)
            for b in range(per_fine):
                hit = ((lane // 2) % width == row) & (lane // (2 * width) == b)
                part = jnp.where(hit, columns[b][i * width : (i + 1) * width], 0.0)
                total = total + jnp.sum(part, axis=0, keepdims=True)
            lanes = slice(t * LANES, (t + 1) * LANES)
            for e in range(2):
                fine_ref[i, e, :, lanes] = ctrl_ref[i, e, :, lanes] + total


def forecast_kernel(groups, strips, width, got_ref, x_ref):
    forecast(groups, strips, width, got_ref, x_ref)


def pack_kernel(groups, strips, width, ana_ref, inc_ref, send_ref):
    pack(groups, strips, width, ana_ref, [inc_ref[q] for q in range(REG_DEV)], send_ref)


def analyse_in_members(x, obs_index, obs_weight, obs_value, obs_var, obs_count):
    states, members = x.shape[1:]
    mean_state = jnp.mean(x, axis=2, keepdims=True)
    spread = x - mean_state
    picks = (obs_index[:, :, :, None] == jnp.arange(states)).astype(jnp.float32)
    operator = jnp.sum(picks * obs_weight[:, :, :, None], axis=2)
    predicted = jnp.einsum("ros,rsk->rko", operator, x, precision=HIGHEST)
    mean_obs = jnp.mean(predicted, axis=1, keepdims=True)
    obs_spread = predicted - mean_obs
    active_obs = jnp.arange(obs_value.shape[1])[None, :] < obs_count[:, None]
    weighted = obs_spread * (active_obs.astype(jnp.float32) / obs_var)[:, None, :]
    gram_sum = jnp.einsum("rko,rjo->rkj", weighted, obs_spread, precision=HIGHEST)
    identity = jnp.eye(members, dtype=jnp.float32)
    scaled = identity + gram_sum / (members - 1)
    frobenius = jnp.sqrt(jnp.sum(scaled * scaled, axis=(1, 2), keepdims=True))
    iterate = scaled / frobenius
    inverse_root = jnp.broadcast_to(identity, scaled.shape)
    dot = functools.partial(jnp.einsum, "rij,rjk->rik", precision=HIGHEST)
    for _ in range(NEWTON):
        factor = 1.5 * identity - 0.5 * dot(inverse_root, iterate)
        iterate = dot(iterate, factor)
        inverse_root = dot(factor, inverse_root)
    transform = inverse_root / jnp.sqrt(frobenius)
    innovation = jnp.einsum(
        "rko,ro->rk", weighted, obs_value - mean_obs[:, 0], precision=HIGHEST
    )
    halfway = jnp.einsum("rkj,rj->rk", transform, innovation, precision=HIGHEST)
    mean_weights = jnp.einsum("rkj,rj->rk", transform, halfway, precision=HIGHEST) / (members - 1)
    increment = jnp.einsum("rk,rsk->rs", mean_weights, spread, precision=HIGHEST)[:, :, None]
    moved = jnp.einsum("rjk,rsj->rsk", transform, spread, precision=HIGHEST)
    return mean_state + increment + moved, increment


def call(kernel, out_shape, specs, scratch=(), cost=None, name=None):
    many = isinstance(out_shape, tuple)
    return pl.pallas_call(
        kernel,
        out_shape=out_shape,
        in_specs=specs,
        out_specs=tuple(VMEM for _ in out_shape) if many else VMEM,
        scratch_shapes=scratch,
        cost_estimate=cost,
        compiler_params=pltpu.CompilerParams(vmem_limit_bytes=GRANT),
        name=name,
    )


def f32(*shape):
    return jax.ShapeDtypeStruct(shape, jnp.float32)


def near(*shape):
    return pltpu.VMEM(shape, jnp.float32)


def kept(array):
    return pltpu.with_memory_space_constraint(array, pltpu.VMEM)


def shards(
    sample_surface_elevation,
    sample_zonal_current,
    sample_meridional_current,
    zonal_edge_layer_courant,
    meridional_edge_layer_courant,
    obs_index,
    obs_weight,
    obs_value,
    obs_var,
    obs_count,
    fine_ctrl,
):
    groups = lax.axis_size("member")
    strips = lax.axis_size("region")
    owners = ("member", "region")
    mem, rows, columns = sample_surface_elevation.shape
    count = groups * strips
    width = columns // count
    members = groups * mem
    assert rows == 1 and 2 * mem == LANES and width == 2 * TILE and STEPS * 2 == TILE
    assert columns % (2 * LANES) == 0 and groups % 2 == 0 and strips % REG_DEV == 0
    flat = (mem * columns // LANES, LANES)
    pair, single, edge = call(
        functools.partial(turn_kernel, mem),
        (near(columns + TILE, LANES), near(columns + TILE, LANES), near(2, TILE, LANES)),
        [VMEM] * 5,
        name="turn",
    )(
        sample_surface_elevation.reshape(flat),
        sample_zonal_current.reshape(flat),
        sample_meridional_current.reshape(flat),
        zonal_edge_layer_courant,
        meridional_edge_layer_courant,
    )
    from_west = passed_along(edge, "fine", 1)
    from_east = from_west if lax.axis_size("fine") == 2 else passed_along(edge, "fine", -1)
    out = call(
        functools.partial(blocks_kernel, width),
        near(count, OUT_ROWS, LANES),
        [VMEM] * 4,
        name="blocks",
    )(kept(pair), kept(single), kept(from_west), kept(from_east))
    got = lax.all_to_all(out, owners, split_axis=0, concat_axis=0, tiled=True)
    got = kept(got)
    states = 3 * width * strips // REG_DEV
    back_shape = near(count, BACK_ROWS, LANES)
    layout = (groups, strips, width)
    if states <= members:
        padded = -(-states // LANES) * LANES
        obs = obs_value.shape[1]
        info, pull = call(
            observe_kernel,
            (near(REG_DEV, padded, padded), near(REG_DEV, padded, LANES)),
            [VMEM] * 4 + [SMEM],
            cost=pl.CostEstimate(
                flops=12 * REG_DEV * padded * padded * obs, bytes_accessed=1 << 20, transcendentals=0
            ),
            name="observe",
        )(
            obs_index.transpose(0, 2, 1),
            obs_weight.transpose(0, 2, 1),
            obs_value,
            obs_var,
            obs_count,
        )
        back = call(
            functools.partial(region_kernel, *layout),
            back_shape,
            [VMEM] * 3,
            scratch=[
                pltpu.VMEM((REG_DEV, padded, members), jnp.float32),
                pltpu.VMEM((REG_DEV, padded, members), jnp.float32),
            ],
            name="region",
        )(got, kept(info), kept(pull))
    else:
        x = call(
            functools.partial(forecast_kernel, *layout),
            f32(REG_DEV, states, members),
            [VMEM],
            name="forecast",
        )(got)
        analysis, increment = analyse_in_members(
            x, obs_index, obs_weight, obs_value, obs_var, obs_count
        )
        back = call(
            functools.partial(pack_kernel, *layout), back_shape, [VMEM] * 2, name="pack"
        )(analysis, increment)
    home = lax.all_to_all(back, owners, split_axis=0, concat_axis=0, tiled=True)
    mine = lax.axis_index("member").astype(jnp.int32).reshape(1)
    ana_h, ana_u, ana_v, fine_out = call(
        functools.partial(home_kernel, mem, strips, width),
        (f32(*flat), f32(*flat), f32(*flat), f32(*fine_ctrl.shape)),
        [SMEM, VMEM, VMEM],
        name="home",
    )(mine, kept(home), fine_ctrl)
    shape = (mem, rows, columns)
    return (ana_h.reshape(shape), ana_u.reshape(shape), ana_v.reshape(shape), fine_out)


def solution(mesh):
    strip = P("member", "region", "fine")
    owner = ("member", "region", "fine")
    fine = P(None, "region", "fine", "member")
    return jax.shard_map(
        shards,
        mesh=mesh,
        in_specs=(
            strip,
            strip,
            strip,
            P("region", "fine"),
            P("region", "fine"),
            P(owner, None, None),
            P(owner, None, None),
            P(owner, None),
            P(owner, None),
            P(owner),
            fine,
        ),
        out_specs=(strip, strip, strip, fine),
        check_vma=False,
    )
```

```python
import functools

import jax
import jax.numpy as jnp
from jax import lax
from jax.experimental import pallas as pl
from jax.experimental.pallas import tpu as pltpu
from jax.sharding import PartitionSpec as P

REG_DEV = 2
STEPS = 4
NEWTON = 8
LANES = 128
TILE = 8
HALF = LANES // 2
GRANT = 32 << 20

HIGHEST = lax.Precision.HIGHEST
NT = (((1,), (1,)), ((), ()))
NN = (((1,), (0,)), ((), ()))
VMEM = pl.BlockSpec(memory_space=pltpu.VMEM)
SMEM = pl.BlockSpec(memory_space=pltpu.SMEM)
HBM = pl.BlockSpec(memory_space=pltpu.HBM)


def passed_along(block, axis, distance):
    count = lax.axis_size(axis)
    route = [((i - distance) % count, i) for i in range(count)]
    return lax.ppermute(block, axis, route)


def lane_of(shape):
    return lax.broadcasted_iota(jnp.int32, shape, 1)


def row_of(shape):
    return lax.broadcasted_iota(jnp.int32, shape, 0)


def swapped(tile):
    return pltpu.roll(tile, HALF, 1)


def low_pair(even, odd):
    return jnp.where(lane_of(even.shape) < HALF, even, swapped(odd))


def high_pair(even, odd):
    return jnp.where(lane_of(even.shape) < HALF, swapped(even), odd)


def split(value):
    high = value.astype(jnp.bfloat16)
    return high, (value - high.astype(jnp.float32)).astype(jnp.bfloat16)


def product(left, right, dims=NN):
    left_high, left_low = split(left)
    right_high, right_low = split(right)
    dot = functools.partial(
        lax.dot_general, dimension_numbers=dims, preferred_element_type=jnp.float32
    )
    return dot(left_high, right_high) + (dot(left_high, right_low) + dot(left_low, right_high))


OUT_ROWS = 5 * TILE
BACK_ROWS = 4 * TILE


def turn_kernel(mem, later, *refs):
    h_ref, u_ref, v_ref, zonal_ref, merid_ref, count_ref = refs[:6]
    sources, refs = refs[6 : 6 + later], refs[6 + later :]
    pair_ref, single_ref, edge_ref, live_ref = refs[:4]
    targets, sems = refs[4 : 4 + later], refs[-1]
    copies = [
        pltpu.make_async_copy(source, target, sems.at[i])
        for i, (source, target) in enumerate(zip(sources, targets))
    ]
    for copy in copies:
        copy.start()
    tiles = h_ref.shape[0] // mem
    columns = tiles * LANES
    zero = jnp.zeros((TILE, LANES), jnp.float32)
    for ref in (pair_ref, single_ref):
        ref[0:TILE, :] = zero
        ref[columns : columns + TILE, :] = zero
    for t in range(tiles):
        rows = pl.ds(t, mem, stride=tiles)
        lanes = slice(t * LANES, (t + 1) * LANES)
        pair = jnp.concatenate([h_ref[rows, :], u_ref[rows, :]], axis=0)
        zonal = jnp.broadcast_to(zonal_ref[:, lanes], (mem // 2, LANES))
        merid = jnp.broadcast_to(merid_ref[:, lanes], (mem // 2, LANES))
        single = jnp.concatenate([v_ref[rows, :], zonal, merid], axis=0)
        place = slice(STEPS + t * LANES, STEPS + (t + 1) * LANES)
        pair_ref[place, :] = pair.T
        single_ref[place, :] = single.T
    early = row_of((TILE, LANES)) < STEPS
    for i, ref in enumerate((pair_ref, single_ref)):
        edge_ref[i] = jnp.where(early, ref[columns : columns + TILE, :], ref[0:TILE, :])
    for q in range(REG_DEV):
        live_ref[q] = jnp.full(live_ref.shape[1:], count_ref[q], jnp.int32)
    for copy in copies:
        copy.wait()


def blocks_kernel(width, pair_ref, single_ref, west_ref, east_ref, *refs):
    send_ref = refs[-1]
    count = send_ref.shape[0]
    shape = (TILE, LANES)
    early = row_of(shape) < STEPS
    lane = lane_of(shape)
    low = lane < HALF
    part = lane % (HALF // 2)
    for d in range(count):
        pair = [pair_ref[width * d + TILE * j : width * d + TILE * (j + 1), :] for j in range(3)]
        single = [
            single_ref[width * d + TILE * j : width * d + TILE * (j + 1), :] for j in range(3)
        ]
        if d == 0:
            pair[0] = jnp.where(early, west_ref[0], pair[0])
            single[0] = jnp.where(early, west_ref[1], single[0])
        if d == count - 1:
            pair[2] = jnp.where(early, pair[2], east_ref[0])
            single[2] = jnp.where(early, single[2], east_ref[1])
        for j in range(3):
            send_ref[d, TILE * j : TILE * (j + 1), :] = pair[j]
        courant = jnp.where(part == 0, single[0], jnp.where(part == 1, single[1], single[2]))
        send_ref[d, 3 * TILE : 4 * TILE, :] = jnp.where(low, single[0], swapped(single[1]))
        send_ref[d, 4 * TILE : 5 * TILE, :] = jnp.where(low, single[2], courant)


def forecast(groups, strips, width, got_ref, x_ref):
    span = width + 2 * STEPS
    per_region = strips // REG_DEV
    cells = per_region * width

    def tiles_of(group, strip):
        block = group * strips + strip
        return [got_ref[block, TILE * j : TILE * (j + 1), :] for j in range(5)]

    zonal, merid = [], []
    for r in range(strips):
        mixed = got_ref[r, 4 * TILE : 5 * TILE, :]

        def column(first):
            parts = [
                jnp.broadcast_to(mixed[:, first + j : first + j + 1], (TILE, LANES))
                for j in range(3)
            ]
            return jnp.concatenate(parts, axis=0)

        zonal.append(column(HALF))
        merid.append(column(HALF + HALF // 2))
    for lane_tile in range(groups // 2):
        h, u, v = [], [], []
        for r in range(strips):
            even, odd = tiles_of(2 * lane_tile, r), tiles_of(2 * lane_tile + 1, r)
            h.append(jnp.concatenate([low_pair(even[j], odd[j]) for j in range(3)], axis=0))
            u.append(jnp.concatenate([high_pair(even[j], odd[j]) for j in range(3)], axis=0))
            v.append(
                jnp.concatenate(
                    [
                        low_pair(even[3], odd[3]),
                        high_pair(even[3], odd[3]),
                        low_pair(even[4], odd[4]),
                    ],
                    axis=0,
                )
            )
        for _ in range(STEPS):
            flux_v = [merid[r] * v[r] for r in range(strips)]
            for r in range(strips):
                flux_u = zonal[r] * u[r]
                south = flux_v[r - 1] if r else jnp.zeros_like(flux_u)
                h[r] = h[r] - (flux_u - pltpu.roll(flux_u, 1, 0) + flux_v[r] - south)
            for r in range(strips):
                north = h[r + 1] if r + 1 < strips else jnp.zeros_like(h[r])
                u[r] = u[r] - (pltpu.roll(h[r], span - 1, 0) - h[r])
                v[r] = v[r] - (north - h[r])
        lanes = slice(lane_tile * LANES, (lane_tile + 1) * LANES)
        for i, field in enumerate((h, u, v)):
            for r in range(strips):
                q, s = divmod(r, per_region)
                place = slice(i * cells + s * width, i * cells + (s + 1) * width)
                x_ref[q, place, lanes] = pltpu.roll(field[r], span - STEPS, 0)[:width]


def observe_kernel(live_ref, index_ref, weight_ref, value_ref, var_ref, info_ref, pull_ref):
    states = info_ref.shape[1]
    obs = index_ref.shape[2]
    for q in range(REG_DEV):
        state = row_of((states, obs))
        operator = jnp.zeros((states, obs), jnp.float32)
        for j in range(index_ref.shape[1]):
            hit = state == index_ref[q, j : j + 1, :]
            operator = operator + jnp.where(hit, weight_ref[q, j : j + 1, :], 0.0)
        live = lane_of((1, obs)) < live_ref[q, 0:1, 0:1]
        inverse = jnp.where(live, 1.0 / var_ref[q : q + 1, :], 0.0)
        scaled = operator * inverse
        info_ref[q] = lax.dot_general(
            scaled, operator, NT, precision=HIGHEST, preferred_element_type=jnp.float32
        )
        pulled = jnp.sum(scaled * value_ref[q : q + 1, :], axis=1, keepdims=True)
        pull_ref[q] = jnp.broadcast_to(pulled, (states, LANES))


def analyse(members, x_ref, info_ref, pull_ref, out_ref):
    states = x_ref.shape[1]
    square = (states, states)
    diagonal = row_of(square) == lane_of(square)
    identity = jnp.where(diagonal, 1.0, 0.0)
    regions = range(REG_DEV)
    scale = 1.0 / (members - 1)
    means, spreads, covs, inverses, iterates, norms = [], [], [], [], [], []
    for q in regions:
        x = x_ref[q]
        mean = jnp.sum(x, axis=1, keepdims=True) / members
        spread = x - mean
        means.append(mean)
        spreads.append(spread)
        covs.append(product(spread, spread, NT))
    for q in regions:
        info = info_ref[q]
        gain = product(covs[q], info) * scale
        gain_t = product(info, covs[q]) * scale
        total = jnp.sum(gain * gain_t + jnp.where(diagonal, 2.0 * gain, 0.0), keepdims=True)
        frobenius = jnp.sqrt(total + members)
        norms.append(frobenius)
        iterates.append((identity + gain) / frobenius)
    factors = [1.5 * identity - 0.5 * iterates[q] for q in regions]
    iterates = [product(iterates[q], factors[q]) for q in regions]
    inverses = factors
    for sweep in range(1, NEWTON):
        factors = [1.5 * identity - 0.5 * product(inverses[q], iterates[q]) for q in regions]
        if sweep < NEWTON - 1:
            iterates = [product(iterates[q], factors[q]) for q in regions]
        inverses = [product(factors[q], inverses[q]) for q in regions]
    increments = []
    for q in regions:
        root = inverses[q] / jnp.sqrt(norms[q])
        mean_row = jnp.sum(jnp.where(diagonal, means[q], 0.0), axis=0, keepdims=True)
        pulled = pull_ref[q][:, 0:1] - jnp.sum(info_ref[q] * mean_row, axis=1, keepdims=True)
        pulled = jnp.sum(covs[q] * pulled, axis=0, keepdims=True)
        shift = jnp.sum(root * pulled, axis=1, keepdims=True) * scale
        out_ref[q] = product(root, spreads[q] + shift) + means[q]
        shift_row = jnp.sum(jnp.where(diagonal, shift, 0.0), axis=0, keepdims=True)
        increments.append(jnp.sum(root * shift_row, axis=1, keepdims=True))
    return increments


def pack(groups, strips, width, ana_ref, increments, send_ref):
    per_region = strips // REG_DEV
    cells = per_region * width
    states = increments[0].shape[0]
    state = row_of((states, LANES))
    lane = lane_of((states, LANES))
    for r in range(strips):
        q, s = divmod(r, per_region)
        wanted = (lane // width) * cells + s * width + lane % width
        hit = (state == wanted) & (lane < 3 * width)
        row = jnp.sum(jnp.where(hit, increments[q], 0.0), axis=0, keepdims=True)
        row = jnp.broadcast_to(row, (TILE, LANES))
        for group in range(groups):
            block = group * strips + r
            lanes = slice((group // 2) * LANES, (group // 2 + 1) * LANES)
            pair = high_pair if group % 2 else low_pair
            for i in range(3):
                first = i * cells + s * width
                tile = pair(
                    ana_ref[q, first : first + TILE, lanes],
                    ana_ref[q, first + TILE : first + 2 * TILE, lanes],
                )
                send_ref[block, TILE * i : TILE * (i + 1), :] = tile
            send_ref[block, 3 * TILE : 4 * TILE, :] = row


def region_kernel(groups, strips, width, got_ref, info_ref, pull_ref, send_ref, x_ref, ana_ref):
    states = 3 * width * strips // REG_DEV
    if states < x_ref.shape[1]:
        x_ref[:, states:, :] = jnp.zeros_like(x_ref[:, states:, :])
    forecast(groups, strips, width, got_ref, x_ref)
    members = x_ref.shape[2]
    increments = analyse(members, x_ref, info_ref, pull_ref, ana_ref)
    pack(groups, strips, width, ana_ref, increments, send_ref)


def home_kernel(mem, strips, width, got_ref, ctrl_ref, h_ref, u_ref, v_ref, fine_ref):
    blocks = got_ref.shape[0]
    tiles = blocks * width // LANES
    per_tile = LANES // width
    for i, out_ref in enumerate((h_ref, u_ref, v_ref)):
        for t in range(0, tiles, 2):
            rows = []
            for k in range(per_tile):
                even = got_ref[t * per_tile + k, TILE * i : TILE * (i + 1), :]
                odd = got_ref[(t + 1) * per_tile + k, TILE * i : TILE * (i + 1), :]
                rows += [low_pair(even, odd), high_pair(even, odd)]
            turned = jnp.concatenate(rows, axis=0).T
            out_ref[pl.ds(t, mem, stride=tiles), :] = turned[:mem]
            out_ref[pl.ds(t + 1, mem, stride=tiles), :] = turned[mem:]
    mine = lax.axis_index("member") * strips
    per_fine = LANES // (2 * width)
    row = row_of((width, LANES))
    lane = lane_of((width, LANES))
    for t in range(ctrl_ref.shape[3] // LANES):
        rows = [got_ref[mine + t * per_fine + b, 3 * TILE : 4 * TILE, :] for b in range(per_fine)]
        columns = [jnp.concatenate([r] * (LANES // TILE), axis=0).T[:, 0:1] for r in rows]
        for i in range(3):
            total = jnp.zeros((1, LANES), jnp.float32)
            for b in range(per_fine):
                hit = ((lane // 2) % width == row) & (lane // (2 * width) == b)
                part = jnp.where(hit, columns[b][i * width : (i + 1) * width], 0.0)
                total = total + jnp.sum(part, axis=0, keepdims=True)
            lanes = slice(t * LANES, (t + 1) * LANES)
            for e in range(2):
                fine_ref[i, e, :, lanes] = ctrl_ref[i, e, :, lanes] + total


def forecast_kernel(groups, strips, width, got_ref, x_ref):
    forecast(groups, strips, width, got_ref, x_ref)


def pack_kernel(groups, strips, width, ana_ref, inc_ref, send_ref):
    pack(groups, strips, width, ana_ref, [inc_ref[q] for q in range(REG_DEV)], send_ref)


def analyse_in_members(x, obs_index, obs_weight, obs_value, obs_var, obs_count):
    states, members = x.shape[1:]
    mean_state = jnp.mean(x, axis=2, keepdims=True)
    spread = x - mean_state
    picks = (obs_index[:, :, :, None] == jnp.arange(states)).astype(jnp.float32)
    operator = jnp.sum(picks * obs_weight[:, :, :, None], axis=2)
    predicted = jnp.einsum("ros,rsk->rko", operator, x, precision=HIGHEST)
    mean_obs = jnp.mean(predicted, axis=1, keepdims=True)
    obs_spread = predicted - mean_obs
    active_obs = jnp.arange(obs_value.shape[1])[None, :] < obs_count[:, None]
    weighted = obs_spread * (active_obs.astype(jnp.float32) / obs_var)[:, None, :]
    gram_sum = jnp.einsum("rko,rjo->rkj", weighted, obs_spread, precision=HIGHEST)
    identity = jnp.eye(members, dtype=jnp.float32)
    scaled = identity + gram_sum / (members - 1)
    frobenius = jnp.sqrt(jnp.sum(scaled * scaled, axis=(1, 2), keepdims=True))
    iterate = scaled / frobenius
    inverse_root = jnp.broadcast_to(identity, scaled.shape)
    dot = functools.partial(jnp.einsum, "rij,rjk->rik", precision=HIGHEST)
    for _ in range(NEWTON):
        factor = 1.5 * identity - 0.5 * dot(inverse_root, iterate)
        iterate = dot(iterate, factor)
        inverse_root = dot(factor, inverse_root)
    transform = inverse_root / jnp.sqrt(frobenius)
    innovation = jnp.einsum(
        "rko,ro->rk", weighted, obs_value - mean_obs[:, 0], precision=HIGHEST
    )
    halfway = jnp.einsum("rkj,rj->rk", transform, innovation, precision=HIGHEST)
    mean_weights = jnp.einsum("rkj,rj->rk", transform, halfway, precision=HIGHEST) / (members - 1)
    increment = jnp.einsum("rk,rsk->rs", mean_weights, spread, precision=HIGHEST)[:, :, None]
    moved = jnp.einsum("rjk,rsj->rsk", transform, spread, precision=HIGHEST)
    return mean_state + increment + moved, increment


def call(kernel, out_shape, specs, scratch=(), cost=None, name=None):
    many = isinstance(out_shape, tuple)
    return pl.pallas_call(
        kernel,
        out_shape=out_shape,
        in_specs=specs,
        out_specs=tuple(VMEM for _ in out_shape) if many else VMEM,
        scratch_shapes=scratch,
        cost_estimate=cost,
        compiler_params=pltpu.CompilerParams(vmem_limit_bytes=GRANT),
        name=name,
    )


def f32(*shape):
    return jax.ShapeDtypeStruct(shape, jnp.float32)


def near(*shape):
    return pltpu.VMEM(shape, jnp.float32)


def far(array):
    return pltpu.with_memory_space_constraint(array, pltpu.HBM)


def kept(array):
    return pltpu.with_memory_space_constraint(array, pltpu.VMEM)


def shards(
    sample_surface_elevation,
    sample_zonal_current,
    sample_meridional_current,
    zonal_edge_layer_courant,
    meridional_edge_layer_courant,
    obs_index,
    obs_weight,
    obs_value,
    obs_var,
    obs_count,
    fine_ctrl,
):
    groups = lax.axis_size("member")
    strips = lax.axis_size("region")
    owners = ("member", "region")
    mem, rows, columns = sample_surface_elevation.shape
    count = groups * strips
    width = columns // count
    members = groups * mem
    assert rows == 1 and 2 * mem == LANES and width == 2 * TILE and STEPS * 2 == TILE
    assert columns % (2 * LANES) == 0 and groups % 2 == 0 and strips % REG_DEV == 0
    flat = (mem * columns // LANES, LANES)
    states = 3 * width * strips // REG_DEV
    small = states <= members
    later = [fine_ctrl]
    if small:
        later += [obs_index.transpose(0, 2, 1), obs_weight.transpose(0, 2, 1), obs_value, obs_var]
    pair, single, edge, live, ctrl, *seen = call(
        functools.partial(turn_kernel, mem, len(later)),
        (
            near(columns + TILE, LANES),
            near(columns + TILE, LANES),
            near(2, TILE, LANES),
            pltpu.VMEM((REG_DEV, TILE, LANES), jnp.int32),
            *(pltpu.VMEM(array.shape, array.dtype) for array in later),
        ),
        [VMEM] * 5 + [SMEM] + [HBM] * len(later),
        scratch=[pltpu.SemaphoreType.DMA((len(later),))],
        name="turn",
    )(
        far(sample_surface_elevation.reshape(flat)),
        far(sample_zonal_current.reshape(flat)),
        far(sample_meridional_current.reshape(flat)),
        far(zonal_edge_layer_courant),
        far(meridional_edge_layer_courant),
        far(obs_count),
        *(far(array) for array in later),
    )
    from_west = passed_along(edge, "fine", 1)
    from_east = from_west if lax.axis_size("fine") == 2 else passed_along(edge, "fine", -1)
    beside = []
    if small:
        padded = -(-states // LANES) * LANES
        obs = obs_value.shape[1]
        info, pull = call(
            observe_kernel,
            (near(REG_DEV, padded, padded), near(REG_DEV, padded, LANES)),
            [VMEM] * 5,
            cost=pl.CostEstimate(
                flops=12 * REG_DEV * padded * padded * obs, bytes_accessed=1 << 20, transcendentals=0
            ),
            name="observe",
        )(kept(live), *(kept(array) for array in seen))
        beside = [kept(pull)]
    out = call(
        functools.partial(blocks_kernel, width),
        near(count, OUT_ROWS, LANES),
        [VMEM] * (4 + len(beside)),
        name="blocks",
    )(kept(pair), kept(single), kept(from_west), kept(from_east), *beside)
    got = kept(lax.all_to_all(out, owners, split_axis=0, concat_axis=0, tiled=True))
    back_shape = near(count, BACK_ROWS, LANES)
    layout = (groups, strips, width)
    if small:
        back = call(
            functools.partial(region_kernel, *layout),
            back_shape,
            [VMEM] * 3,
            scratch=[
                pltpu.VMEM((REG_DEV, padded, members), jnp.float32),
                pltpu.VMEM((REG_DEV, padded, members), jnp.float32),
            ],
            name="region",
        )(got, kept(info), kept(pull))
    else:
        x = call(
            functools.partial(forecast_kernel, *layout),
            f32(REG_DEV, states, members),
            [VMEM],
            name="forecast",
        )(got)
        analysis, increment = analyse_in_members(
            x, obs_index, obs_weight, obs_value, obs_var, obs_count
        )
        back = call(
            functools.partial(pack_kernel, *layout), back_shape, [VMEM] * 2, name="pack"
        )(analysis, increment)
    home = lax.all_to_all(back, owners, split_axis=0, concat_axis=0, tiled=True)
    ana_h, ana_u, ana_v, fine_out = call(
        functools.partial(home_kernel, mem, strips, width),
        (f32(*flat), f32(*flat), f32(*flat), f32(*fine_ctrl.shape)),
        [VMEM, VMEM],
        name="home",
    )(kept(home), kept(ctrl))
    shape = (mem, rows, columns)
    return (ana_h.reshape(shape), ana_u.reshape(shape), ana_v.reshape(shape), fine_out)


def solution(mesh):
    strip = P("member", "region", "fine")
    owner = ("member", "region", "fine")
    fine = P(None, "region", "fine", "member")
    return jax.shard_map(
        shards,
        mesh=mesh,
        in_specs=(
            strip,
            strip,
            strip,
            P("region", "fine"),
            P("region", "fine"),
            P(owner, None, None),
            P(owner, None, None),
            P(owner, None),
            P(owner, None),
            P(owner),
            fine,
        ),
        out_specs=(strip, strip, strip, fine),
        check_vma=False,
    )
```

```python
import functools

import jax
import jax.numpy as jnp
from jax import lax
from jax.experimental import pallas as pl
from jax.experimental.pallas import tpu as pltpu
from jax.sharding import PartitionSpec as P

REG_DEV = 2
STEPS = 4
NEWTON = 8
LANES = 128
TILE = 8
HALF = LANES // 2
GRANT = 32 << 20

HIGHEST = lax.Precision.HIGHEST
NT = (((1,), (1,)), ((), ()))
NN = (((1,), (0,)), ((), ()))
VMEM = pl.BlockSpec(memory_space=pltpu.VMEM)
SMEM = pl.BlockSpec(memory_space=pltpu.SMEM)
HBM = pl.BlockSpec(memory_space=pltpu.HBM)


def passed_along(block, axis, distance):
    count = lax.axis_size(axis)
    route = [((i - distance) % count, i) for i in range(count)]
    return lax.ppermute(block, axis, route)


def lane_of(shape):
    return lax.broadcasted_iota(jnp.int32, shape, 1)


def row_of(shape):
    return lax.broadcasted_iota(jnp.int32, shape, 0)


def swapped(tile):
    return pltpu.roll(tile, HALF, 1)


def low_pair(even, odd):
    return jnp.where(lane_of(even.shape) < HALF, even, swapped(odd))


def high_pair(even, odd):
    return jnp.where(lane_of(even.shape) < HALF, swapped(even), odd)


def split(value):
    high = value.astype(jnp.bfloat16)
    return high, (value - high.astype(jnp.float32)).astype(jnp.bfloat16)


def beside(value):
    return jnp.concatenate(split(value), axis=1)


def stacked(value):
    both = jnp.concatenate(split(value), axis=1)
    return jnp.concatenate([both, both], axis=0)


def times(left, right):
    out = lax.dot_general(left, right, NN, preferred_element_type=jnp.float32)
    half = out.shape[1] // 2
    return out[:, :half] + out[:, half:]


def squared(value):
    both = jnp.concatenate(split(value), axis=0)
    out = lax.dot_general(both, both, NT, preferred_element_type=jnp.float32)
    half = out.shape[0] // 2
    out = out[:, :half] + out[:, half:]
    return out[:half] + out[half:]


OUT_ROWS = 5 * TILE
BACK_ROWS = 4 * TILE


def turn_kernel(mem, later, *refs):
    sources, refs = refs[: 6 + later], refs[6 + later :]
    pair_ref, single_ref, edge_ref, live_ref = refs[:4]
    targets, sems = refs[4 + later : -1] + refs[4 : 4 + later], refs[-1]
    copies = [
        pltpu.make_async_copy(source, target, sems.at[i])
        for i, (source, target) in enumerate(zip(sources, targets))
    ]
    for copy in copies:
        copy.start()
    h_ref, u_ref, v_ref, zonal_ref, merid_ref, count_ref = targets[:6]
    tiles = h_ref.shape[0] // mem
    columns = tiles * LANES
    zero = jnp.zeros((TILE, LANES), jnp.float32)
    for ref in (pair_ref, single_ref):
        ref[0:TILE, :] = zero
        ref[columns : columns + TILE, :] = zero
    for copy in copies[:5]:
        copy.wait()
    for t in range(tiles):
        rows = pl.ds(t, mem, stride=tiles)
        lanes = slice(t * LANES, (t + 1) * LANES)
        pair = jnp.concatenate([h_ref[rows, :], u_ref[rows, :]], axis=0)
        zonal = jnp.broadcast_to(zonal_ref[:, lanes], (mem // 2, LANES))
        merid = jnp.broadcast_to(merid_ref[:, lanes], (mem // 2, LANES))
        single = jnp.concatenate([v_ref[rows, :], zonal, merid], axis=0)
        place = slice(STEPS + t * LANES, STEPS + (t + 1) * LANES)
        pair_ref[place, :] = pair.T
        single_ref[place, :] = single.T
    early = row_of((TILE, LANES)) < STEPS
    for i, ref in enumerate((pair_ref, single_ref)):
        edge_ref[i] = jnp.where(early, ref[columns : columns + TILE, :], ref[0:TILE, :])
    for copy in copies[5:]:
        copy.wait()
    for q in range(REG_DEV):
        live_ref[q] = jnp.full(live_ref.shape[1:], count_ref[q], jnp.int32)


def blocks_kernel(width, pair_ref, single_ref, west_ref, east_ref, *refs):
    send_ref = refs[-1]
    count = send_ref.shape[0]
    shape = (TILE, LANES)
    early = row_of(shape) < STEPS
    lane = lane_of(shape)
    low = lane < HALF
    part = lane % (HALF // 2)
    for d in range(count):
        pair = [pair_ref[width * d + TILE * j : width * d + TILE * (j + 1), :] for j in range(3)]
        single = [
            single_ref[width * d + TILE * j : width * d + TILE * (j + 1), :] for j in range(3)
        ]
        if d == 0:
            pair[0] = jnp.where(early, west_ref[0], pair[0])
            single[0] = jnp.where(early, west_ref[1], single[0])
        if d == count - 1:
            pair[2] = jnp.where(early, pair[2], east_ref[0])
            single[2] = jnp.where(early, single[2], east_ref[1])
        for j in range(3):
            send_ref[d, TILE * j : TILE * (j + 1), :] = pair[j]
        courant = jnp.where(part == 0, single[0], jnp.where(part == 1, single[1], single[2]))
        send_ref[d, 3 * TILE : 4 * TILE, :] = jnp.where(low, single[0], swapped(single[1]))
        send_ref[d, 4 * TILE : 5 * TILE, :] = jnp.where(low, single[2], courant)


def forecast(groups, strips, width, got_ref, x_ref):
    span = width + 2 * STEPS
    per_region = strips // REG_DEV
    cells = per_region * width

    def tiles_of(group, strip):
        block = group * strips + strip
        return [got_ref[block, TILE * j : TILE * (j + 1), :] for j in range(5)]

    zonal, merid = [], []
    for r in range(strips):
        mixed = got_ref[r, 4 * TILE : 5 * TILE, :]

        def column(first):
            parts = [
                jnp.broadcast_to(mixed[:, first + j : first + j + 1], (TILE, LANES))
                for j in range(3)
            ]
            return jnp.concatenate(parts, axis=0)

        zonal.append(column(HALF))
        merid.append(column(HALF + HALF // 2))
    for lane_tile in range(groups // 2):
        h, u, v = [], [], []
        for r in range(strips):
            even, odd = tiles_of(2 * lane_tile, r), tiles_of(2 * lane_tile + 1, r)
            h.append(jnp.concatenate([low_pair(even[j], odd[j]) for j in range(3)], axis=0))
            u.append(jnp.concatenate([high_pair(even[j], odd[j]) for j in range(3)], axis=0))
            v.append(
                jnp.concatenate(
                    [
                        low_pair(even[3], odd[3]),
                        high_pair(even[3], odd[3]),
                        low_pair(even[4], odd[4]),
                    ],
                    axis=0,
                )
            )
        for _ in range(STEPS):
            flux_v = [merid[r] * v[r] for r in range(strips)]
            for r in range(strips):
                flux_u = zonal[r] * u[r]
                south = flux_v[r - 1] if r else jnp.zeros_like(flux_u)
                h[r] = h[r] - (flux_u - pltpu.roll(flux_u, 1, 0) + flux_v[r] - south)
            for r in range(strips):
                north = h[r + 1] if r + 1 < strips else jnp.zeros_like(h[r])
                u[r] = u[r] - (pltpu.roll(h[r], span - 1, 0) - h[r])
                v[r] = v[r] - (north - h[r])
        lanes = slice(lane_tile * LANES, (lane_tile + 1) * LANES)
        for i, field in enumerate((h, u, v)):
            for r in range(strips):
                q, s = divmod(r, per_region)
                place = slice(i * cells + s * width, i * cells + (s + 1) * width)
                x_ref[q, place, lanes] = pltpu.roll(field[r], span - STEPS, 0)[:width]


def observe_kernel(live_ref, index_ref, weight_ref, value_ref, var_ref, info_ref, pull_ref):
    states = info_ref.shape[1]
    obs = index_ref.shape[2]
    for q in range(REG_DEV):
        state = row_of((states, obs))
        operator = jnp.zeros((states, obs), jnp.float32)
        for j in range(index_ref.shape[1]):
            hit = state == index_ref[q, j : j + 1, :]
            operator = operator + jnp.where(hit, weight_ref[q, j : j + 1, :], 0.0)
        live = lane_of((1, obs)) < live_ref[q, 0:1, 0:1]
        inverse = jnp.where(live, 1.0 / var_ref[q : q + 1, :], 0.0)
        scaled = operator * inverse
        info_ref[q] = lax.dot_general(
            scaled, operator, NT, precision=HIGHEST, preferred_element_type=jnp.float32
        )
        pulled = jnp.sum(scaled * value_ref[q : q + 1, :], axis=1, keepdims=True)
        pull_ref[q] = jnp.broadcast_to(pulled, (states, LANES))


def analyse(members, x_ref, info_ref, pull_ref, out_ref):
    states = x_ref.shape[1]
    square = (states, states)
    diagonal = row_of(square) == lane_of(square)
    identity = jnp.where(diagonal, 1.0, 0.0)
    regions = range(REG_DEV)
    scale = 1.0 / (members - 1)

    def as_row(column):
        return jnp.sum(jnp.where(diagonal, column, 0.0), axis=0, keepdims=True)

    def applied(matrix, row):
        return jnp.sum(matrix * row, axis=1, keepdims=True)

    x = [x_ref[q] for q in regions]
    means = [jnp.sum(x[q], axis=1, keepdims=True) / members for q in regions]
    spreads = [x[q] - means[q] for q in regions]
    covs = [squared(spreads[q]) for q in regions]
    gains = [times(beside(covs[q]), stacked(info_ref[q] * scale)) for q in regions]
    rights = [stacked(gains[q]) for q in regions]
    gains_2 = [times(beside(gains[q]), rights[q]) for q in regions]
    pulls, inverse_norms, firsts, iterates, inverses = [], [], [], [], []
    for q in regions:
        pulled = pull_ref[q][:, 0:1] - applied(info_ref[q], as_row(means[q]))
        pulls.append(jnp.sum(covs[q] * pulled, axis=0, keepdims=True))
        trace = jnp.sum(jnp.where(diagonal, gains_2[q] + 2.0 * gains[q], 0.0), keepdims=True)
        inverse_norms.append(lax.rsqrt(trace + members))
    for q in regions:
        norm = inverse_norms[q]
        first = (identity + gains[q]) * norm
        second = (identity + 2.0 * gains[q] + gains_2[q]) * (norm * norm)
        third = (second + times(beside(second), rights[q])) * norm
        inverses.append(1.5 * identity - 0.5 * first)
        iterates.append(2.25 * first - 1.5 * second + 0.25 * third)
    for sweep in range(1, NEWTON - 1):
        rights = [stacked(iterates[q]) for q in regions]
        lefts = [
            jnp.concatenate([beside(iterates[q]), beside(inverses[q])], axis=0) for q in regions
        ]
        both = [times(lefts[q], rights[q]) for q in regions]
        seconds = [both[q][:states] for q in regions]
        thirds = [times(beside(seconds[q]), rights[q]) for q in regions]
        inverses = [1.5 * inverses[q] - 0.5 * both[q][states:] for q in regions]
        iterates = [
            2.25 * iterates[q] - 1.5 * seconds[q] + 0.25 * thirds[q] for q in regions
        ]
    increments = []
    for q in regions:
        high, low = split(spreads[q])
        wide = beside(inverses[q])
        moved = lax.dot_general(
            wide, jnp.concatenate([high, high], axis=0), NN, preferred_element_type=jnp.float32
        )
        moved = moved + lax.dot_general(
            wide[:, :states], low, NN, preferred_element_type=jnp.float32
        )
        twice = applied(inverses[q], as_row(applied(inverses[q], pulls[q])))
        factor = 1.5 * identity - 0.5 * iterates[q]
        twice = applied(factor, as_row(applied(factor, as_row(twice))))
        increment = twice * (inverse_norms[q] * scale)
        increments.append(increment)
        high, low = split(moved * jnp.sqrt(inverse_norms[q]))
        wide = beside(factor)
        moved = lax.dot_general(
            wide, jnp.concatenate([high, high], axis=0), NN, preferred_element_type=jnp.float32
        )
        moved = moved + lax.dot_general(
            wide[:, :states], low, NN, preferred_element_type=jnp.float32
        )
        out_ref[q] = moved + (means[q] + increment)
    return increments


def pack(groups, strips, width, ana_ref, increments, send_ref):
    per_region = strips // REG_DEV
    cells = per_region * width
    states = increments[0].shape[0]
    state = row_of((states, LANES))
    lane = lane_of((states, LANES))
    for r in range(strips):
        q, s = divmod(r, per_region)
        wanted = (lane // width) * cells + s * width + lane % width
        hit = (state == wanted) & (lane < 3 * width)
        row = jnp.sum(jnp.where(hit, increments[q], 0.0), axis=0, keepdims=True)
        row = jnp.broadcast_to(row, (TILE, LANES))
        for group in range(groups):
            block = group * strips + r
            lanes = slice((group // 2) * LANES, (group // 2 + 1) * LANES)
            pair = high_pair if group % 2 else low_pair
            for i in range(3):
                first = i * cells + s * width
                tile = pair(
                    ana_ref[q, first : first + TILE, lanes],
                    ana_ref[q, first + TILE : first + 2 * TILE, lanes],
                )
                send_ref[block, TILE * i : TILE * (i + 1), :] = tile
            send_ref[block, 3 * TILE : 4 * TILE, :] = row


def region_kernel(groups, strips, width, got_ref, info_ref, pull_ref, send_ref, x_ref, ana_ref):
    states = 3 * width * strips // REG_DEV
    if states < x_ref.shape[1]:
        x_ref[:, states:, :] = jnp.zeros_like(x_ref[:, states:, :])
    forecast(groups, strips, width, got_ref, x_ref)
    members = x_ref.shape[2]
    increments = analyse(members, x_ref, info_ref, pull_ref, ana_ref)
    pack(groups, strips, width, ana_ref, increments, send_ref)


def home_kernel(mem, strips, width, got_ref, ctrl_ref, h_ref, u_ref, v_ref, fine_ref):
    blocks = got_ref.shape[0]
    tiles = blocks * width // LANES
    per_tile = LANES // width
    for i, out_ref in enumerate((h_ref, u_ref, v_ref)):
        for t in range(0, tiles, 2):
            rows = []
            for k in range(per_tile):
                even = got_ref[t * per_tile + k, TILE * i : TILE * (i + 1), :]
                odd = got_ref[(t + 1) * per_tile + k, TILE * i : TILE * (i + 1), :]
                rows += [low_pair(even, odd), high_pair(even, odd)]
            turned = jnp.concatenate(rows, axis=0).T
            out_ref[pl.ds(t, mem, stride=tiles), :] = turned[:mem]
            out_ref[pl.ds(t + 1, mem, stride=tiles), :] = turned[mem:]
    mine = lax.axis_index("member") * strips
    per_fine = LANES // (2 * width)
    row = row_of((width, LANES))
    lane = lane_of((width, LANES))
    for t in range(ctrl_ref.shape[3] // LANES):
        rows = [got_ref[mine + t * per_fine + b, 3 * TILE : 4 * TILE, :] for b in range(per_fine)]
        columns = [jnp.concatenate([r] * (LANES // TILE), axis=0).T[:, 0:1] for r in rows]
        for i in range(3):
            total = jnp.zeros((1, LANES), jnp.float32)
            for b in range(per_fine):
                hit = ((lane // 2) % width == row) & (lane // (2 * width) == b)
                part = jnp.where(hit, columns[b][i * width : (i + 1) * width], 0.0)
                total = total + jnp.sum(part, axis=0, keepdims=True)
            lanes = slice(t * LANES, (t + 1) * LANES)
            for e in range(2):
                fine_ref[i, e, :, lanes] = ctrl_ref[i, e, :, lanes] + total


def forecast_kernel(groups, strips, width, got_ref, x_ref):
    forecast(groups, strips, width, got_ref, x_ref)


def pack_kernel(groups, strips, width, ana_ref, inc_ref, send_ref):
    pack(groups, strips, width, ana_ref, [inc_ref[q] for q in range(REG_DEV)], send_ref)


def analyse_in_members(x, obs_index, obs_weight, obs_value, obs_var, obs_count):
    states, members = x.shape[1:]
    mean_state = jnp.mean(x, axis=2, keepdims=True)
    spread = x - mean_state
    picks = (obs_index[:, :, :, None] == jnp.arange(states)).astype(jnp.float32)
    operator = jnp.sum(picks * obs_weight[:, :, :, None], axis=2)
    predicted = jnp.einsum("ros,rsk->rko", operator, x, precision=HIGHEST)
    mean_obs = jnp.mean(predicted, axis=1, keepdims=True)
    obs_spread = predicted - mean_obs
    active_obs = jnp.arange(obs_value.shape[1])[None, :] < obs_count[:, None]
    weighted = obs_spread * (active_obs.astype(jnp.float32) / obs_var)[:, None, :]
    gram_sum = jnp.einsum("rko,rjo->rkj", weighted, obs_spread, precision=HIGHEST)
    identity = jnp.eye(members, dtype=jnp.float32)
    scaled = identity + gram_sum / (members - 1)
    frobenius = jnp.sqrt(jnp.sum(scaled * scaled, axis=(1, 2), keepdims=True))
    iterate = scaled / frobenius
    inverse_root = jnp.broadcast_to(identity, scaled.shape)
    dot = functools.partial(jnp.einsum, "rij,rjk->rik", precision=HIGHEST)
    for _ in range(NEWTON):
        factor = 1.5 * identity - 0.5 * dot(inverse_root, iterate)
        iterate = dot(iterate, factor)
        inverse_root = dot(factor, inverse_root)
    transform = inverse_root / jnp.sqrt(frobenius)
    innovation = jnp.einsum(
        "rko,ro->rk", weighted, obs_value - mean_obs[:, 0], precision=HIGHEST
    )
    halfway = jnp.einsum("rkj,rj->rk", transform, innovation, precision=HIGHEST)
    mean_weights = jnp.einsum("rkj,rj->rk", transform, halfway, precision=HIGHEST) / (members - 1)
    increment = jnp.einsum("rk,rsk->rs", mean_weights, spread, precision=HIGHEST)[:, :, None]
    moved = jnp.einsum("rjk,rsj->rsk", transform, spread, precision=HIGHEST)
    return mean_state + increment + moved, increment


def call(kernel, out_shape, specs, scratch=(), cost=None, name=None):
    many = isinstance(out_shape, tuple)
    return pl.pallas_call(
        kernel,
        out_shape=out_shape,
        in_specs=specs,
        out_specs=tuple(VMEM for _ in out_shape) if many else VMEM,
        scratch_shapes=scratch,
        cost_estimate=cost,
        compiler_params=pltpu.CompilerParams(vmem_limit_bytes=GRANT),
        name=name,
    )


def f32(*shape):
    return jax.ShapeDtypeStruct(shape, jnp.float32)


def near(*shape):
    return pltpu.VMEM(shape, jnp.float32)


def far(array):
    return pltpu.with_memory_space_constraint(array, pltpu.HBM)


def kept(array):
    return pltpu.with_memory_space_constraint(array, pltpu.VMEM)


def shards(
    sample_surface_elevation,
    sample_zonal_current,
    sample_meridional_current,
    zonal_edge_layer_courant,
    meridional_edge_layer_courant,
    obs_index,
    obs_weight,
    obs_value,
    obs_var,
    obs_count,
    fine_ctrl,
):
    groups = lax.axis_size("member")
    strips = lax.axis_size("region")
    owners = ("member", "region")
    mem, rows, columns = sample_surface_elevation.shape
    count = groups * strips
    width = columns // count
    members = groups * mem
    assert rows == 1 and 2 * mem == LANES and width == 2 * TILE and STEPS * 2 == TILE
    assert columns % (2 * LANES) == 0 and groups % 2 == 0 and strips % REG_DEV == 0
    flat = (mem * columns // LANES, LANES)
    states = 3 * width * strips // REG_DEV
    small = states <= members
    later = [fine_ctrl]
    if small:
        later += [obs_index.transpose(0, 2, 1), obs_weight.transpose(0, 2, 1), obs_value, obs_var]
    pair, single, edge, live, ctrl, *seen = call(
        functools.partial(turn_kernel, mem, len(later)),
        (
            near(columns + TILE, LANES),
            near(columns + TILE, LANES),
            near(2, TILE, LANES),
            pltpu.VMEM((REG_DEV, TILE, LANES), jnp.int32),
            *(pltpu.VMEM(array.shape, array.dtype) for array in later),
        ),
        [HBM] * (6 + len(later)),
        scratch=[
            *[pltpu.VMEM(flat, jnp.float32)] * 3,
            *[pltpu.VMEM((1, columns), jnp.float32)] * 2,
            pltpu.SMEM((REG_DEV,), jnp.int32),
            pltpu.SemaphoreType.DMA((6 + len(later),)),
        ],
        name="turn",
    )(
        far(sample_surface_elevation.reshape(flat)),
        far(sample_zonal_current.reshape(flat)),
        far(sample_meridional_current.reshape(flat)),
        far(zonal_edge_layer_courant),
        far(meridional_edge_layer_courant),
        far(obs_count),
        *(far(array) for array in later),
    )
    from_west = passed_along(edge, "fine", 1)
    from_east = from_west if lax.axis_size("fine") == 2 else passed_along(edge, "fine", -1)
    ahead = []
    if small:
        padded = -(-states // LANES) * LANES
        obs = obs_value.shape[1]
        info, pull = call(
            observe_kernel,
            (near(REG_DEV, padded, padded), near(REG_DEV, padded, LANES)),
            [VMEM] * 5,
            cost=pl.CostEstimate(
                flops=12 * REG_DEV * padded * padded * obs, bytes_accessed=1 << 20, transcendentals=0
            ),
            name="observe",
        )(kept(live), *(kept(array) for array in seen))
        ahead = [kept(pull)]
    out = call(
        functools.partial(blocks_kernel, width),
        near(count, OUT_ROWS, LANES),
        [VMEM] * (4 + len(ahead)),
        name="blocks",
    )(kept(pair), kept(single), kept(from_west), kept(from_east), *ahead)
    got = kept(lax.all_to_all(out, owners, split_axis=0, concat_axis=0, tiled=True))
    back_shape = near(count, BACK_ROWS, LANES)
    layout = (groups, strips, width)
    if small:
        back = call(
            functools.partial(region_kernel, *layout),
            back_shape,
            [VMEM] * 3,
            scratch=[
                pltpu.VMEM((REG_DEV, padded, members), jnp.float32),
                pltpu.VMEM((REG_DEV, padded, members), jnp.float32),
            ],
            name="region",
        )(got, kept(info), kept(pull))
    else:
        x = call(
            functools.partial(forecast_kernel, *layout),
            f32(REG_DEV, states, members),
            [VMEM],
            name="forecast",
        )(got)
        analysis, increment = analyse_in_members(
            x, obs_index, obs_weight, obs_value, obs_var, obs_count
        )
        back = call(
            functools.partial(pack_kernel, *layout), back_shape, [VMEM] * 2, name="pack"
        )(analysis, increment)
    home = lax.all_to_all(back, owners, split_axis=0, concat_axis=0, tiled=True)
    ana_h, ana_u, ana_v, fine_out = call(
        functools.partial(home_kernel, mem, strips, width),
        (f32(*flat), f32(*flat), f32(*flat), f32(*fine_ctrl.shape)),
        [VMEM, VMEM],
        name="home",
    )(kept(home), kept(ctrl))
    shape = (mem, rows, columns)
    return (ana_h.reshape(shape), ana_u.reshape(shape), ana_v.reshape(shape), fine_out)


def solution(mesh):
    strip = P("member", "region", "fine")
    owner = ("member", "region", "fine")
    fine = P(None, "region", "fine", "member")
    return jax.shard_map(
        shards,
        mesh=mesh,
        in_specs=(
            strip,
            strip,
            strip,
            P("region", "fine"),
            P("region", "fine"),
            P(owner, None, None),
            P(owner, None, None),
            P(owner, None),
            P(owner, None),
            P(owner),
            fine,
        ),
        out_specs=(strip, strip, strip, fine),
        check_vma=False,
    )
```

```python
import functools

import jax
import jax.numpy as jnp
from jax import lax
from jax.experimental import pallas as pl
from jax.experimental.pallas import tpu as pltpu
from jax.sharding import PartitionSpec as P

REG_DEV = 2
STEPS = 4
NEWTON = 8
LANES = 128
TILE = 8
HALF = LANES // 2
GRANT = 32 << 20

HIGHEST = lax.Precision.HIGHEST
NT = (((1,), (1,)), ((), ()))
NN = (((1,), (0,)), ((), ()))
VMEM = pl.BlockSpec(memory_space=pltpu.VMEM)
SMEM = pl.BlockSpec(memory_space=pltpu.SMEM)
HBM = pl.BlockSpec(memory_space=pltpu.HBM)


def passed_along(block, axis, distance):
    count = lax.axis_size(axis)
    route = [((i - distance) % count, i) for i in range(count)]
    return lax.ppermute(block, axis, route)


def lane_of(shape):
    return lax.broadcasted_iota(jnp.int32, shape, 1)


def row_of(shape):
    return lax.broadcasted_iota(jnp.int32, shape, 0)


def swapped(tile):
    return pltpu.roll(tile, HALF, 1)


def low_pair(even, odd):
    return jnp.where(lane_of(even.shape) < HALF, even, swapped(odd))


def high_pair(even, odd):
    return jnp.where(lane_of(even.shape) < HALF, swapped(even), odd)


def split(value):
    high = value.astype(jnp.bfloat16)
    return high, (value - high.astype(jnp.float32)).astype(jnp.bfloat16)


def beside(value):
    return jnp.concatenate(split(value), axis=1)


def stacked(value):
    both = jnp.concatenate(split(value), axis=1)
    return jnp.concatenate([both, both], axis=0)


def times(left, right):
    out = lax.dot_general(left, right, NN, preferred_element_type=jnp.float32)
    half = out.shape[1] // 2
    return out[:, :half] + out[:, half:]


def squared(value):
    both = jnp.concatenate(split(value), axis=0)
    out = lax.dot_general(both, both, NT, preferred_element_type=jnp.float32)
    half = out.shape[0] // 2
    out = out[:, :half] + out[:, half:]
    return out[:half] + out[half:]


OUT_ROWS = 5 * TILE
BACK_ROWS = 3 * TILE + 1


def turn_kernel(mem, later, *refs):
    sources, refs = refs[: 6 + later], refs[6 + later :]
    pair_ref, single_ref, edge_ref, live_ref = refs[:4]
    targets, sems = refs[4 + later : -1] + refs[4 : 4 + later], refs[-1]
    copies = [
        pltpu.make_async_copy(source, target, sems.at[i])
        for i, (source, target) in enumerate(zip(sources, targets))
    ]
    for copy in copies:
        copy.start()
    h_ref, u_ref, v_ref, zonal_ref, merid_ref, count_ref = targets[:6]
    tiles = h_ref.shape[0] // mem
    columns = tiles * LANES
    zero = jnp.zeros((TILE, LANES), jnp.float32)
    for ref in (pair_ref, single_ref):
        ref[0:TILE, :] = zero
        ref[columns : columns + TILE, :] = zero
    for copy in copies[:5]:
        copy.wait()
    for t in range(tiles):
        rows = pl.ds(t, mem, stride=tiles)
        lanes = slice(t * LANES, (t + 1) * LANES)
        pair = jnp.concatenate([h_ref[rows, :], u_ref[rows, :]], axis=0)
        zonal = jnp.broadcast_to(zonal_ref[:, lanes], (mem // 2, LANES))
        merid = jnp.broadcast_to(merid_ref[:, lanes], (mem // 2, LANES))
        single = jnp.concatenate([v_ref[rows, :], zonal, merid], axis=0)
        place = slice(STEPS + t * LANES, STEPS + (t + 1) * LANES)
        pair_ref[place, :] = pair.T
        single_ref[place, :] = single.T
    early = row_of((TILE, LANES)) < STEPS
    for i, ref in enumerate((pair_ref, single_ref)):
        edge_ref[i] = jnp.where(early, ref[columns : columns + TILE, :], ref[0:TILE, :])
    for copy in copies[5:]:
        copy.wait()
    for q in range(REG_DEV):
        live_ref[q] = jnp.full(live_ref.shape[1:], count_ref[q], jnp.int32)


def blocks_kernel(width, pair_ref, single_ref, west_ref, east_ref, *refs):
    send_ref = refs[-1]
    count = send_ref.shape[0]
    shape = (TILE, LANES)
    early = row_of(shape) < STEPS
    lane = lane_of(shape)
    low = lane < HALF
    part = lane % (HALF // 2)
    for d in range(count):
        pair = [pair_ref[width * d + TILE * j : width * d + TILE * (j + 1), :] for j in range(3)]
        single = [
            single_ref[width * d + TILE * j : width * d + TILE * (j + 1), :] for j in range(3)
        ]
        if d == 0:
            pair[0] = jnp.where(early, west_ref[0], pair[0])
            single[0] = jnp.where(early, west_ref[1], single[0])
        if d == count - 1:
            pair[2] = jnp.where(early, pair[2], east_ref[0])
            single[2] = jnp.where(early, single[2], east_ref[1])
        for j in range(3):
            send_ref[d, TILE * j : TILE * (j + 1), :] = pair[j]
        courant = jnp.where(part == 0, single[0], jnp.where(part == 1, single[1], single[2]))
        send_ref[d, 3 * TILE : 4 * TILE, :] = jnp.where(low, single[0], swapped(single[1]))
        send_ref[d, 4 * TILE : 5 * TILE, :] = jnp.where(low, single[2], courant)


def forecast(groups, strips, width, got_ref, x_ref):
    span = width + 2 * STEPS
    per_region = strips // REG_DEV
    cells = per_region * width

    def tiles_of(group, strip):
        block = group * strips + strip
        return [got_ref[block, TILE * j : TILE * (j + 1), :] for j in range(5)]

    zonal, merid = [], []
    for r in range(strips):
        mixed = got_ref[r, 4 * TILE : 5 * TILE, :]

        def column(first):
            parts = [
                jnp.broadcast_to(mixed[:, first + j : first + j + 1], (TILE, LANES))
                for j in range(3)
            ]
            return jnp.concatenate(parts, axis=0)

        zonal.append(column(HALF))
        merid.append(column(HALF + HALF // 2))
    for lane_tile in range(groups // 2):
        h, u, v = [], [], []
        for r in range(strips):
            even, odd = tiles_of(2 * lane_tile, r), tiles_of(2 * lane_tile + 1, r)
            h.append(jnp.concatenate([low_pair(even[j], odd[j]) for j in range(3)], axis=0))
            u.append(jnp.concatenate([high_pair(even[j], odd[j]) for j in range(3)], axis=0))
            v.append(
                jnp.concatenate(
                    [
                        low_pair(even[3], odd[3]),
                        high_pair(even[3], odd[3]),
                        low_pair(even[4], odd[4]),
                    ],
                    axis=0,
                )
            )
        for _ in range(STEPS):
            flux_v = [merid[r] * v[r] for r in range(strips)]
            for r in range(strips):
                flux_u = zonal[r] * u[r]
                south = flux_v[r - 1] if r else jnp.zeros_like(flux_u)
                h[r] = h[r] - (flux_u - pltpu.roll(flux_u, 1, 0) + flux_v[r] - south)
            for r in range(strips):
                north = h[r + 1] if r + 1 < strips else jnp.zeros_like(h[r])
                u[r] = u[r] - (pltpu.roll(h[r], span - 1, 0) - h[r])
                v[r] = v[r] - (north - h[r])
        lanes = slice(lane_tile * LANES, (lane_tile + 1) * LANES)
        for i, field in enumerate((h, u, v)):
            for r in range(strips):
                q, s = divmod(r, per_region)
                place = slice(i * cells + s * width, i * cells + (s + 1) * width)
                x_ref[q, place, lanes] = pltpu.roll(field[r], span - STEPS, 0)[:width]


def observe_kernel(live_ref, index_ref, weight_ref, value_ref, var_ref, info_ref, pull_ref):
    states = info_ref.shape[1]
    obs = index_ref.shape[2]
    for q in range(REG_DEV):
        state = row_of((states, obs))
        operator = jnp.zeros((states, obs), jnp.float32)
        for j in range(index_ref.shape[1]):
            hit = state == index_ref[q, j : j + 1, :]
            operator = operator + jnp.where(hit, weight_ref[q, j : j + 1, :], 0.0)
        live = lane_of((1, obs)) < live_ref[q, 0:1, 0:1]
        inverse = jnp.where(live, 1.0 / var_ref[q : q + 1, :], 0.0)
        scaled = operator * inverse
        info_ref[q] = lax.dot_general(
            scaled, operator, NT, precision=HIGHEST, preferred_element_type=jnp.float32
        )
        pulled = jnp.sum(scaled * value_ref[q : q + 1, :], axis=1, keepdims=True)
        pull_ref[q] = jnp.broadcast_to(pulled, (states, LANES))


def analyse(members, x_ref, info_ref, pull_ref, out_ref):
    states = x_ref.shape[1]
    square = (states, states)
    diagonal = row_of(square) == lane_of(square)
    identity = jnp.where(diagonal, 1.0, 0.0)
    regions = range(REG_DEV)
    scale = 1.0 / (members - 1)

    def as_row(column):
        return jnp.sum(jnp.where(diagonal, column, 0.0), axis=0, keepdims=True)

    def applied(matrix, row):
        return jnp.sum(matrix * row, axis=1, keepdims=True)

    x = [x_ref[q] for q in regions]
    means = [jnp.sum(x[q], axis=1, keepdims=True) / members for q in regions]
    spreads = [x[q] - means[q] for q in regions]
    covs = [squared(spreads[q]) for q in regions]
    gains = [times(beside(covs[q]), stacked(info_ref[q] * scale)) for q in regions]
    rights = [stacked(gains[q]) for q in regions]
    gains_2 = [times(beside(gains[q]), rights[q]) for q in regions]
    pulls, inverse_norms, firsts, iterates, inverses = [], [], [], [], []
    for q in regions:
        pulled = pull_ref[q][:, 0:1] - applied(info_ref[q], as_row(means[q]))
        pulls.append(jnp.sum(covs[q] * pulled, axis=0, keepdims=True))
        trace = jnp.sum(jnp.where(diagonal, gains_2[q] + 2.0 * gains[q], 0.0), keepdims=True)
        inverse_norms.append(lax.rsqrt(trace + members))
    for q in regions:
        norm = inverse_norms[q]
        first = (identity + gains[q]) * norm
        second = (identity + 2.0 * gains[q] + gains_2[q]) * (norm * norm)
        third = (second + times(beside(second), rights[q])) * norm
        inverses.append(1.5 * identity - 0.5 * first)
        iterates.append(2.25 * first - 1.5 * second + 0.25 * third)
    for sweep in range(1, NEWTON - 1):
        rights = [stacked(iterates[q]) for q in regions]
        lefts = [
            jnp.concatenate([beside(iterates[q]), beside(inverses[q])], axis=0) for q in regions
        ]
        both = [times(lefts[q], rights[q]) for q in regions]
        seconds = [both[q][:states] for q in regions]
        thirds = [times(beside(seconds[q]), rights[q]) for q in regions]
        inverses = [1.5 * inverses[q] - 0.5 * both[q][states:] for q in regions]
        iterates = [
            2.25 * iterates[q] - 1.5 * seconds[q] + 0.25 * thirds[q] for q in regions
        ]
    increments = []
    for q in regions:
        high, low = split(spreads[q])
        wide = beside(inverses[q])
        moved = lax.dot_general(
            wide, jnp.concatenate([high, high], axis=0), NN, preferred_element_type=jnp.float32
        )
        moved = moved + lax.dot_general(
            wide[:, :states], low, NN, preferred_element_type=jnp.float32
        )
        twice = applied(inverses[q], as_row(applied(inverses[q], pulls[q])))
        factor = 1.5 * identity - 0.5 * iterates[q]
        twice = applied(factor, as_row(applied(factor, as_row(twice))))
        increment = twice * (inverse_norms[q] * scale)
        increments.append(increment)
        high, low = split(moved * jnp.sqrt(inverse_norms[q]))
        wide = beside(factor)
        moved = lax.dot_general(
            wide, jnp.concatenate([high, high], axis=0), NN, preferred_element_type=jnp.float32
        )
        moved = moved + lax.dot_general(
            wide[:, :states], low, NN, preferred_element_type=jnp.float32
        )
        out_ref[q] = moved + (means[q] + increment)
    return increments


def pack(groups, strips, width, ana_ref, increments, send_ref):
    per_region = strips // REG_DEV
    cells = per_region * width
    states = increments[0].shape[0]
    state = row_of((states, LANES))
    lane = lane_of((states, LANES))
    for r in range(strips):
        q, s = divmod(r, per_region)
        wanted = (lane // width) * cells + s * width + lane % width
        hit = (state == wanted) & (lane < 3 * width)
        row = jnp.sum(jnp.where(hit, increments[q], 0.0), axis=0, keepdims=True)
        for group in range(groups):
            block = group * strips + r
            lanes = slice((group // 2) * LANES, (group // 2 + 1) * LANES)
            pair = high_pair if group % 2 else low_pair
            for i in range(3):
                first = i * cells + s * width
                tile = pair(
                    ana_ref[q, first : first + TILE, lanes],
                    ana_ref[q, first + TILE : first + 2 * TILE, lanes],
                )
                send_ref[BACK_ROWS * block + TILE * i : BACK_ROWS * block + TILE * (i + 1), :] = tile
            send_ref[BACK_ROWS * (block + 1) - 1 : BACK_ROWS * (block + 1), :] = row


def region_kernel(groups, strips, width, got_ref, info_ref, pull_ref, send_ref, x_ref, ana_ref):
    states = 3 * width * strips // REG_DEV
    if states < x_ref.shape[1]:
        x_ref[:, states:, :] = jnp.zeros_like(x_ref[:, states:, :])
    forecast(groups, strips, width, got_ref, x_ref)
    members = x_ref.shape[2]
    increments = analyse(members, x_ref, info_ref, pull_ref, ana_ref)
    pack(groups, strips, width, ana_ref, increments, send_ref)


def home_kernel(mem, strips, width, got_ref, ctrl_ref, h_ref, u_ref, v_ref, fine_ref):
    tiles = got_ref.shape[0] // BACK_ROWS * width // LANES
    per_tile = LANES // width
    for i, out_ref in enumerate((h_ref, u_ref, v_ref)):
        for t in range(0, tiles, 2):
            rows = []
            for k in range(per_tile):
                first = BACK_ROWS * (t * per_tile + k) + TILE * i
                even = got_ref[first : first + TILE, :]
                first += BACK_ROWS * per_tile
                odd = got_ref[first : first + TILE, :]
                rows += [low_pair(even, odd), high_pair(even, odd)]
            turned = jnp.concatenate(rows, axis=0).T
            out_ref[pl.ds(t, mem, stride=tiles), :] = turned[:mem]
            out_ref[pl.ds(t + 1, mem, stride=tiles), :] = turned[mem:]
    mine = lax.axis_index("member") * strips
    per_fine = LANES // (2 * width)
    row = row_of((width, LANES))
    lane = lane_of((width, LANES))
    for t in range(ctrl_ref.shape[3] // LANES):
        rows = [
            got_ref[pl.ds(BACK_ROWS * (mine + t * per_fine + b) + BACK_ROWS - 1, 1), :]
            for b in range(per_fine)
        ]
        columns = [jnp.broadcast_to(r, (LANES, LANES)).T[:, 0:1] for r in rows]
        for i in range(3):
            total = jnp.zeros((1, LANES), jnp.float32)
            for b in range(per_fine):
                hit = ((lane // 2) % width == row) & (lane // (2 * width) == b)
                part = jnp.where(hit, columns[b][i * width : (i + 1) * width], 0.0)
                total = total + jnp.sum(part, axis=0, keepdims=True)
            lanes = slice(t * LANES, (t + 1) * LANES)
            for e in range(2):
                fine_ref[i, e, :, lanes] = ctrl_ref[i, e, :, lanes] + total


def forecast_kernel(groups, strips, width, got_ref, x_ref):
    forecast(groups, strips, width, got_ref, x_ref)


def pack_kernel(groups, strips, width, ana_ref, inc_ref, send_ref):
    pack(groups, strips, width, ana_ref, [inc_ref[q] for q in range(REG_DEV)], send_ref)


def analyse_in_members(x, obs_index, obs_weight, obs_value, obs_var, obs_count):
    states, members = x.shape[1:]
    mean_state = jnp.mean(x, axis=2, keepdims=True)
    spread = x - mean_state
    picks = (obs_index[:, :, :, None] == jnp.arange(states)).astype(jnp.float32)
    operator = jnp.sum(picks * obs_weight[:, :, :, None], axis=2)
    predicted = jnp.einsum("ros,rsk->rko", operator, x, precision=HIGHEST)
    mean_obs = jnp.mean(predicted, axis=1, keepdims=True)
    obs_spread = predicted - mean_obs
    active_obs = jnp.arange(obs_value.shape[1])[None, :] < obs_count[:, None]
    weighted = obs_spread * (active_obs.astype(jnp.float32) / obs_var)[:, None, :]
    gram_sum = jnp.einsum("rko,rjo->rkj", weighted, obs_spread, precision=HIGHEST)
    identity = jnp.eye(members, dtype=jnp.float32)
    scaled = identity + gram_sum / (members - 1)
    frobenius = jnp.sqrt(jnp.sum(scaled * scaled, axis=(1, 2), keepdims=True))
    iterate = scaled / frobenius
    inverse_root = jnp.broadcast_to(identity, scaled.shape)
    dot = functools.partial(jnp.einsum, "rij,rjk->rik", precision=HIGHEST)
    for _ in range(NEWTON):
        factor = 1.5 * identity - 0.5 * dot(inverse_root, iterate)
        iterate = dot(iterate, factor)
        inverse_root = dot(factor, inverse_root)
    transform = inverse_root / jnp.sqrt(frobenius)
    innovation = jnp.einsum(
        "rko,ro->rk", weighted, obs_value - mean_obs[:, 0], precision=HIGHEST
    )
    halfway = jnp.einsum("rkj,rj->rk", transform, innovation, precision=HIGHEST)
    mean_weights = jnp.einsum("rkj,rj->rk", transform, halfway, precision=HIGHEST) / (members - 1)
    increment = jnp.einsum("rk,rsk->rs", mean_weights, spread, precision=HIGHEST)[:, :, None]
    moved = jnp.einsum("rjk,rsj->rsk", transform, spread, precision=HIGHEST)
    return mean_state + increment + moved, increment


def call(kernel, out_shape, specs, scratch=(), cost=None, name=None):
    many = isinstance(out_shape, tuple)
    return pl.pallas_call(
        kernel,
        out_shape=out_shape,
        in_specs=specs,
        out_specs=tuple(VMEM for _ in out_shape) if many else VMEM,
        scratch_shapes=scratch,
        cost_estimate=cost,
        compiler_params=pltpu.CompilerParams(vmem_limit_bytes=GRANT),
        name=name,
    )


def exchanged(blocks, axes, count):
    dense = blocks.reshape(count, -1, 1, LANES)
    return lax.all_to_all(dense, axes, split_axis=0, concat_axis=0, tiled=True).reshape(blocks.shape)


def f32(*shape):
    return jax.ShapeDtypeStruct(shape, jnp.float32)


def near(*shape):
    return pltpu.VMEM(shape, jnp.float32)


def far(array):
    return pltpu.with_memory_space_constraint(array, pltpu.HBM)


def kept(array):
    return pltpu.with_memory_space_constraint(array, pltpu.VMEM)


def shards(
    sample_surface_elevation,
    sample_zonal_current,
    sample_meridional_current,
    zonal_edge_layer_courant,
    meridional_edge_layer_courant,
    obs_index,
    obs_weight,
    obs_value,
    obs_var,
    obs_count,
    fine_ctrl,
):
    groups = lax.axis_size("member")
    strips = lax.axis_size("region")
    owners = ("member", "region")
    mem, rows, columns = sample_surface_elevation.shape
    count = groups * strips
    width = columns // count
    members = groups * mem
    assert rows == 1 and 2 * mem == LANES and width == 2 * TILE and STEPS * 2 == TILE
    assert columns % (2 * LANES) == 0 and groups % 2 == 0 and strips % REG_DEV == 0
    flat = (mem * columns // LANES, LANES)
    states = 3 * width * strips // REG_DEV
    small = states <= members
    later = [fine_ctrl]
    if small:
        later += [obs_index.transpose(0, 2, 1), obs_weight.transpose(0, 2, 1), obs_value, obs_var]
    pair, single, edge, live, ctrl, *seen = call(
        functools.partial(turn_kernel, mem, len(later)),
        (
            near(columns + TILE, LANES),
            near(columns + TILE, LANES),
            near(2, TILE, LANES),
            pltpu.VMEM((REG_DEV, TILE, LANES), jnp.int32),
            *(pltpu.VMEM(array.shape, array.dtype) for array in later),
        ),
        [HBM] * (6 + len(later)),
        scratch=[
            *[pltpu.VMEM(flat, jnp.float32)] * 3,
            *[pltpu.VMEM((1, columns), jnp.float32)] * 2,
            pltpu.SMEM((REG_DEV,), jnp.int32),
            pltpu.SemaphoreType.DMA((6 + len(later),)),
        ],
        name="turn",
    )(
        far(sample_surface_elevation.reshape(flat)),
        far(sample_zonal_current.reshape(flat)),
        far(sample_meridional_current.reshape(flat)),
        far(zonal_edge_layer_courant),
        far(meridional_edge_layer_courant),
        far(obs_count),
        *(far(array) for array in later),
    )
    from_west = passed_along(edge, "fine", 1)
    from_east = from_west if lax.axis_size("fine") == 2 else passed_along(edge, "fine", -1)
    ahead = []
    if small:
        padded = -(-states // LANES) * LANES
        obs = obs_value.shape[1]
        info, pull = call(
            observe_kernel,
            (near(REG_DEV, padded, padded), near(REG_DEV, padded, LANES)),
            [VMEM] * 5,
            cost=pl.CostEstimate(
                flops=12 * REG_DEV * padded * padded * obs, bytes_accessed=1 << 20, transcendentals=0
            ),
            name="observe",
        )(kept(live), *(kept(array) for array in seen))
        ahead = [kept(pull)]
    out = call(
        functools.partial(blocks_kernel, width),
        near(count, OUT_ROWS, LANES),
        [VMEM] * (4 + len(ahead)),
        name="blocks",
    )(kept(pair), kept(single), kept(from_west), kept(from_east), *ahead)
    got = kept(lax.all_to_all(out, owners, split_axis=0, concat_axis=0, tiled=True))
    back_shape = near(count * BACK_ROWS, LANES)
    layout = (groups, strips, width)
    if small:
        back = call(
            functools.partial(region_kernel, *layout),
            back_shape,
            [VMEM] * 3,
            scratch=[
                pltpu.VMEM((REG_DEV, padded, members), jnp.float32),
                pltpu.VMEM((REG_DEV, padded, members), jnp.float32),
            ],
            name="region",
        )(got, kept(info), kept(pull))
    else:
        x = call(
            functools.partial(forecast_kernel, *layout),
            f32(REG_DEV, states, members),
            [VMEM],
            name="forecast",
        )(got)
        analysis, increment = analyse_in_members(
            x, obs_index, obs_weight, obs_value, obs_var, obs_count
        )
        back = call(
            functools.partial(pack_kernel, *layout), back_shape, [VMEM] * 2, name="pack"
        )(analysis, increment)
    home = exchanged(back, owners, count)
    ana_h, ana_u, ana_v, fine_out = call(
        functools.partial(home_kernel, mem, strips, width),
        (f32(*flat), f32(*flat), f32(*flat), f32(*fine_ctrl.shape)),
        [VMEM, VMEM],
        name="home",
    )(kept(home), kept(ctrl))
    shape = (mem, rows, columns)
    return (ana_h.reshape(shape), ana_u.reshape(shape), ana_v.reshape(shape), fine_out)


def solution(mesh):
    strip = P("member", "region", "fine")
    owner = ("member", "region", "fine")
    fine = P(None, "region", "fine", "member")
    return jax.shard_map(
        shards,
        mesh=mesh,
        in_specs=(
            strip,
            strip,
            strip,
            P("region", "fine"),
            P("region", "fine"),
            P(owner, None, None),
            P(owner, None, None),
            P(owner, None),
            P(owner, None),
            P(owner),
            fine,
        ),
        out_specs=(strip, strip, strip, fine),
        check_vma=False,
    )
```

```python
import functools

import jax
import jax.numpy as jnp
from jax import lax
from jax.experimental import pallas as pl
from jax.experimental.pallas import tpu as pltpu
from jax.sharding import PartitionSpec as P

REG_DEV = 2
STEPS = 4
NEWTON = 8
LANES = 128
TILE = 8
HALF = LANES // 2
GRANT = 32 << 20


HIGHEST = lax.Precision.HIGHEST
NT = (((1,), (1,)), ((), ()))
NN = (((1,), (0,)), ((), ()))
VMEM = pl.BlockSpec(memory_space=pltpu.VMEM)
SMEM = pl.BlockSpec(memory_space=pltpu.SMEM)
HBM = pl.BlockSpec(memory_space=pltpu.HBM)


def passed_along(block, axis, distance):
    count = lax.axis_size(axis)
    route = [((i - distance) % count, i) for i in range(count)]
    return lax.ppermute(block, axis, route)


def lane_of(shape):
    return lax.broadcasted_iota(jnp.int32, shape, 1)


def row_of(shape):
    return lax.broadcasted_iota(jnp.int32, shape, 0)


def swapped(tile):
    return pltpu.roll(tile, HALF, 1)


def low_pair(even, odd):
    return jnp.where(lane_of(even.shape) < HALF, even, swapped(odd))


def high_pair(even, odd):
    return jnp.where(lane_of(even.shape) < HALF, swapped(even), odd)


def split(value):
    high = value.astype(jnp.bfloat16)
    return high, (value - high.astype(jnp.float32)).astype(jnp.bfloat16)


def beside(value):
    return jnp.concatenate(split(value), axis=1)


def stacked(value):
    both = jnp.concatenate(split(value), axis=1)
    return jnp.concatenate([both, both], axis=0)


def times(left, right):
    out = lax.dot_general(left, right, NN, preferred_element_type=jnp.float32)
    half = out.shape[1] // 2
    return out[:, :half] + out[:, half:]


def squared(value):
    both = jnp.concatenate(split(value), axis=0)
    out = lax.dot_general(both, both, NT, preferred_element_type=jnp.float32)
    half = out.shape[0] // 2
    out = out[:, :half] + out[:, half:]
    return out[:half] + out[half:]


BACK_ROWS = 3 * TILE + 1


def turn_kernel(mem, later, *refs):
    sources, refs = refs[: 6 + later], refs[6 + later :]
    pair_ref, single_ref, edge_ref, live_ref = refs[:4]
    targets, sems = refs[4 + later : -1] + refs[4 : 4 + later], refs[-1]
    copies = [
        pltpu.make_async_copy(source, target, sems.at[i])
        for i, (source, target) in enumerate(zip(sources, targets))
    ]
    for copy in copies:
        copy.start()
    h_ref, u_ref, v_ref, zonal_ref, merid_ref, count_ref = targets[:6]
    tiles = h_ref.shape[0] // mem
    columns = tiles * LANES
    zero = jnp.zeros((TILE, LANES), jnp.float32)
    for ref in (pair_ref, single_ref):
        ref[0:TILE, :] = zero
        ref[columns : columns + TILE, :] = zero
    for copy in copies[:5]:
        copy.wait()
    for t in range(tiles):
        rows = pl.ds(t, mem, stride=tiles)
        lanes = slice(t * LANES, (t + 1) * LANES)
        pair = jnp.concatenate([h_ref[rows, :], u_ref[rows, :]], axis=0)
        zonal = jnp.broadcast_to(zonal_ref[:, lanes], (mem // 2, LANES))
        merid = jnp.broadcast_to(merid_ref[:, lanes], (mem // 2, LANES))
        single = jnp.concatenate([v_ref[rows, :], zonal, merid], axis=0)
        place = slice(STEPS + t * LANES, STEPS + (t + 1) * LANES)
        pair_ref[place, :] = pair.T
        single_ref[place, :] = single.T
    early = row_of((TILE, LANES)) < STEPS
    for i, ref in enumerate((pair_ref, single_ref)):
        edge_ref[i] = jnp.where(early, ref[columns : columns + TILE, :], ref[0:TILE, :])
    for copy in copies[5:]:
        copy.wait()
    for q in range(REG_DEV):
        live_ref[q] = jnp.full(live_ref.shape[1:], count_ref[q], jnp.int32)


def blocks_kernel(groups, strips, width, pair_ref, single_ref, west_ref, east_ref, *refs):
    send_refs = refs[-strips:]
    me = lax.axis_index("region")
    shape = (TILE, LANES)
    early = row_of(shape) < STEPS
    part = lane_of(shape) % (HALF // 2)
    span = 3 * TILE
    for s, send_ref in enumerate(send_refs):
        owner = me ^ s
        first, last = early & (owner == 0), ~early & (owner == strips - 1)
        courant = jnp.zeros(shape, jnp.float32)
        for p in range(groups // 2):
            for j in range(3):
                pairs, singles = [], []
                for group in (2 * p, 2 * p + 1):
                    start = pl.multiple_of(width * (group * strips + owner) + TILE * j, TILE)
                    pair = pair_ref[pl.ds(start, TILE), :]
                    single = single_ref[pl.ds(start, TILE), :]
                    if group == 0 and j == 0:
                        pair = jnp.where(first, west_ref[0], pair)
                        single = jnp.where(first, west_ref[1], single)
                    if group == groups - 1 and j == 2:
                        pair = jnp.where(last, east_ref[0], pair)
                        single = jnp.where(last, east_ref[1], single)
                    pairs.append(pair)
                    singles.append(single)
                    courant = jnp.where(part == 3 * group + j, single, courant)
                place = 3 * span * p + TILE * j
                send_ref[place : place + TILE, :] = low_pair(*pairs)
                send_ref[place + span : place + span + TILE, :] = high_pair(*pairs)
                send_ref[place + 2 * span : place + 2 * span + TILE, :] = low_pair(*singles)
        place = 3 * span * (groups // 2)
        send_ref[place : place + TILE, :] = courant


def forecast_kernel(groups, strips, width, *refs):
    got_refs, refs = refs[:strips], refs[strips:]
    send_refs, (got_ref, turned_ref) = refs[:groups], refs[groups:]
    span = width + 2 * STEPS
    per_region = strips // REG_DEV
    cells = per_region * width
    me = lax.axis_index("region")
    for s, ref in enumerate(got_refs):
        got_ref[me ^ s] = ref[...]
    low = lane_of((TILE, LANES)) < HALF
    tail = 3 * span * (groups // 2)
    for p in range(groups // 2):

        def field(r, i):
            return got_ref[r, 3 * span * p + span * i : 3 * span * p + span * (i + 1), :]

        def courant(r, first):
            mixed = got_ref[r, tail : tail + TILE, :]
            parts = []
            for j in range(3):
                even, odd = first + 6 * p + j, first + 6 * p + 3 + j
                parts.append(
                    jnp.where(
                        low,
                        jnp.broadcast_to(mixed[:, even : even + 1], (TILE, LANES)),
                        jnp.broadcast_to(mixed[:, odd : odd + 1], (TILE, LANES)),
                    )
                )
            return jnp.concatenate(parts, axis=0)

        h = [field(r, 0) for r in range(strips)]
        u = [field(r, 1) for r in range(strips)]
        v = [field(r, 2) for r in range(strips)]
        zonal = [courant(r, HALF) for r in range(strips)]
        merid = [courant(r, HALF + HALF // 2) for r in range(strips)]
        for _ in range(STEPS):
            flux_v = [merid[r] * v[r] for r in range(strips)]
            for r in range(strips):
                flux_u = zonal[r] * u[r]
                south = flux_v[r - 1] if r else jnp.zeros_like(flux_u)
                h[r] = h[r] - (flux_u - pltpu.roll(flux_u, 1, 0) + flux_v[r] - south)
            for r in range(strips):
                north = h[r + 1] if r + 1 < strips else jnp.zeros_like(h[r])
                u[r] = u[r] - (pltpu.roll(h[r], span - 1, 0) - h[r])
                v[r] = v[r] - (north - h[r])
        for i, state in enumerate((h, u, v)):
            inner = [pltpu.roll(state[r], span - STEPS, 0)[:width] for r in range(strips)]
            for s in range(per_region):
                lower, upper = inner[s], inner[per_region + s]
                place = slice(i * cells + s * width, i * cells + (s + 1) * width)
                turned_ref[2 * p, place, :] = low_pair(lower, upper)
                turned_ref[2 * p + 1, place, :] = high_pair(lower, upper)
    mine = lax.axis_index("member")
    for s, ref in enumerate(send_refs):
        ref[...] = turned_ref[mine ^ s]


def collect(got_refs, all_ref, x_ref):
    states = all_ref.shape[1]
    mine = lax.axis_index("member")
    for s, ref in enumerate(got_refs):
        all_ref[mine ^ s] = ref[...]
    for p in range(len(got_refs) // 2):
        even, odd = all_ref[2 * p], all_ref[2 * p + 1]
        lanes = slice(p * LANES, (p + 1) * LANES)
        x_ref[0, :states, lanes] = low_pair(even, odd)
        x_ref[1, :states, lanes] = high_pair(even, odd)


def observe_kernel(live_ref, index_ref, weight_ref, value_ref, var_ref, info_ref, pull_ref):
    states = info_ref.shape[1]
    obs = index_ref.shape[2]
    for q in range(REG_DEV):
        state = row_of((states, obs))
        operator = jnp.zeros((states, obs), jnp.float32)
        for j in range(index_ref.shape[1]):
            hit = state == index_ref[q, j : j + 1, :]
            operator = operator + jnp.where(hit, weight_ref[q, j : j + 1, :], 0.0)
        live = lane_of((1, obs)) < live_ref[q, 0:1, 0:1]
        inverse = jnp.where(live, 1.0 / var_ref[q : q + 1, :], 0.0)
        scaled = operator * inverse
        info_ref[q] = lax.dot_general(
            scaled, operator, NT, precision=HIGHEST, preferred_element_type=jnp.float32
        )
        pulled = jnp.sum(scaled * value_ref[q : q + 1, :], axis=1, keepdims=True)
        pull_ref[q] = jnp.broadcast_to(pulled, (states, LANES))


def analyse(members, x_ref, info_ref, pull_ref, out_ref):
    states = x_ref.shape[1]
    square = (states, states)
    diagonal = row_of(square) == lane_of(square)
    identity = jnp.where(diagonal, 1.0, 0.0)
    regions = range(REG_DEV)
    scale = 1.0 / (members - 1)

    def as_row(column):
        return jnp.sum(jnp.where(diagonal, column, 0.0), axis=0, keepdims=True)

    def applied(matrix, row):
        return jnp.sum(matrix * row, axis=1, keepdims=True)

    x = [x_ref[q] for q in regions]
    means = [jnp.sum(x[q], axis=1, keepdims=True) / members for q in regions]
    spreads = [x[q] - means[q] for q in regions]
    covs = [squared(spreads[q]) for q in regions]
    gains = [times(beside(covs[q]), stacked(info_ref[q] * scale)) for q in regions]
    rights = [stacked(gains[q]) for q in regions]
    gains_2 = [times(beside(gains[q]), rights[q]) for q in regions]
    pulls, inverse_norms, firsts, iterates, inverses = [], [], [], [], []
    for q in regions:
        pulled = pull_ref[q][:, 0:1] - applied(info_ref[q], as_row(means[q]))
        pulls.append(jnp.sum(covs[q] * pulled, axis=0, keepdims=True))
        trace = jnp.sum(jnp.where(diagonal, gains_2[q] + 2.0 * gains[q], 0.0), keepdims=True)
        inverse_norms.append(lax.rsqrt(trace + members))
    for q in regions:
        norm = inverse_norms[q]
        first = (identity + gains[q]) * norm
        second = (identity + 2.0 * gains[q] + gains_2[q]) * (norm * norm)
        third = (second + times(beside(second), rights[q])) * norm
        inverses.append(1.5 * identity - 0.5 * first)
        iterates.append(2.25 * first - 1.5 * second + 0.25 * third)
    for sweep in range(1, NEWTON - 1):
        rights = [stacked(iterates[q]) for q in regions]
        lefts = [
            jnp.concatenate([beside(iterates[q]), beside(inverses[q])], axis=0) for q in regions
        ]
        both = [times(lefts[q], rights[q]) for q in regions]
        seconds = [both[q][:states] for q in regions]
        thirds = [times(beside(seconds[q]), rights[q]) for q in regions]
        inverses = [1.5 * inverses[q] - 0.5 * both[q][states:] for q in regions]
        iterates = [
            2.25 * iterates[q] - 1.5 * seconds[q] + 0.25 * thirds[q] for q in regions
        ]
    increments = []
    for q in regions:
        high, low = split(spreads[q])
        wide = beside(inverses[q])
        moved = lax.dot_general(
            wide, jnp.concatenate([high, high], axis=0), NN, preferred_element_type=jnp.float32
        )
        moved = moved + lax.dot_general(
            wide[:, :states], low, NN, preferred_element_type=jnp.float32
        )
        twice = applied(inverses[q], as_row(applied(inverses[q], pulls[q])))
        factor = 1.5 * identity - 0.5 * iterates[q]
        twice = applied(factor, as_row(applied(factor, as_row(twice))))
        increment = twice * (inverse_norms[q] * scale)
        increments.append(increment)
        high, low = split(moved * jnp.sqrt(inverse_norms[q]))
        wide = beside(factor)
        moved = lax.dot_general(
            wide, jnp.concatenate([high, high], axis=0), NN, preferred_element_type=jnp.float32
        )
        moved = moved + lax.dot_general(
            wide[:, :states], low, NN, preferred_element_type=jnp.float32
        )
        out_ref[q] = moved + (means[q] + increment)
    return increments


def pack(groups, strips, width, ana_ref, increments, send_ref):
    per_region = strips // REG_DEV
    cells = per_region * width
    states = increments[0].shape[0]
    state = row_of((states, LANES))
    lane = lane_of((states, LANES))
    for r in range(strips):
        q, s = divmod(r, per_region)
        wanted = (lane // width) * cells + s * width + lane % width
        hit = (state == wanted) & (lane < 3 * width)
        row = jnp.sum(jnp.where(hit, increments[q], 0.0), axis=0, keepdims=True)
        for group in range(groups):
            block = group * strips + r
            lanes = slice((group // 2) * LANES, (group // 2 + 1) * LANES)
            pair = high_pair if group % 2 else low_pair
            for i in range(3):
                first = i * cells + s * width
                tile = pair(
                    ana_ref[q, first : first + TILE, lanes],
                    ana_ref[q, first + TILE : first + 2 * TILE, lanes],
                )
                send_ref[BACK_ROWS * block + TILE * i : BACK_ROWS * block + TILE * (i + 1), :] = tile
            send_ref[BACK_ROWS * (block + 1) - 1 : BACK_ROWS * (block + 1), :] = row


def region_kernel(groups, strips, width, *refs):
    got_refs, (info_ref, pull_ref, send_ref, all_ref, x_ref, ana_ref) = refs[:groups], refs[groups:]
    states = all_ref.shape[1]
    if states < x_ref.shape[1]:
        x_ref[:, states:, :] = jnp.zeros_like(x_ref[:, states:, :])
    collect(got_refs, all_ref, x_ref)
    increments = analyse(x_ref.shape[2], x_ref, info_ref, pull_ref, ana_ref)
    pack(groups, strips, width, ana_ref, increments, send_ref)


def home_kernel(mem, strips, width, got_ref, ctrl_ref, h_ref, u_ref, v_ref, fine_ref):
    tiles = got_ref.shape[0] // BACK_ROWS * width // LANES
    per_tile = LANES // width
    for i, out_ref in enumerate((h_ref, u_ref, v_ref)):
        for t in range(0, tiles, 2):
            rows = []
            for k in range(per_tile):
                first = BACK_ROWS * (t * per_tile + k) + TILE * i
                even = got_ref[first : first + TILE, :]
                first += BACK_ROWS * per_tile
                odd = got_ref[first : first + TILE, :]
                rows += [low_pair(even, odd), high_pair(even, odd)]
            turned = jnp.concatenate(rows, axis=0).T
            out_ref[pl.ds(t, mem, stride=tiles), :] = turned[:mem]
            out_ref[pl.ds(t + 1, mem, stride=tiles), :] = turned[mem:]
    mine = lax.axis_index("member") * strips
    per_fine = LANES // (2 * width)
    row = row_of((width, LANES))
    lane = lane_of((width, LANES))
    for t in range(ctrl_ref.shape[3] // LANES):
        rows = [
            got_ref[pl.ds(BACK_ROWS * (mine + t * per_fine + b) + BACK_ROWS - 1, 1), :]
            for b in range(per_fine)
        ]
        columns = [jnp.broadcast_to(r, (LANES, LANES)).T[:, 0:1] for r in rows]
        for i in range(3):
            total = jnp.zeros((1, LANES), jnp.float32)
            for b in range(per_fine):
                hit = ((lane // 2) % width == row) & (lane // (2 * width) == b)
                part = jnp.where(hit, columns[b][i * width : (i + 1) * width], 0.0)
                total = total + jnp.sum(part, axis=0, keepdims=True)
            lanes = slice(t * LANES, (t + 1) * LANES)
            for e in range(2):
                fine_ref[i, e, :, lanes] = ctrl_ref[i, e, :, lanes] + total


def collect_kernel(groups, *refs):
    collect(refs[:groups], refs[-1], refs[-2])


def pack_kernel(groups, strips, width, ana_ref, inc_ref, send_ref):
    pack(groups, strips, width, ana_ref, [inc_ref[q] for q in range(REG_DEV)], send_ref)


def analyse_in_members(x, obs_index, obs_weight, obs_value, obs_var, obs_count):
    states, members = x.shape[1:]
    mean_state = jnp.mean(x, axis=2, keepdims=True)
    spread = x - mean_state
    picks = (obs_index[:, :, :, None] == jnp.arange(states)).astype(jnp.float32)
    operator = jnp.sum(picks * obs_weight[:, :, :, None], axis=2)
    predicted = jnp.einsum("ros,rsk->rko", operator, x, precision=HIGHEST)
    mean_obs = jnp.mean(predicted, axis=1, keepdims=True)
    obs_spread = predicted - mean_obs
    active_obs = jnp.arange(obs_value.shape[1])[None, :] < obs_count[:, None]
    weighted = obs_spread * (active_obs.astype(jnp.float32) / obs_var)[:, None, :]
    gram_sum = jnp.einsum("rko,rjo->rkj", weighted, obs_spread, precision=HIGHEST)
    identity = jnp.eye(members, dtype=jnp.float32)
    scaled = identity + gram_sum / (members - 1)
    frobenius = jnp.sqrt(jnp.sum(scaled * scaled, axis=(1, 2), keepdims=True))
    iterate = scaled / frobenius
    inverse_root = jnp.broadcast_to(identity, scaled.shape)
    dot = functools.partial(jnp.einsum, "rij,rjk->rik", precision=HIGHEST)
    for _ in range(NEWTON):
        factor = 1.5 * identity - 0.5 * dot(inverse_root, iterate)
        iterate = dot(iterate, factor)
        inverse_root = dot(factor, inverse_root)
    transform = inverse_root / jnp.sqrt(frobenius)
    innovation = jnp.einsum(
        "rko,ro->rk", weighted, obs_value - mean_obs[:, 0], precision=HIGHEST
    )
    halfway = jnp.einsum("rkj,rj->rk", transform, innovation, precision=HIGHEST)
    mean_weights = jnp.einsum("rkj,rj->rk", transform, halfway, precision=HIGHEST) / (members - 1)
    increment = jnp.einsum("rk,rsk->rs", mean_weights, spread, precision=HIGHEST)[:, :, None]
    moved = jnp.einsum("rjk,rsj->rsk", transform, spread, precision=HIGHEST)
    return mean_state + increment + moved, increment


def call(kernel, out_shape, specs, scratch=(), cost=None, name=None):
    many = isinstance(out_shape, tuple)
    return pl.pallas_call(
        kernel,
        out_shape=out_shape,
        in_specs=specs,
        out_specs=tuple(VMEM for _ in out_shape) if many else VMEM,
        scratch_shapes=scratch,
        cost_estimate=cost,
        compiler_params=pltpu.CompilerParams(vmem_limit_bytes=GRANT),
        name=name,
    )


def swapped_blocks(blocks, axis):
    count = len(blocks)
    if count <= 4:
        routes = [[(i, i ^ s) for i in range(count)] for s in range(count)]
        moved = [lax.ppermute(blocks[s], axis, routes[s]) for s in range(1, count)]
        return [kept(block) for block in [blocks[0], *moved]]
    order = lax.axis_index(axis) ^ jnp.arange(count)
    moved = lax.all_to_all(jnp.stack(blocks)[order], axis, split_axis=0, concat_axis=0, tiled=True)
    return [kept(block) for block in moved[order]]


def exchanged(blocks, axes, count):
    dense = blocks.reshape(count, -1, 1, LANES)
    return lax.all_to_all(dense, axes, split_axis=0, concat_axis=0, tiled=True).reshape(blocks.shape)


def f32(*shape):
    return jax.ShapeDtypeStruct(shape, jnp.float32)


def near(*shape):
    return pltpu.VMEM(shape, jnp.float32)


def far(array):
    return pltpu.with_memory_space_constraint(array, pltpu.HBM)


def kept(array):
    return pltpu.with_memory_space_constraint(array, pltpu.VMEM)


def shards(
    sample_surface_elevation,
    sample_zonal_current,
    sample_meridional_current,
    zonal_edge_layer_courant,
    meridional_edge_layer_courant,
    obs_index,
    obs_weight,
    obs_value,
    obs_var,
    obs_count,
    fine_ctrl,
):
    groups = lax.axis_size("member")
    strips = lax.axis_size("region")
    owners = ("member", "region")
    mem, rows, columns = sample_surface_elevation.shape
    count = groups * strips
    width = columns // count
    members = groups * mem
    assert rows == 1 and 2 * mem == LANES and width == 2 * TILE and STEPS * 2 == TILE
    assert columns % (2 * LANES) == 0 and strips % REG_DEV == 0 and REG_DEV == 2
    assert all(size > 1 and size & (size - 1) == 0 for size in (groups, strips))
    assert 3 * groups <= HALF // 2
    flat = (mem * columns // LANES, LANES)
    states = 3 * width * strips // REG_DEV
    small = states <= members
    later = [fine_ctrl]
    if small:
        later += [obs_index.transpose(0, 2, 1), obs_weight.transpose(0, 2, 1), obs_value, obs_var]
    pair, single, edge, live, ctrl, *seen = call(
        functools.partial(turn_kernel, mem, len(later)),
        (
            near(columns + TILE, LANES),
            near(columns + TILE, LANES),
            near(2, TILE, LANES),
            pltpu.VMEM((REG_DEV, TILE, LANES), jnp.int32),
            *(pltpu.VMEM(array.shape, array.dtype) for array in later),
        ),
        [HBM] * (6 + len(later)),
        scratch=[
            *[pltpu.VMEM(flat, jnp.float32)] * 3,
            *[pltpu.VMEM((1, columns), jnp.float32)] * 2,
            pltpu.SMEM((REG_DEV,), jnp.int32),
            pltpu.SemaphoreType.DMA((6 + len(later),)),
        ],
        name="turn",
    )(
        far(sample_surface_elevation.reshape(flat)),
        far(sample_zonal_current.reshape(flat)),
        far(sample_meridional_current.reshape(flat)),
        far(zonal_edge_layer_courant),
        far(meridional_edge_layer_courant),
        far(obs_count),
        *(far(array) for array in later),
    )
    from_west = passed_along(edge, "fine", 1)
    from_east = from_west if lax.axis_size("fine") == 2 else passed_along(edge, "fine", -1)
    ahead = []
    if small:
        padded = -(-states // LANES) * LANES
        obs = obs_value.shape[1]
        info, pull = call(
            observe_kernel,
            (near(REG_DEV, padded, padded), near(REG_DEV, padded, LANES)),
            [VMEM] * 5,
            cost=pl.CostEstimate(
                flops=12 * REG_DEV * padded * padded * obs, bytes_accessed=1 << 20, transcendentals=0
            ),
            name="observe",
        )(kept(live), *(kept(array) for array in seen))
        ahead = [kept(pull)]
    layout = (groups, strips, width)
    span = width + 2 * STEPS
    out = call(
        functools.partial(blocks_kernel, *layout),
        tuple([near(3 * span * (groups // 2) + TILE, LANES)] * strips),
        [VMEM] * (4 + len(ahead)),
        name="blocks",
    )(kept(pair), kept(single), kept(from_west), kept(from_east), *ahead)
    got = swapped_blocks(out, "region")
    turned = call(
        functools.partial(forecast_kernel, *layout),
        tuple([near(states, LANES)] * groups),
        [VMEM] * strips,
        scratch=[
            pltpu.VMEM((strips, *out[0].shape), jnp.float32),
            pltpu.VMEM((groups, states, LANES), jnp.float32),
        ],
        name="forecast",
    )(*got)
    got = swapped_blocks(turned, "member")
    back_shape = near(count * BACK_ROWS, LANES)
    gathered = pltpu.VMEM((groups, states, LANES), jnp.float32)
    if small:
        back = call(
            functools.partial(region_kernel, *layout),
            back_shape,
            [VMEM] * (groups + 2),
            scratch=[
                gathered,
                pltpu.VMEM((REG_DEV, padded, members), jnp.float32),
                pltpu.VMEM((REG_DEV, padded, members), jnp.float32),
            ],
            name="region",
        )(*got, kept(info), kept(pull))
    else:
        x = call(
            functools.partial(collect_kernel, groups),
            f32(REG_DEV, states, members),
            [VMEM] * groups,
            scratch=[gathered],
            name="collect",
        )(*got)
        analysis, increment = analyse_in_members(
            x, obs_index, obs_weight, obs_value, obs_var, obs_count
        )
        back = call(
            functools.partial(pack_kernel, *layout), back_shape, [VMEM] * 2, name="pack"
        )(analysis, increment)
    home = exchanged(back, owners, count)
    ana_h, ana_u, ana_v, fine_out = call(
        functools.partial(home_kernel, mem, strips, width),
        (f32(*flat), f32(*flat), f32(*flat), f32(*fine_ctrl.shape)),
        [VMEM, VMEM],
        name="home",
    )(kept(home), kept(ctrl))
    shape = (mem, rows, columns)
    return (ana_h.reshape(shape), ana_u.reshape(shape), ana_v.reshape(shape), fine_out)


def solution(mesh):
    strip = P("member", "region", "fine")
    owner = ("member", "region", "fine")
    fine = P(None, "region", "fine", "member")
    return jax.shard_map(
        shards,
        mesh=mesh,
        in_specs=(
            strip,
            strip,
            strip,
            P("region", "fine"),
            P("region", "fine"),
            P(owner, None, None),
            P(owner, None, None),
            P(owner, None),
            P(owner, None),
            P(owner),
            fine,
        ),
        out_specs=(strip, strip, strip, fine),
        check_vma=False,
    )
```

```python
import functools

import jax
import jax.numpy as jnp
from jax import lax
from jax.experimental import pallas as pl
from jax.experimental.pallas import tpu as pltpu
from jax.sharding import PartitionSpec as P

REG_DEV = 2
STEPS = 4
NEWTON = 8
LANES = 128
TILE = 8
HALF = LANES // 2
GRANT = 32 << 20


HIGHEST = lax.Precision.HIGHEST
NT = (((1,), (1,)), ((), ()))
NN = (((1,), (0,)), ((), ()))
VMEM = pl.BlockSpec(memory_space=pltpu.VMEM)
SMEM = pl.BlockSpec(memory_space=pltpu.SMEM)
HBM = pl.BlockSpec(memory_space=pltpu.HBM)


def passed_along(block, axis, distance):
    count = lax.axis_size(axis)
    route = [((i - distance) % count, i) for i in range(count)]
    return lax.ppermute(block, axis, route)


def lane_of(shape):
    return lax.broadcasted_iota(jnp.int32, shape, 1)


def row_of(shape):
    return lax.broadcasted_iota(jnp.int32, shape, 0)


def swapped(tile):
    return pltpu.roll(tile, HALF, 1)


def low_pair(even, odd):
    return jnp.where(lane_of(even.shape) < HALF, even, swapped(odd))


def high_pair(even, odd):
    return jnp.where(lane_of(even.shape) < HALF, swapped(even), odd)


def split(value):
    high = value.astype(jnp.bfloat16)
    return high, (value - high.astype(jnp.float32)).astype(jnp.bfloat16)


def beside(value):
    return jnp.concatenate(split(value), axis=1)


def stacked(value):
    both = jnp.concatenate(split(value), axis=1)
    return jnp.concatenate([both, both], axis=0)


def times(left, right):
    out = lax.dot_general(left, right, NN, preferred_element_type=jnp.float32)
    half = out.shape[1] // 2
    return out[:, :half] + out[:, half:]


def squared(value):
    both = jnp.concatenate(split(value), axis=0)
    out = lax.dot_general(both, both, NT, preferred_element_type=jnp.float32)
    half = out.shape[0] // 2
    out = out[:, :half] + out[:, half:]
    return out[:half] + out[half:]


BACK_ROWS = 3 * TILE + 1


def send_kernel(groups, strips, width, mem, later, *refs):
    sources, refs = refs[: 6 + later], refs[6 + later :]
    send_refs, refs = refs[:strips], refs[strips:]
    edge_ref, live_ref = refs[:2]
    targets, (pair_ref, single_ref, sems) = refs[2 + later : -3] + refs[2 : 2 + later], refs[-3:]
    copies = [
        pltpu.make_async_copy(source, target, sems.at[i])
        for i, (source, target) in enumerate(zip(sources, targets))
    ]
    for copy in copies:
        copy.start()
    h_ref, u_ref, v_ref, zonal_ref, merid_ref, count_ref = targets[:6]
    tiles = h_ref.shape[0] // mem
    columns = tiles * LANES
    shape = (TILE, LANES)
    zero = jnp.zeros(shape, jnp.float32)
    for ref in (pair_ref, single_ref):
        ref[0:TILE, :] = zero
        ref[columns : columns + TILE, :] = zero
    for copy in copies[:5]:
        copy.wait()
    for t in range(tiles):
        rows = pl.ds(t, mem, stride=tiles)
        lanes = slice(t * LANES, (t + 1) * LANES)
        pair = jnp.concatenate([h_ref[rows, :], u_ref[rows, :]], axis=0)
        zonal = jnp.broadcast_to(zonal_ref[:, lanes], (mem // 2, LANES))
        merid = jnp.broadcast_to(merid_ref[:, lanes], (mem // 2, LANES))
        single = jnp.concatenate([v_ref[rows, :], zonal, merid], axis=0)
        place = slice(STEPS + t * LANES, STEPS + (t + 1) * LANES)
        pair_ref[place, :] = pair.T
        single_ref[place, :] = single.T
    early = row_of(shape) < STEPS
    for i, ref in enumerate((pair_ref, single_ref)):
        edge_ref[i] = jnp.where(early, ref[columns : columns + TILE, :], ref[0:TILE, :])
    me = lax.axis_index("region")
    part = lane_of(shape) % (HALF // 2)
    span = 3 * TILE
    for s, send_ref in enumerate(send_refs):
        owner = me ^ s
        courant = zero
        for p in range(groups // 2):
            for j in range(3):
                pairs, singles = [], []
                for group in (2 * p, 2 * p + 1):
                    start = pl.multiple_of(width * (group * strips + owner) + TILE * j, TILE)
                    pairs.append(pair_ref[pl.ds(start, TILE), :])
                    singles.append(single_ref[pl.ds(start, TILE), :])
                    courant = jnp.where(part == 3 * group + j, singles[-1], courant)
                place = 3 * span * p + TILE * j
                send_ref[place : place + TILE, :] = low_pair(*pairs)
                send_ref[place + span : place + span + TILE, :] = high_pair(*pairs)
                send_ref[place + 2 * span : place + 2 * span + TILE, :] = low_pair(*singles)
        place = 3 * span * (groups // 2)
        send_ref[place : place + TILE, :] = courant
    for copy in copies[5:]:
        copy.wait()
    for q in range(REG_DEV):
        live_ref[q] = jnp.full(live_ref.shape[1:], count_ref[q], jnp.int32)


def forecast_kernel(groups, strips, width, *refs):
    got_refs, west_refs = refs[:strips], refs[strips : 2 * strips]
    east_refs, refs = refs[2 * strips : 3 * strips], refs[3 * strips :]
    send_refs, (got_ref, west_ref, east_ref, turned_ref) = refs[:groups], refs[groups:]
    span = width + 2 * STEPS
    per_region = strips // REG_DEV
    cells = per_region * width
    me = lax.axis_index("region")
    for arrived, ref in ((got_refs, got_ref), (west_refs, west_ref), (east_refs, east_ref)):
        for s in range(strips):
            ref[me ^ s] = arrived[s][...]
    shape = (TILE, LANES)
    low = lane_of(shape) < HALF
    early = row_of(shape) < STEPS
    first = early & low & (me == 0)
    last = ~early & ~low & (me == strips - 1)

    def patched(p, parts, west, east):
        if p == 0:
            parts[0] = jnp.where(first, west, parts[0])
        if p == groups // 2 - 1:
            parts[2] = jnp.where(last, east, parts[2])
        return jnp.concatenate(parts, axis=0)

    tail = 3 * span * (groups // 2)
    for p in range(groups // 2):

        def field(r, i):
            place = 3 * span * p + span * i
            parts = [got_ref[r, place + TILE * j : place + TILE * (j + 1), :] for j in range(3)]
            west, east = west_ref[r, i // 2], east_ref[r, i // 2]
            if i == 1:
                return patched(p, parts, swapped(west), east)
            return patched(p, parts, west, swapped(east))

        def courant(r, place):
            mixed = got_ref[r, tail : tail + TILE, :]

            def lane(tile, at):
                return jnp.broadcast_to(tile[:, at : at + 1], shape)

            parts = []
            for j in range(3):
                even = place + 6 * p + j
                parts.append(jnp.where(low, lane(mixed, even), lane(mixed, even + 3)))
            return patched(p, parts, lane(west_ref[r, 1], place), lane(east_ref[r, 1], place))

        h = [field(r, 0) for r in range(strips)]
        u = [field(r, 1) for r in range(strips)]
        v = [field(r, 2) for r in range(strips)]
        zonal = [courant(r, HALF) for r in range(strips)]
        merid = [courant(r, HALF + HALF // 2) for r in range(strips)]
        for _ in range(STEPS):
            flux_v = [merid[r] * v[r] for r in range(strips)]
            for r in range(strips):
                flux_u = zonal[r] * u[r]
                south = flux_v[r - 1] if r else jnp.zeros_like(flux_u)
                h[r] = h[r] - (flux_u - pltpu.roll(flux_u, 1, 0) + flux_v[r] - south)
            for r in range(strips):
                north = h[r + 1] if r + 1 < strips else jnp.zeros_like(h[r])
                u[r] = u[r] - (pltpu.roll(h[r], span - 1, 0) - h[r])
                v[r] = v[r] - (north - h[r])
        for i, state in enumerate((h, u, v)):
            inner = [pltpu.roll(state[r], span - STEPS, 0)[:width] for r in range(strips)]
            for s in range(per_region):
                lower, upper = inner[s], inner[per_region + s]
                place = slice(i * cells + s * width, i * cells + (s + 1) * width)
                turned_ref[2 * p, place, :] = low_pair(lower, upper)
                turned_ref[2 * p + 1, place, :] = high_pair(lower, upper)
    mine = lax.axis_index("member")
    for s, ref in enumerate(send_refs):
        ref[...] = turned_ref[mine ^ s]


def collect(got_refs, all_ref, x_ref):
    states = all_ref.shape[1]
    mine = lax.axis_index("member")
    for s, ref in enumerate(got_refs):
        all_ref[mine ^ s] = ref[...]
    for p in range(len(got_refs) // 2):
        even, odd = all_ref[2 * p], all_ref[2 * p + 1]
        lanes = slice(p * LANES, (p + 1) * LANES)
        x_ref[0, :states, lanes] = low_pair(even, odd)
        x_ref[1, :states, lanes] = high_pair(even, odd)


def observe_kernel(live_ref, index_ref, weight_ref, value_ref, var_ref, info_ref, pull_ref):
    states = info_ref.shape[1]
    obs = index_ref.shape[2]
    for q in range(REG_DEV):
        state = row_of((states, obs))
        operator = jnp.zeros((states, obs), jnp.float32)
        for j in range(index_ref.shape[1]):
            hit = state == index_ref[q, j : j + 1, :]
            operator = operator + jnp.where(hit, weight_ref[q, j : j + 1, :], 0.0)
        live = lane_of((1, obs)) < live_ref[q, 0:1, 0:1]
        inverse = jnp.where(live, 1.0 / var_ref[q : q + 1, :], 0.0)
        scaled = operator * inverse
        info_ref[q] = lax.dot_general(
            scaled, operator, NT, precision=HIGHEST, preferred_element_type=jnp.float32
        )
        pulled = jnp.sum(scaled * value_ref[q : q + 1, :], axis=1, keepdims=True)
        pull_ref[q] = jnp.broadcast_to(pulled, (states, LANES))


def analyse(members, x_ref, info_ref, pull_ref, out_ref):
    states = x_ref.shape[1]
    square = (states, states)
    diagonal = row_of(square) == lane_of(square)
    identity = jnp.where(diagonal, 1.0, 0.0)
    regions = range(REG_DEV)
    scale = 1.0 / (members - 1)

    def as_row(column):
        return jnp.sum(jnp.where(diagonal, column, 0.0), axis=0, keepdims=True)

    def applied(matrix, row):
        return jnp.sum(matrix * row, axis=1, keepdims=True)

    x = [x_ref[q] for q in regions]
    means = [jnp.sum(x[q], axis=1, keepdims=True) / members for q in regions]
    spreads = [x[q] - means[q] for q in regions]
    covs = [squared(spreads[q]) for q in regions]
    gains = [times(beside(covs[q]), stacked(info_ref[q] * scale)) for q in regions]
    rights = [stacked(gains[q]) for q in regions]
    gains_2 = [times(beside(gains[q]), rights[q]) for q in regions]
    pulls, inverse_norms, firsts, iterates, inverses = [], [], [], [], []
    for q in regions:
        pulled = pull_ref[q][:, 0:1] - applied(info_ref[q], as_row(means[q]))
        pulls.append(jnp.sum(covs[q] * pulled, axis=0, keepdims=True))
        trace = jnp.sum(jnp.where(diagonal, gains_2[q] + 2.0 * gains[q], 0.0), keepdims=True)
        inverse_norms.append(lax.rsqrt(trace + members))
    for q in regions:
        norm = inverse_norms[q]
        first = (identity + gains[q]) * norm
        second = (identity + 2.0 * gains[q] + gains_2[q]) * (norm * norm)
        third = (second + times(beside(second), rights[q])) * norm
        inverses.append(1.5 * identity - 0.5 * first)
        iterates.append(2.25 * first - 1.5 * second + 0.25 * third)
    for sweep in range(1, NEWTON - 1):
        rights = [stacked(iterates[q]) for q in regions]
        lefts = [
            jnp.concatenate([beside(iterates[q]), beside(inverses[q])], axis=0) for q in regions
        ]
        both = [times(lefts[q], rights[q]) for q in regions]
        seconds = [both[q][:states] for q in regions]
        thirds = [times(beside(seconds[q]), rights[q]) for q in regions]
        inverses = [1.5 * inverses[q] - 0.5 * both[q][states:] for q in regions]
        iterates = [
            2.25 * iterates[q] - 1.5 * seconds[q] + 0.25 * thirds[q] for q in regions
        ]
    increments = []
    for q in regions:
        high, low = split(spreads[q])
        wide = beside(inverses[q])
        moved = lax.dot_general(
            wide, jnp.concatenate([high, high], axis=0), NN, preferred_element_type=jnp.float32
        )
        moved = moved + lax.dot_general(
            wide[:, :states], low, NN, preferred_element_type=jnp.float32
        )
        twice = applied(inverses[q], as_row(applied(inverses[q], pulls[q])))
        factor = 1.5 * identity - 0.5 * iterates[q]
        twice = applied(factor, as_row(applied(factor, as_row(twice))))
        increment = twice * (inverse_norms[q] * scale)
        increments.append(increment)
        high, low = split(moved * jnp.sqrt(inverse_norms[q]))
        wide = beside(factor)
        moved = lax.dot_general(
            wide, jnp.concatenate([high, high], axis=0), NN, preferred_element_type=jnp.float32
        )
        moved = moved + lax.dot_general(
            wide[:, :states], low, NN, preferred_element_type=jnp.float32
        )
        out_ref[q] = moved + (means[q] + increment)
    return increments


def pack(groups, strips, width, ana_ref, increments, send_ref):
    per_region = strips // REG_DEV
    cells = per_region * width
    states = increments[0].shape[0]
    state = row_of((states, LANES))
    lane = lane_of((states, LANES))
    for r in range(strips):
        q, s = divmod(r, per_region)
        wanted = (lane // width) * cells + s * width + lane % width
        hit = (state == wanted) & (lane < 3 * width)
        row = jnp.sum(jnp.where(hit, increments[q], 0.0), axis=0, keepdims=True)
        for group in range(groups):
            block = group * strips + r
            lanes = slice((group // 2) * LANES, (group // 2 + 1) * LANES)
            pair = high_pair if group % 2 else low_pair
            for i in range(3):
                first = i * cells + s * width
                tile = pair(
                    ana_ref[q, first : first + TILE, lanes],
                    ana_ref[q, first + TILE : first + 2 * TILE, lanes],
                )
                send_ref[BACK_ROWS * block + TILE * i : BACK_ROWS * block + TILE * (i + 1), :] = tile
            send_ref[BACK_ROWS * (block + 1) - 1 : BACK_ROWS * (block + 1), :] = row


def region_kernel(groups, strips, width, *refs):
    got_refs, (info_ref, pull_ref, send_ref, all_ref, x_ref, ana_ref) = refs[:groups], refs[groups:]
    states = all_ref.shape[1]
    if states < x_ref.shape[1]:
        x_ref[:, states:, :] = jnp.zeros_like(x_ref[:, states:, :])
    collect(got_refs, all_ref, x_ref)
    increments = analyse(x_ref.shape[2], x_ref, info_ref, pull_ref, ana_ref)
    pack(groups, strips, width, ana_ref, increments, send_ref)


def home_kernel(mem, strips, width, got_ref, ctrl_ref, h_ref, u_ref, v_ref, fine_ref):
    tiles = got_ref.shape[0] // BACK_ROWS * width // LANES
    per_tile = LANES // width
    for i, out_ref in enumerate((h_ref, u_ref, v_ref)):
        for t in range(0, tiles, 2):
            rows = []
            for k in range(per_tile):
                first = BACK_ROWS * (t * per_tile + k) + TILE * i
                even = got_ref[first : first + TILE, :]
                first += BACK_ROWS * per_tile
                odd = got_ref[first : first + TILE, :]
                rows += [low_pair(even, odd), high_pair(even, odd)]
            turned = jnp.concatenate(rows, axis=0).T
            out_ref[pl.ds(t, mem, stride=tiles), :] = turned[:mem]
            out_ref[pl.ds(t + 1, mem, stride=tiles), :] = turned[mem:]
    mine = lax.axis_index("member") * strips
    per_fine = LANES // (2 * width)
    row = row_of((width, LANES))
    lane = lane_of((width, LANES))
    for t in range(ctrl_ref.shape[3] // LANES):
        rows = [
            got_ref[pl.ds(BACK_ROWS * (mine + t * per_fine + b) + BACK_ROWS - 1, 1), :]
            for b in range(per_fine)
        ]
        columns = [jnp.broadcast_to(r, (LANES, LANES)).T[:, 0:1] for r in rows]
        for i in range(3):
            total = jnp.zeros((1, LANES), jnp.float32)
            for b in range(per_fine):
                hit = ((lane // 2) % width == row) & (lane // (2 * width) == b)
                part = jnp.where(hit, columns[b][i * width : (i + 1) * width], 0.0)
                total = total + jnp.sum(part, axis=0, keepdims=True)
            lanes = slice(t * LANES, (t + 1) * LANES)
            for e in range(2):
                fine_ref[i, e, :, lanes] = ctrl_ref[i, e, :, lanes] + total


def collect_kernel(groups, *refs):
    collect(refs[:groups], refs[-1], refs[-2])


def pack_kernel(groups, strips, width, ana_ref, inc_ref, send_ref):
    pack(groups, strips, width, ana_ref, [inc_ref[q] for q in range(REG_DEV)], send_ref)


def analyse_in_members(x, obs_index, obs_weight, obs_value, obs_var, obs_count):
    states, members = x.shape[1:]
    mean_state = jnp.mean(x, axis=2, keepdims=True)
    spread = x - mean_state
    picks = (obs_index[:, :, :, None] == jnp.arange(states)).astype(jnp.float32)
    operator = jnp.sum(picks * obs_weight[:, :, :, None], axis=2)
    predicted = jnp.einsum("ros,rsk->rko", operator, x, precision=HIGHEST)
    mean_obs = jnp.mean(predicted, axis=1, keepdims=True)
    obs_spread = predicted - mean_obs
    active_obs = jnp.arange(obs_value.shape[1])[None, :] < obs_count[:, None]
    weighted = obs_spread * (active_obs.astype(jnp.float32) / obs_var)[:, None, :]
    gram_sum = jnp.einsum("rko,rjo->rkj", weighted, obs_spread, precision=HIGHEST)
    identity = jnp.eye(members, dtype=jnp.float32)
    scaled = identity + gram_sum / (members - 1)
    frobenius = jnp.sqrt(jnp.sum(scaled * scaled, axis=(1, 2), keepdims=True))
    iterate = scaled / frobenius
    inverse_root = jnp.broadcast_to(identity, scaled.shape)
    dot = functools.partial(jnp.einsum, "rij,rjk->rik", precision=HIGHEST)
    for _ in range(NEWTON):
        factor = 1.5 * identity - 0.5 * dot(inverse_root, iterate)
        iterate = dot(iterate, factor)
        inverse_root = dot(factor, inverse_root)
    transform = inverse_root / jnp.sqrt(frobenius)
    innovation = jnp.einsum(
        "rko,ro->rk", weighted, obs_value - mean_obs[:, 0], precision=HIGHEST
    )
    halfway = jnp.einsum("rkj,rj->rk", transform, innovation, precision=HIGHEST)
    mean_weights = jnp.einsum("rkj,rj->rk", transform, halfway, precision=HIGHEST) / (members - 1)
    increment = jnp.einsum("rk,rsk->rs", mean_weights, spread, precision=HIGHEST)[:, :, None]
    moved = jnp.einsum("rjk,rsj->rsk", transform, spread, precision=HIGHEST)
    return mean_state + increment + moved, increment


def call(kernel, out_shape, specs, scratch=(), cost=None, name=None):
    many = isinstance(out_shape, tuple)
    return pl.pallas_call(
        kernel,
        out_shape=out_shape,
        in_specs=specs,
        out_specs=tuple(VMEM for _ in out_shape) if many else VMEM,
        scratch_shapes=scratch,
        cost_estimate=cost,
        compiler_params=pltpu.CompilerParams(vmem_limit_bytes=GRANT),
        name=name,
    )


def swapped_blocks(blocks, axis):
    count = len(blocks)
    if count <= 4:
        routes = [[(i, i ^ s) for i in range(count)] for s in range(count)]
        moved = [lax.ppermute(blocks[s], axis, routes[s]) for s in range(1, count)]
        return [kept(block) for block in [blocks[0], *moved]]
    order = lax.axis_index(axis) ^ jnp.arange(count)
    moved = lax.all_to_all(jnp.stack(blocks)[order], axis, split_axis=0, concat_axis=0, tiled=True)
    return [kept(block) for block in moved[order]]


def exchanged(blocks, axes, count):
    dense = blocks.reshape(count, -1, 1, LANES)
    return lax.all_to_all(dense, axes, split_axis=0, concat_axis=0, tiled=True).reshape(blocks.shape)


def f32(*shape):
    return jax.ShapeDtypeStruct(shape, jnp.float32)


def near(*shape):
    return pltpu.VMEM(shape, jnp.float32)


def far(array):
    return pltpu.with_memory_space_constraint(array, pltpu.HBM)


def kept(array):
    return pltpu.with_memory_space_constraint(array, pltpu.VMEM)


def shards(
    sample_surface_elevation,
    sample_zonal_current,
    sample_meridional_current,
    zonal_edge_layer_courant,
    meridional_edge_layer_courant,
    obs_index,
    obs_weight,
    obs_value,
    obs_var,
    obs_count,
    fine_ctrl,
):
    groups = lax.axis_size("member")
    strips = lax.axis_size("region")
    owners = ("member", "region")
    mem, rows, columns = sample_surface_elevation.shape
    count = groups * strips
    width = columns // count
    members = groups * mem
    assert rows == 1 and 2 * mem == LANES and width == 2 * TILE and STEPS * 2 == TILE
    assert columns % (2 * LANES) == 0 and strips % REG_DEV == 0 and REG_DEV == 2
    assert all(size > 1 and size & (size - 1) == 0 for size in (groups, strips))
    assert 3 * groups <= HALF // 2
    flat = (mem * columns // LANES, LANES)
    states = 3 * width * strips // REG_DEV
    small = states <= members
    later = [fine_ctrl]
    if small:
        later += [obs_index.transpose(0, 2, 1), obs_weight.transpose(0, 2, 1), obs_value, obs_var]
    layout = (groups, strips, width)
    span = width + 2 * STEPS
    block = (3 * span * (groups // 2) + TILE, LANES)
    sent = call(
        functools.partial(send_kernel, *layout, mem, len(later)),
        (
            *[near(*block)] * strips,
            near(2, TILE, LANES),
            pltpu.VMEM((REG_DEV, TILE, LANES), jnp.int32),
            *(pltpu.VMEM(array.shape, array.dtype) for array in later),
        ),
        [HBM] * (6 + len(later)),
        scratch=[
            *[pltpu.VMEM(flat, jnp.float32)] * 3,
            *[pltpu.VMEM((1, columns), jnp.float32)] * 2,
            pltpu.SMEM((REG_DEV,), jnp.int32),
            *[pltpu.VMEM((columns + TILE, LANES), jnp.float32)] * 2,
            pltpu.SemaphoreType.DMA((6 + len(later),)),
        ],
        name="send",
    )(
        far(sample_surface_elevation.reshape(flat)),
        far(sample_zonal_current.reshape(flat)),
        far(sample_meridional_current.reshape(flat)),
        far(zonal_edge_layer_courant),
        far(meridional_edge_layer_courant),
        far(obs_count),
        *(far(array) for array in later),
    )
    out, (edge, live, ctrl, *seen) = sent[:strips], sent[strips:]
    west = passed_along(edge, "fine", 1)
    got = swapped_blocks(out, "region")
    wests = swapped_blocks([west] * strips, "region")
    easts = wests
    if lax.axis_size("fine") > 2:
        easts = swapped_blocks([passed_along(edge, "fine", -1)] * strips, "region")
    if small:
        padded = -(-states // LANES) * LANES
        obs = obs_value.shape[1]
        info, pull = call(
            observe_kernel,
            (near(REG_DEV, padded, padded), near(REG_DEV, padded, LANES)),
            [VMEM] * 5,
            cost=pl.CostEstimate(
                flops=12 * REG_DEV * padded * padded * obs, bytes_accessed=1 << 20, transcendentals=0
            ),
            name="observe",
        )(kept(live), *(kept(array) for array in seen))
    turned = call(
        functools.partial(forecast_kernel, *layout),
        tuple([near(states, LANES)] * groups),
        [VMEM] * (3 * strips),
        scratch=[
            pltpu.VMEM((strips, *block), jnp.float32),
            *[pltpu.VMEM((strips, 2, TILE, LANES), jnp.float32)] * 2,
            pltpu.VMEM((groups, states, LANES), jnp.float32),
        ],
        name="forecast",
    )(*got, *wests, *easts)
    got = swapped_blocks(turned, "member")
    back_shape = near(count * BACK_ROWS, LANES)
    gathered = pltpu.VMEM((groups, states, LANES), jnp.float32)
    if small:
        back = call(
            functools.partial(region_kernel, *layout),
            back_shape,
            [VMEM] * (groups + 2),
            scratch=[
                gathered,
                pltpu.VMEM((REG_DEV, padded, members), jnp.float32),
                pltpu.VMEM((REG_DEV, padded, members), jnp.float32),
            ],
            name="region",
        )(*got, kept(info), kept(pull))
    else:
        x = call(
            functools.partial(collect_kernel, groups),
            f32(REG_DEV, states, members),
            [VMEM] * groups,
            scratch=[gathered],
            name="collect",
        )(*got)
        analysis, increment = analyse_in_members(
            x, obs_index, obs_weight, obs_value, obs_var, obs_count
        )
        back = call(
            functools.partial(pack_kernel, *layout), back_shape, [VMEM] * 2, name="pack"
        )(analysis, increment)
    home = exchanged(back, owners, count)
    ana_h, ana_u, ana_v, fine_out = call(
        functools.partial(home_kernel, mem, strips, width),
        (f32(*flat), f32(*flat), f32(*flat), f32(*fine_ctrl.shape)),
        [VMEM, VMEM],
        name="home",
    )(kept(home), kept(ctrl))
    shape = (mem, rows, columns)
    return (ana_h.reshape(shape), ana_u.reshape(shape), ana_v.reshape(shape), fine_out)


def solution(mesh):
    strip = P("member", "region", "fine")
    owner = ("member", "region", "fine")
    fine = P(None, "region", "fine", "member")
    return jax.shard_map(
        shards,
        mesh=mesh,
        in_specs=(
            strip,
            strip,
            strip,
            P("region", "fine"),
            P("region", "fine"),
            P(owner, None, None),
            P(owner, None, None),
            P(owner, None),
            P(owner, None),
            P(owner),
            fine,
        ),
        out_specs=(strip, strip, strip, fine),
        check_vma=False,
    )
```

```python
import functools

import jax
import jax.numpy as jnp
from jax import lax
from jax.experimental import pallas as pl
from jax.experimental.pallas import tpu as pltpu
from jax.sharding import PartitionSpec as P


REG_DEV = 2
STEPS = 4
NEWTON = 8
LANES = 128
TILE = 8
HALF = LANES // 2
GRANT = 32 << 20


HIGHEST = lax.Precision.HIGHEST
NT = (((1,), (1,)), ((), ()))
NN = (((1,), (0,)), ((), ()))
VMEM = pl.BlockSpec(memory_space=pltpu.VMEM)
SMEM = pl.BlockSpec(memory_space=pltpu.SMEM)
HBM = pl.BlockSpec(memory_space=pltpu.HBM)


def passed_along(block, axis, distance):
    count = lax.axis_size(axis)
    route = [((i - distance) % count, i) for i in range(count)]
    return lax.ppermute(block, axis, route)


def lane_of(shape):
    return lax.broadcasted_iota(jnp.int32, shape, 1)


def row_of(shape):
    return lax.broadcasted_iota(jnp.int32, shape, 0)


def swapped(tile):
    return pltpu.roll(tile, HALF, 1)


def low_pair(even, odd):
    return jnp.where(lane_of(even.shape) < HALF, even, swapped(odd))


def high_pair(even, odd):
    return jnp.where(lane_of(even.shape) < HALF, swapped(even), odd)


def split(value):
    high = value.astype(jnp.bfloat16)
    return high, (value - high.astype(jnp.float32)).astype(jnp.bfloat16)


def beside(value):
    return jnp.concatenate(split(value), axis=1)


def stacked(value):
    both = jnp.concatenate(split(value), axis=1)
    return jnp.concatenate([both, both], axis=0)


def times(left, right):
    out = lax.dot_general(left, right, NN, preferred_element_type=jnp.float32)
    half = out.shape[1] // 2
    return out[:, :half] + out[:, half:]


def squared(value):
    both = jnp.concatenate(split(value), axis=0)
    out = lax.dot_general(both, both, NT, preferred_element_type=jnp.float32)
    half = out.shape[0] // 2
    out = out[:, :half] + out[:, half:]
    return out[:half] + out[half:]


BACK_ROWS = 3 * TILE + 1


def turn_kernel(mem, later, *refs):
    sources, refs = refs[: 6 + later], refs[6 + later :]
    pair_ref, single_ref, edge_ref, live_ref = refs[:4]
    targets, sems = refs[4 + later : -1] + refs[4 : 4 + later], refs[-1]
    copies = [
        pltpu.make_async_copy(source, target, sems.at[i])
        for i, (source, target) in enumerate(zip(sources, targets))
    ]
    for copy in copies:
        copy.start()
    h_ref, u_ref, v_ref, zonal_ref, merid_ref, count_ref = targets[:6]
    tiles = h_ref.shape[0] // mem
    columns = tiles * LANES
    zero = jnp.zeros((TILE, LANES), jnp.float32)
    for ref in (pair_ref, single_ref):
        ref[0:TILE, :] = zero
        ref[columns : columns + TILE, :] = zero
    for copy in copies[:5]:
        copy.wait()
    for t in range(tiles):
        rows = pl.ds(t, mem, stride=tiles)
        lanes = slice(t * LANES, (t + 1) * LANES)
        pair = jnp.concatenate([h_ref[rows, :], u_ref[rows, :]], axis=0)
        zonal = jnp.broadcast_to(zonal_ref[:, lanes], (mem // 2, LANES))
        merid = jnp.broadcast_to(merid_ref[:, lanes], (mem // 2, LANES))
        single = jnp.concatenate([v_ref[rows, :], zonal, merid], axis=0)
        place = slice(STEPS + t * LANES, STEPS + (t + 1) * LANES)
        pair_ref[place, :] = pair.T
        single_ref[place, :] = single.T
    early = row_of((TILE, LANES)) < STEPS
    for i, ref in enumerate((pair_ref, single_ref)):
        edge_ref[i] = jnp.where(early, ref[columns : columns + TILE, :], ref[0:TILE, :])
    for copy in copies[5:]:
        copy.wait()
    for q in range(REG_DEV):
        live_ref[q] = jnp.full(live_ref.shape[1:], count_ref[q], jnp.int32)


def blocks_kernel(groups, strips, width, pair_ref, single_ref, west_ref, east_ref, *refs):
    send_refs = refs[-strips:]
    me = lax.axis_index("region")
    shape = (TILE, LANES)
    early = row_of(shape) < STEPS
    part = lane_of(shape) % (HALF // 2)
    span = 3 * TILE
    for s, send_ref in enumerate(send_refs):
        owner = me ^ s
        first, last = early & (owner == 0), ~early & (owner == strips - 1)
        courant = jnp.zeros(shape, jnp.float32)
        for p in range(groups // 2):
            for j in range(3):
                pairs, singles = [], []
                for group in (2 * p, 2 * p + 1):
                    start = pl.multiple_of(width * (group * strips + owner) + TILE * j, TILE)
                    pair = pair_ref[pl.ds(start, TILE), :]
                    single = single_ref[pl.ds(start, TILE), :]
                    if group == 0 and j == 0:
                        pair = jnp.where(first, west_ref[0], pair)
                        single = jnp.where(first, west_ref[1], single)
                    if group == groups - 1 and j == 2:
                        pair = jnp.where(last, east_ref[0], pair)
                        single = jnp.where(last, east_ref[1], single)
                    pairs.append(pair)
                    singles.append(single)
                    courant = jnp.where(part == 3 * group + j, single, courant)
                place = 3 * span * p + TILE * j
                send_ref[place : place + TILE, :] = low_pair(*pairs)
                send_ref[place + span : place + span + TILE, :] = high_pair(*pairs)
                send_ref[place + 2 * span : place + 2 * span + TILE, :] = low_pair(*singles)
        place = 3 * span * (groups // 2)
        send_ref[place : place + TILE, :] = courant


def forecast_kernel(groups, strips, width, *refs):
    got_refs, refs = refs[:strips], refs[strips:]
    send_refs, (got_ref, turned_ref) = refs[:groups], refs[groups:]
    span = width + 2 * STEPS
    per_region = strips // REG_DEV
    cells = per_region * width
    me = lax.axis_index("region")
    for s, ref in enumerate(got_refs):
        got_ref[me ^ s] = ref[...]
    low = lane_of((TILE, LANES)) < HALF
    tail = 3 * span * (groups // 2)
    for p in range(groups // 2):

        def field(r, i):
            return got_ref[r, 3 * span * p + span * i : 3 * span * p + span * (i + 1), :]

        def courant(r, first):
            mixed = got_ref[r, tail : tail + TILE, :]
            parts = []
            for j in range(3):
                even, odd = first + 6 * p + j, first + 6 * p + 3 + j
                parts.append(
                    jnp.where(
                        low,
                        jnp.broadcast_to(mixed[:, even : even + 1], (TILE, LANES)),
                        jnp.broadcast_to(mixed[:, odd : odd + 1], (TILE, LANES)),
                    )
                )
            return jnp.concatenate(parts, axis=0)

        h = [field(r, 0) for r in range(strips)]
        u = [field(r, 1) for r in range(strips)]
        v = [field(r, 2) for r in range(strips)]
        zonal = [courant(r, HALF) for r in range(strips)]
        merid = [courant(r, HALF + HALF // 2) for r in range(strips)]
        for _ in range(STEPS):
            flux_v = [merid[r] * v[r] for r in range(strips)]
            for r in range(strips):
                flux_u = zonal[r] * u[r]
                south = flux_v[r - 1] if r else jnp.zeros_like(flux_u)
                h[r] = h[r] - (flux_u - pltpu.roll(flux_u, 1, 0) + flux_v[r] - south)
            for r in range(strips):
                north = h[r + 1] if r + 1 < strips else jnp.zeros_like(h[r])
                u[r] = u[r] - (pltpu.roll(h[r], span - 1, 0) - h[r])
                v[r] = v[r] - (north - h[r])
        for i, state in enumerate((h, u, v)):
            inner = [pltpu.roll(state[r], span - STEPS, 0)[:width] for r in range(strips)]
            for s in range(per_region):
                lower, upper = inner[s], inner[per_region + s]
                place = slice(i * cells + s * width, i * cells + (s + 1) * width)
                turned_ref[2 * p, place, :] = low_pair(lower, upper)
                turned_ref[2 * p + 1, place, :] = high_pair(lower, upper)
    mine = lax.axis_index("member")
    for s, ref in enumerate(send_refs):
        ref[...] = turned_ref[mine ^ s]


def collect(got_refs, all_ref, x_ref):
    states = all_ref.shape[1]
    mine = lax.axis_index("member")
    for s, ref in enumerate(got_refs):
        all_ref[mine ^ s] = ref[...]
    for p in range(len(got_refs) // 2):
        even, odd = all_ref[2 * p], all_ref[2 * p + 1]
        lanes = slice(p * LANES, (p + 1) * LANES)
        x_ref[0, :states, lanes] = low_pair(even, odd)
        x_ref[1, :states, lanes] = high_pair(even, odd)


def observe_kernel(live_ref, index_ref, weight_ref, value_ref, var_ref, info_ref, pull_ref):
    states = info_ref.shape[1]
    obs = index_ref.shape[2]
    for q in range(REG_DEV):
        state = row_of((states, obs))
        operator = jnp.zeros((states, obs), jnp.float32)
        for j in range(index_ref.shape[1]):
            hit = state == index_ref[q, j : j + 1, :]
            operator = operator + jnp.where(hit, weight_ref[q, j : j + 1, :], 0.0)
        live = lane_of((1, obs)) < live_ref[q, 0:1, 0:1]
        inverse = jnp.where(live, 1.0 / var_ref[q : q + 1, :], 0.0)
        scaled = operator * inverse
        info_ref[q] = lax.dot_general(
            scaled, operator, NT, precision=HIGHEST, preferred_element_type=jnp.float32
        )
        pulled = jnp.sum(scaled * value_ref[q : q + 1, :], axis=1, keepdims=True)
        pull_ref[q] = jnp.broadcast_to(pulled, (states, LANES))


def analyse(members, x_ref, info_ref, pull_ref, out_ref):
    states = x_ref.shape[1]
    square = (states, states)
    diagonal = row_of(square) == lane_of(square)
    identity = jnp.where(diagonal, 1.0, 0.0)
    regions = range(REG_DEV)
    scale = 1.0 / (members - 1)

    def as_row(column):
        return jnp.sum(jnp.where(diagonal, column, 0.0), axis=0, keepdims=True)

    def applied(matrix, row):
        return jnp.sum(matrix * row, axis=1, keepdims=True)

    x = [x_ref[q] for q in regions]
    means = [jnp.sum(x[q], axis=1, keepdims=True) / members for q in regions]
    spreads = [x[q] - means[q] for q in regions]
    covs = [squared(spreads[q]) for q in regions]
    gains = [times(beside(covs[q]), stacked(info_ref[q] * scale)) for q in regions]
    rights = [stacked(gains[q]) for q in regions]
    gains_2 = [times(beside(gains[q]), rights[q]) for q in regions]
    pulls, inverse_norms, iterates, inverses = [], [], [], []
    for q in regions:
        pulled = pull_ref[q][:, 0:1] - applied(info_ref[q], as_row(means[q]))
        pulls.append(jnp.sum(covs[q] * pulled, axis=0, keepdims=True))
        trace = jnp.sum(jnp.where(diagonal, gains_2[q] + 2.0 * gains[q], 0.0), keepdims=True)
        inverse_norms.append(lax.rsqrt(trace + members))
    for q in regions:
        norm = inverse_norms[q]
        first = (identity + gains[q]) * norm
        second = (identity + 2.0 * gains[q] + gains_2[q]) * (norm * norm)
        third = (second + times(beside(second), rights[q])) * norm
        inverses.append(1.5 * identity - 0.5 * first)
        iterates.append(2.25 * first - 1.5 * second + 0.25 * third)
    for _ in range(1, NEWTON - 1):
        rights = [stacked(iterates[q]) for q in regions]
        lefts = [
            jnp.concatenate([beside(iterates[q]), beside(inverses[q])], axis=0) for q in regions
        ]
        both = [times(lefts[q], rights[q]) for q in regions]
        seconds = [both[q][:states] for q in regions]
        thirds = [times(beside(seconds[q]), rights[q]) for q in regions]
        inverses = [1.5 * inverses[q] - 0.5 * both[q][states:] for q in regions]
        iterates = [
            2.25 * iterates[q] - 1.5 * seconds[q] + 0.25 * thirds[q] for q in regions
        ]
    increments = []
    for q in regions:
        high, low = split(spreads[q])
        wide = beside(inverses[q])
        moved = lax.dot_general(
            wide, jnp.concatenate([high, high], axis=0), NN, preferred_element_type=jnp.float32
        )
        moved = moved + lax.dot_general(
            wide[:, :states], low, NN, preferred_element_type=jnp.float32
        )
        twice = applied(inverses[q], as_row(applied(inverses[q], pulls[q])))
        factor = 1.5 * identity - 0.5 * iterates[q]
        twice = applied(factor, as_row(applied(factor, as_row(twice))))
        increment = twice * (inverse_norms[q] * scale)
        increments.append(increment)
        high, low = split(moved * jnp.sqrt(inverse_norms[q]))
        wide = beside(factor)
        moved = lax.dot_general(
            wide, jnp.concatenate([high, high], axis=0), NN, preferred_element_type=jnp.float32
        )
        moved = moved + lax.dot_general(
            wide[:, :states], low, NN, preferred_element_type=jnp.float32
        )
        out_ref[q] = moved + (means[q] + increment)
    return increments


def pack(groups, strips, width, ana_ref, increments, send_ref):
    per_region = strips // REG_DEV
    cells = per_region * width
    states = increments[0].shape[0]
    state = row_of((states, LANES))
    lane = lane_of((states, LANES))
    for r in range(strips):
        q, s = divmod(r, per_region)
        wanted = (lane // width) * cells + s * width + lane % width
        hit = (state == wanted) & (lane < 3 * width)
        row = jnp.sum(jnp.where(hit, increments[q], 0.0), axis=0, keepdims=True)
        for group in range(groups):
            block = group * strips + r
            lanes = slice((group // 2) * LANES, (group // 2 + 1) * LANES)
            pair = high_pair if group % 2 else low_pair
            for i in range(3):
                first = i * cells + s * width
                tile = pair(
                    ana_ref[q, first : first + TILE, lanes],
                    ana_ref[q, first + TILE : first + 2 * TILE, lanes],
                )
                send_ref[BACK_ROWS * block + TILE * i : BACK_ROWS * block + TILE * (i + 1), :] = tile
            send_ref[BACK_ROWS * (block + 1) - 1 : BACK_ROWS * (block + 1), :] = row


def region_kernel(groups, strips, width, *refs):
    got_refs, (info_ref, pull_ref, send_ref, all_ref, x_ref, ana_ref) = refs[:groups], refs[groups:]
    states = all_ref.shape[1]
    if states < x_ref.shape[1]:
        x_ref[:, states:, :] = jnp.zeros_like(x_ref[:, states:, :])
    collect(got_refs, all_ref, x_ref)
    increments = analyse(x_ref.shape[2], x_ref, info_ref, pull_ref, ana_ref)
    pack(groups, strips, width, ana_ref, increments, send_ref)


def home_kernel(mem, strips, width, got_ref, ctrl_ref, h_ref, u_ref, v_ref, fine_ref):
    tiles = got_ref.shape[0] // BACK_ROWS * width // LANES
    per_tile = LANES // width
    for i, out_ref in enumerate((h_ref, u_ref, v_ref)):
        for t in range(0, tiles, 2):
            rows = []
            for k in range(per_tile):
                first = BACK_ROWS * (t * per_tile + k) + TILE * i
                even = got_ref[first : first + TILE, :]
                first += BACK_ROWS * per_tile
                odd = got_ref[first : first + TILE, :]
                rows += [low_pair(even, odd), high_pair(even, odd)]
            turned = jnp.concatenate(rows, axis=0).T
            out_ref[pl.ds(t, mem, stride=tiles), :] = turned[:mem]
            out_ref[pl.ds(t + 1, mem, stride=tiles), :] = turned[mem:]
    mine = lax.axis_index("member") * strips
    per_fine = LANES // (2 * width)
    row = row_of((width, LANES))
    lane = lane_of((width, LANES))
    for t in range(ctrl_ref.shape[3] // LANES):
        rows = [
            got_ref[pl.ds(BACK_ROWS * (mine + t * per_fine + b) + BACK_ROWS - 1, 1), :]
            for b in range(per_fine)
        ]
        columns = [jnp.broadcast_to(r, (LANES, LANES)).T[:, 0:1] for r in rows]
        for i in range(3):
            total = jnp.zeros((1, LANES), jnp.float32)
            for b in range(per_fine):
                hit = ((lane // 2) % width == row) & (lane // (2 * width) == b)
                part = jnp.where(hit, columns[b][i * width : (i + 1) * width], 0.0)
                total = total + jnp.sum(part, axis=0, keepdims=True)
            lanes = slice(t * LANES, (t + 1) * LANES)
            for e in range(2):
                fine_ref[i, e, :, lanes] = ctrl_ref[i, e, :, lanes] + total


def collect_kernel(groups, *refs):
    collect(refs[:groups], refs[-1], refs[-2])


def pack_kernel(groups, strips, width, ana_ref, inc_ref, send_ref):
    pack(groups, strips, width, ana_ref, [inc_ref[q] for q in range(REG_DEV)], send_ref)


def analyse_in_members(x, obs_index, obs_weight, obs_value, obs_var, obs_count):
    states, members = x.shape[1:]
    mean_state = jnp.mean(x, axis=2, keepdims=True)
    spread = x - mean_state
    picks = (obs_index[:, :, :, None] == jnp.arange(states)).astype(jnp.float32)
    operator = jnp.sum(picks * obs_weight[:, :, :, None], axis=2)
    predicted = jnp.einsum("ros,rsk->rko", operator, x, precision=HIGHEST)
    mean_obs = jnp.mean(predicted, axis=1, keepdims=True)
    obs_spread = predicted - mean_obs
    active_obs = jnp.arange(obs_value.shape[1])[None, :] < obs_count[:, None]
    weighted = obs_spread * (active_obs.astype(jnp.float32) / obs_var)[:, None, :]
    gram_sum = jnp.einsum("rko,rjo->rkj", weighted, obs_spread, precision=HIGHEST)
    identity = jnp.eye(members, dtype=jnp.float32)
    scaled = identity + gram_sum / (members - 1)
    frobenius = jnp.sqrt(jnp.sum(scaled * scaled, axis=(1, 2), keepdims=True))
    iterate = scaled / frobenius
    inverse_root = jnp.broadcast_to(identity, scaled.shape)
    dot = functools.partial(jnp.einsum, "rij,rjk->rik", precision=HIGHEST)
    for _ in range(NEWTON):
        factor = 1.5 * identity - 0.5 * dot(inverse_root, iterate)
        iterate = dot(iterate, factor)
        inverse_root = dot(factor, inverse_root)
    transform = inverse_root / jnp.sqrt(frobenius)
    innovation = jnp.einsum(
        "rko,ro->rk", weighted, obs_value - mean_obs[:, 0], precision=HIGHEST
    )
    halfway = jnp.einsum("rkj,rj->rk", transform, innovation, precision=HIGHEST)
    mean_weights = jnp.einsum("rkj,rj->rk", transform, halfway, precision=HIGHEST) / (members - 1)
    increment = jnp.einsum("rk,rsk->rs", mean_weights, spread, precision=HIGHEST)[:, :, None]
    moved = jnp.einsum("rjk,rsj->rsk", transform, spread, precision=HIGHEST)
    return mean_state + increment + moved, increment


def call(kernel, out_shape, specs, scratch=(), cost=None):
    many = isinstance(out_shape, tuple)
    return pl.pallas_call(
        kernel,
        out_shape=out_shape,
        in_specs=specs,
        out_specs=tuple(VMEM for _ in out_shape) if many else VMEM,
        scratch_shapes=scratch,
        cost_estimate=cost,
        compiler_params=pltpu.CompilerParams(vmem_limit_bytes=GRANT),
    )


def swapped_blocks(blocks, axis):
    count = len(blocks)
    if count <= 4:
        routes = [[(i, i ^ s) for i in range(count)] for s in range(count)]
        moved = []
        for s in range(1, count):
            moved.append(lax.ppermute(blocks[s], axis, routes[s]))
        return [kept(block) for block in [blocks[0], *moved]]
    order = lax.axis_index(axis) ^ jnp.arange(count)
    moved = lax.all_to_all(jnp.stack(blocks)[order], axis, split_axis=0, concat_axis=0, tiled=True)
    return [kept(block) for block in moved[order]]


def exchanged(blocks, axes, count):
    dense = blocks.reshape(count, -1, 1, LANES)
    return lax.all_to_all(dense, axes, split_axis=0, concat_axis=0, tiled=True).reshape(blocks.shape)


def f32(*shape):
    return jax.ShapeDtypeStruct(shape, jnp.float32)


def near(*shape):
    return pltpu.VMEM(shape, jnp.float32)


def far(array):
    return pltpu.with_memory_space_constraint(array, pltpu.HBM)


def kept(array):
    return pltpu.with_memory_space_constraint(array, pltpu.VMEM)


def shards(
    sample_surface_elevation,
    sample_zonal_current,
    sample_meridional_current,
    zonal_edge_layer_courant,
    meridional_edge_layer_courant,
    obs_index,
    obs_weight,
    obs_value,
    obs_var,
    obs_count,
    fine_ctrl,
):
    groups = lax.axis_size("member")
    strips = lax.axis_size("region")
    owners = ("member", "region")
    mem, rows, columns = sample_surface_elevation.shape
    count = groups * strips
    width = columns // count
    members = groups * mem
    assert rows == 1 and 2 * mem == LANES and width == 2 * TILE and STEPS * 2 == TILE
    assert columns % (2 * LANES) == 0 and strips % REG_DEV == 0 and REG_DEV == 2
    assert all(size > 1 and size & (size - 1) == 0 for size in (groups, strips))
    assert 3 * groups <= HALF // 2
    flat = (mem * columns // LANES, LANES)
    states = 3 * width * strips // REG_DEV
    small = states <= members
    later = [fine_ctrl]
    if small:
        later += [obs_index.transpose(0, 2, 1), obs_weight.transpose(0, 2, 1), obs_value, obs_var]
    pair, single, edge, live, ctrl, *seen = call(
        functools.partial(turn_kernel, mem, len(later)),
        (
            near(columns + TILE, LANES),
            near(columns + TILE, LANES),
            near(2, TILE, LANES),
            pltpu.VMEM((REG_DEV, TILE, LANES), jnp.int32),
            *(pltpu.VMEM(array.shape, array.dtype) for array in later),
        ),
        [HBM] * (6 + len(later)),
        scratch=[
            *[pltpu.VMEM(flat, jnp.float32)] * 3,
            *[pltpu.VMEM((1, columns), jnp.float32)] * 2,
            pltpu.SMEM((REG_DEV,), jnp.int32),
            pltpu.SemaphoreType.DMA((6 + len(later),)),
        ],
    )(
        far(sample_surface_elevation.reshape(flat)),
        far(sample_zonal_current.reshape(flat)),
        far(sample_meridional_current.reshape(flat)),
        far(zonal_edge_layer_courant),
        far(meridional_edge_layer_courant),
        far(obs_count),
        *(far(array) for array in later),
    )
    from_west = passed_along(edge, "fine", 1)
    from_east = from_west if lax.axis_size("fine") == 2 else passed_along(edge, "fine", -1)
    ahead = []
    if small:
        padded = -(-states // LANES) * LANES
        obs = obs_value.shape[1]
        info, pull = call(
            observe_kernel,
            (near(REG_DEV, padded, padded), near(REG_DEV, padded, LANES)),
            [VMEM] * 5,
            cost=pl.CostEstimate(
                flops=12 * REG_DEV * padded * padded * obs, bytes_accessed=1 << 20, transcendentals=0
            ),
        )(kept(live), *(kept(array) for array in seen))
        ahead = [kept(pull)]
    layout = (groups, strips, width)
    span = width + 2 * STEPS
    out = call(
        functools.partial(blocks_kernel, *layout),
        tuple([near(3 * span * (groups // 2) + TILE, LANES)] * strips),
        [VMEM] * (4 + len(ahead)),
    )(kept(pair), kept(single), kept(from_west), kept(from_east), *ahead)
    got = swapped_blocks(out, "region")
    turned = call(
        functools.partial(forecast_kernel, *layout),
        tuple([near(states, LANES)] * groups),
        [VMEM] * strips,
        scratch=[
            pltpu.VMEM((strips, *out[0].shape), jnp.float32),
            pltpu.VMEM((groups, states, LANES), jnp.float32),
        ],
    )(*got)
    got = swapped_blocks(turned, "member")
    back_shape = near(count * BACK_ROWS, LANES)
    gathered = pltpu.VMEM((groups, states, LANES), jnp.float32)
    if small:
        back = call(
            functools.partial(region_kernel, *layout),
            back_shape,
            [VMEM] * (groups + 2),
            scratch=[
                gathered,
                pltpu.VMEM((REG_DEV, padded, members), jnp.float32),
                pltpu.VMEM((REG_DEV, padded, members), jnp.float32),
            ],
        )(*got, kept(info), kept(pull))
    else:
        x = call(
            functools.partial(collect_kernel, groups),
            f32(REG_DEV, states, members),
            [VMEM] * groups,
            scratch=[gathered],
        )(*got)
        analysis, increment = analyse_in_members(
            x, obs_index, obs_weight, obs_value, obs_var, obs_count
        )
        back = call(
            functools.partial(pack_kernel, *layout), back_shape, [VMEM] * 2
        )(analysis, increment)
    home = exchanged(back, owners, count)
    ana_h, ana_u, ana_v, fine_out = call(
        functools.partial(home_kernel, mem, strips, width),
        (f32(*flat), f32(*flat), f32(*flat), f32(*fine_ctrl.shape)),
        [VMEM, VMEM],
    )(kept(home), kept(ctrl))
    shape = (mem, rows, columns)
    return (ana_h.reshape(shape), ana_u.reshape(shape), ana_v.reshape(shape), fine_out)


def solution(mesh):
    strip = P("member", "region", "fine")
    owner = ("member", "region", "fine")
    fine = P(None, "region", "fine", "member")
    return jax.shard_map(
        shards,
        mesh=mesh,
        in_specs=(
            strip,
            strip,
            strip,
            P("region", "fine"),
            P("region", "fine"),
            P(owner, None, None),
            P(owner, None, None),
            P(owner, None),
            P(owner, None),
            P(owner),
            fine,
        ),
        out_specs=(strip, strip, strip, fine),
        check_vma=False,
    )
```

```python
import functools

import jax
import jax.numpy as jnp
from jax import lax
from jax.experimental import pallas as pl
from jax.experimental.pallas import tpu as pltpu
from jax.sharding import PartitionSpec as P


REG_DEV = 2
STEPS = 4
NEWTON = 8
LANES = 128
TILE = 8
HALF = LANES // 2
GRANT = 32 << 20


HIGHEST = lax.Precision.HIGHEST
NT = (((1,), (1,)), ((), ()))
NN = (((1,), (0,)), ((), ()))
VMEM = pl.BlockSpec(memory_space=pltpu.VMEM)
SMEM = pl.BlockSpec(memory_space=pltpu.SMEM)
HBM = pl.BlockSpec(memory_space=pltpu.HBM)


def passed_along(block, axis, distance):
    count = lax.axis_size(axis)
    route = [((i - distance) % count, i) for i in range(count)]
    return lax.ppermute(block, axis, route)


def lane_of(shape):
    return lax.broadcasted_iota(jnp.int32, shape, 1)


def row_of(shape):
    return lax.broadcasted_iota(jnp.int32, shape, 0)


def swapped(tile):
    return pltpu.roll(tile, HALF, 1)


def low_pair(even, odd):
    return jnp.where(lane_of(even.shape) < HALF, even, swapped(odd))


def high_pair(even, odd):
    return jnp.where(lane_of(even.shape) < HALF, swapped(even), odd)


def split(value):
    high = value.astype(jnp.bfloat16)
    return high, (value - high.astype(jnp.float32)).astype(jnp.bfloat16)


def beside(value):
    return jnp.concatenate(split(value), axis=1)


def filled(value, rows):
    if value.shape[0] == rows:
        return value
    return jnp.concatenate([value, jnp.zeros((rows - value.shape[0], value.shape[1]), value.dtype)], axis=0)


def stacked(value):
    both = filled(jnp.concatenate(split(value), axis=1), value.shape[1])
    return jnp.concatenate([both, both], axis=0)


def times(left, right):
    out = lax.dot_general(left, right, NN, preferred_element_type=jnp.float32)
    half = out.shape[1] // 2
    return out[:, :half] + out[:, half:]


def squared(value, columns):
    high, low = split(value)
    both = jnp.concatenate([high, low], axis=0)
    wide = jnp.concatenate([filled(high, columns), filled(low, columns)], axis=0)
    out = lax.dot_general(both, wide, NT, preferred_element_type=jnp.float32)
    out = out[:, :columns] + out[:, columns:]
    half = out.shape[0] // 2
    return out[:half] + out[half:]


def applied_to(left, value):
    columns = left.shape[1]
    wide = beside(left)
    high, low = (filled(part, columns) for part in split(value))
    dot = functools.partial(
        lax.dot_general, dimension_numbers=NN, preferred_element_type=jnp.float32
    )
    return dot(wide, jnp.concatenate([high, high], axis=0)) + dot(wide[:, :columns], low)


BACK_ROWS = 3 * TILE + 1


def turn_kernel(mem, later, *refs):
    sources, refs = refs[: 6 + later], refs[6 + later :]
    pair_ref, single_ref, edge_ref, live_ref = refs[:4]
    targets, sems = refs[4 + later : -1] + refs[4 : 4 + later], refs[-1]
    copies = [
        pltpu.make_async_copy(source, target, sems.at[i])
        for i, (source, target) in enumerate(zip(sources, targets))
    ]
    for copy in copies:
        copy.start()
    h_ref, u_ref, v_ref, zonal_ref, merid_ref, count_ref = targets[:6]
    tiles = h_ref.shape[0] // mem
    columns = tiles * LANES
    zero = jnp.zeros((TILE, LANES), jnp.float32)
    for ref in (pair_ref, single_ref):
        ref[0:TILE, :] = zero
        ref[columns : columns + TILE, :] = zero
    for copy in copies[:5]:
        copy.wait()
    for t in range(tiles):
        rows = pl.ds(t, mem, stride=tiles)
        lanes = slice(t * LANES, (t + 1) * LANES)
        pair = jnp.concatenate([h_ref[rows, :], u_ref[rows, :]], axis=0)
        zonal = jnp.broadcast_to(zonal_ref[:, lanes], (mem // 2, LANES))
        merid = jnp.broadcast_to(merid_ref[:, lanes], (mem // 2, LANES))
        single = jnp.concatenate([v_ref[rows, :], zonal, merid], axis=0)
        place = slice(STEPS + t * LANES, STEPS + (t + 1) * LANES)
        pair_ref[place, :] = pair.T
        single_ref[place, :] = single.T
    early = row_of((TILE, LANES)) < STEPS
    for i, ref in enumerate((pair_ref, single_ref)):
        edge_ref[i] = jnp.where(early, ref[columns : columns + TILE, :], ref[0:TILE, :])
    for copy in copies[5:]:
        copy.wait()
    for q in range(REG_DEV):
        live_ref[q] = jnp.full(live_ref.shape[1:], count_ref[q], jnp.int32)


def blocks_kernel(groups, strips, width, pair_ref, single_ref, west_ref, east_ref, *refs):
    send_refs = refs[-strips:]
    me = lax.axis_index("region")
    shape = (TILE, LANES)
    early = row_of(shape) < STEPS
    part = lane_of(shape) % (HALF // 2)
    span = 3 * TILE
    for s, send_ref in enumerate(send_refs):
        owner = me ^ s
        first, last = early & (owner == 0), ~early & (owner == strips - 1)
        courant = jnp.zeros(shape, jnp.float32)
        for p in range(groups // 2):
            for j in range(3):
                pairs, singles = [], []
                for group in (2 * p, 2 * p + 1):
                    start = pl.multiple_of(width * (group * strips + owner) + TILE * j, TILE)
                    pair = pair_ref[pl.ds(start, TILE), :]
                    single = single_ref[pl.ds(start, TILE), :]
                    if group == 0 and j == 0:
                        pair = jnp.where(first, west_ref[0], pair)
                        single = jnp.where(first, west_ref[1], single)
                    if group == groups - 1 and j == 2:
                        pair = jnp.where(last, east_ref[0], pair)
                        single = jnp.where(last, east_ref[1], single)
                    pairs.append(pair)
                    singles.append(single)
                    courant = jnp.where(part == 3 * group + j, single, courant)
                place = 3 * span * p + TILE * j
                send_ref[place : place + TILE, :] = low_pair(*pairs)
                send_ref[place + span : place + span + TILE, :] = high_pair(*pairs)
                send_ref[place + 2 * span : place + 2 * span + TILE, :] = low_pair(*singles)
        place = 3 * span * (groups // 2)
        send_ref[place : place + TILE, :] = courant


def forecast_kernel(groups, strips, width, *refs):
    got_refs, refs = refs[:strips], refs[strips:]
    send_refs, (got_ref, turned_ref) = refs[:groups], refs[groups:]
    span = width + 2 * STEPS
    per_region = strips // REG_DEV
    cells = per_region * width
    me = lax.axis_index("region")
    for s, ref in enumerate(got_refs):
        got_ref[me ^ s] = ref[...]
    low = lane_of((TILE, LANES)) < HALF
    tail = 3 * span * (groups // 2)
    for p in range(groups // 2):

        def field(r, i):
            return got_ref[r, 3 * span * p + span * i : 3 * span * p + span * (i + 1), :]

        def courant(r, first):
            mixed = got_ref[r, tail : tail + TILE, :]
            parts = []
            for j in range(3):
                even, odd = first + 6 * p + j, first + 6 * p + 3 + j
                parts.append(
                    jnp.where(
                        low,
                        jnp.broadcast_to(mixed[:, even : even + 1], (TILE, LANES)),
                        jnp.broadcast_to(mixed[:, odd : odd + 1], (TILE, LANES)),
                    )
                )
            return jnp.concatenate(parts, axis=0)

        h = [field(r, 0) for r in range(strips)]
        u = [field(r, 1) for r in range(strips)]
        v = [field(r, 2) for r in range(strips)]
        zonal = [courant(r, HALF) for r in range(strips)]
        merid = [courant(r, HALF + HALF // 2) for r in range(strips)]
        for _ in range(STEPS):
            flux_v = [merid[r] * v[r] for r in range(strips)]
            for r in range(strips):
                flux_u = zonal[r] * u[r]
                south = flux_v[r - 1] if r else jnp.zeros_like(flux_u)
                h[r] = h[r] - (flux_u - pltpu.roll(flux_u, 1, 0) + flux_v[r] - south)
            for r in range(strips):
                north = h[r + 1] if r + 1 < strips else jnp.zeros_like(h[r])
                u[r] = u[r] - (pltpu.roll(h[r], span - 1, 0) - h[r])
                v[r] = v[r] - (north - h[r])
        for i, state in enumerate((h, u, v)):
            inner = [pltpu.roll(state[r], span - STEPS, 0)[:width] for r in range(strips)]
            for s in range(per_region):
                lower, upper = inner[s], inner[per_region + s]
                place = slice(i * cells + s * width, i * cells + (s + 1) * width)
                turned_ref[2 * p, place, :] = low_pair(lower, upper)
                turned_ref[2 * p + 1, place, :] = high_pair(lower, upper)
    mine = lax.axis_index("member")
    for s, ref in enumerate(send_refs):
        ref[...] = turned_ref[mine ^ s]


def collect(got_refs, all_ref, x_ref):
    mine = lax.axis_index("member")
    for s, ref in enumerate(got_refs):
        all_ref[mine ^ s] = ref[...]
    for p in range(len(got_refs) // 2):
        even, odd = all_ref[2 * p], all_ref[2 * p + 1]
        lanes = slice(p * LANES, (p + 1) * LANES)
        x_ref[0, :, lanes] = low_pair(even, odd)
        x_ref[1, :, lanes] = high_pair(even, odd)


def observe_kernel(live_ref, index_ref, weight_ref, value_ref, var_ref, info_ref, pull_ref):
    states, padded = info_ref.shape[1:]
    obs = index_ref.shape[2]
    for q in range(REG_DEV):
        state = row_of((states, obs))
        operator = jnp.zeros((states, obs), jnp.float32)
        for j in range(index_ref.shape[1]):
            hit = state == index_ref[q, j : j + 1, :]
            operator = operator + jnp.where(hit, weight_ref[q, j : j + 1, :], 0.0)
        live = lane_of((1, obs)) < live_ref[q, 0:1, 0:1]
        inverse = jnp.where(live, 1.0 / var_ref[q : q + 1, :], 0.0)
        scaled = operator * inverse
        info_ref[q] = lax.dot_general(
            scaled,
            filled(operator, padded),
            NT,
            precision=HIGHEST,
            preferred_element_type=jnp.float32,
        )
        pulled = jnp.sum(scaled * value_ref[q : q + 1, :], axis=1, keepdims=True)
        pull_ref[q] = jnp.broadcast_to(pulled, (states, LANES))


def analyse(members, x_ref, info_ref, pull_ref, out_ref):
    states, padded = info_ref.shape[1:]
    square = (states, padded)
    diagonal = row_of(square) == lane_of(square)
    identity = jnp.where(diagonal, 1.0, 0.0)
    regions = range(REG_DEV)
    scale = 1.0 / (members - 1)

    def as_row(column):
        return jnp.sum(jnp.where(diagonal, column, 0.0), axis=0, keepdims=True)

    def applied(matrix, row):
        return jnp.sum(matrix * row, axis=1, keepdims=True)

    x = [x_ref[q] for q in regions]
    means = [jnp.sum(x[q], axis=1, keepdims=True) / members for q in regions]
    spreads = [x[q] - means[q] for q in regions]
    covs = [squared(spreads[q], padded) for q in regions]
    gains = [times(beside(covs[q]), stacked(info_ref[q] * scale)) for q in regions]
    rights = [stacked(gains[q]) for q in regions]
    gains_2 = [times(beside(gains[q]), rights[q]) for q in regions]
    pulls, inverse_norms, iterates, inverses = [], [], [], []
    for q in regions:
        pulled = pull_ref[q][:, 0:1] - applied(info_ref[q], as_row(means[q]))
        pulls.append(jnp.sum(covs[q] * pulled, axis=0, keepdims=True))
        trace = jnp.sum(jnp.where(diagonal, gains_2[q] + 2.0 * gains[q], 0.0), keepdims=True)
        inverse_norms.append(lax.rsqrt(trace + members))
    for q in regions:
        norm = inverse_norms[q]
        first = (identity + gains[q]) * norm
        second = (identity + 2.0 * gains[q] + gains_2[q]) * (norm * norm)
        third = (second + times(beside(second), rights[q])) * norm
        inverses.append(1.5 * identity - 0.5 * first)
        iterates.append(2.25 * first - 1.5 * second + 0.25 * third)
    for _ in range(1, NEWTON - 1):
        rights = [stacked(iterates[q]) for q in regions]
        lefts = [
            jnp.concatenate([beside(iterates[q]), beside(inverses[q])], axis=0) for q in regions
        ]
        both = [times(lefts[q], rights[q]) for q in regions]
        seconds = [both[q][:states] for q in regions]
        thirds = [times(beside(seconds[q]), rights[q]) for q in regions]
        inverses = [1.5 * inverses[q] - 0.5 * both[q][states:] for q in regions]
        iterates = [
            2.25 * iterates[q] - 1.5 * seconds[q] + 0.25 * thirds[q] for q in regions
        ]
    increments = []
    for q in regions:
        moved = applied_to(inverses[q], spreads[q])
        twice = applied(inverses[q], as_row(applied(inverses[q], pulls[q])))
        factor = 1.5 * identity - 0.5 * iterates[q]
        twice = applied(factor, as_row(applied(factor, as_row(twice))))
        increment = twice * (inverse_norms[q] * scale)
        increments.append(increment)
        moved = applied_to(factor, moved * jnp.sqrt(inverse_norms[q]))
        out_ref[q] = moved + (means[q] + increment)
    return increments


def pack(groups, strips, width, ana_ref, increments, send_ref):
    per_region = strips // REG_DEV
    cells = per_region * width
    states = increments[0].shape[0]
    state = row_of((states, LANES))
    lane = lane_of((states, LANES))
    for r in range(strips):
        q, s = divmod(r, per_region)
        wanted = (lane // width) * cells + s * width + lane % width
        hit = (state == wanted) & (lane < 3 * width)
        row = jnp.sum(jnp.where(hit, increments[q], 0.0), axis=0, keepdims=True)
        for group in range(groups):
            block = group * strips + r
            lanes = slice((group // 2) * LANES, (group // 2 + 1) * LANES)
            pair = high_pair if group % 2 else low_pair
            for i in range(3):
                first = i * cells + s * width
                tile = pair(
                    ana_ref[q, first : first + TILE, lanes],
                    ana_ref[q, first + TILE : first + 2 * TILE, lanes],
                )
                send_ref[BACK_ROWS * block + TILE * i : BACK_ROWS * block + TILE * (i + 1), :] = tile
            send_ref[BACK_ROWS * (block + 1) - 1 : BACK_ROWS * (block + 1), :] = row


def region_kernel(groups, strips, width, *refs):
    got_refs, (info_ref, pull_ref, send_ref, all_ref, x_ref, ana_ref) = refs[:groups], refs[groups:]
    collect(got_refs, all_ref, x_ref)
    increments = analyse(x_ref.shape[2], x_ref, info_ref, pull_ref, ana_ref)
    pack(groups, strips, width, ana_ref, increments, send_ref)


def home_kernel(mem, strips, width, got_ref, ctrl_ref, *refs):
    targets, (h_ref, u_ref, v_ref, fine_ref, sems) = refs[:4], refs[4:]
    copies = [
        pltpu.make_async_copy(source, target, sems.at[i])
        for i, (source, target) in enumerate(zip((h_ref, u_ref, v_ref, fine_ref), targets))
    ]
    tiles = got_ref.shape[0] // BACK_ROWS * width // LANES
    per_tile = LANES // width
    for i, out_ref in enumerate((h_ref, u_ref, v_ref)):
        for t in range(0, tiles, 2):
            rows = []
            for k in range(per_tile):
                first = BACK_ROWS * (t * per_tile + k) + TILE * i
                even = got_ref[first : first + TILE, :]
                first += BACK_ROWS * per_tile
                odd = got_ref[first : first + TILE, :]
                rows += [low_pair(even, odd), high_pair(even, odd)]
            turned = jnp.concatenate(rows, axis=0).T
            out_ref[pl.ds(t, mem, stride=tiles), :] = turned[:mem]
            out_ref[pl.ds(t + 1, mem, stride=tiles), :] = turned[mem:]
        copies[i].start()
    mine = lax.axis_index("member") * strips
    per_fine = LANES // (2 * width)
    row = row_of((width, LANES))
    lane = lane_of((width, LANES))
    for t in range(ctrl_ref.shape[3] // LANES):
        rows = [
            got_ref[pl.ds(BACK_ROWS * (mine + t * per_fine + b) + BACK_ROWS - 1, 1), :]
            for b in range(per_fine)
        ]
        columns = [jnp.broadcast_to(r, (LANES, LANES)).T[:, 0:1] for r in rows]
        for i in range(3):
            total = jnp.zeros((1, LANES), jnp.float32)
            for b in range(per_fine):
                hit = ((lane // 2) % width == row) & (lane // (2 * width) == b)
                part = jnp.where(hit, columns[b][i * width : (i + 1) * width], 0.0)
                total = total + jnp.sum(part, axis=0, keepdims=True)
            lanes = slice(t * LANES, (t + 1) * LANES)
            for e in range(2):
                fine_ref[i, e, :, lanes] = ctrl_ref[i, e, :, lanes] + total
    copies[3].start()
    for copy in copies:
        copy.wait()


def collect_kernel(groups, *refs):
    collect(refs[:groups], refs[-1], refs[-2])


def pack_kernel(groups, strips, width, ana_ref, inc_ref, send_ref):
    pack(groups, strips, width, ana_ref, [inc_ref[q] for q in range(REG_DEV)], send_ref)


def analyse_in_members(x, obs_index, obs_weight, obs_value, obs_var, obs_count):
    states, members = x.shape[1:]
    mean_state = jnp.mean(x, axis=2, keepdims=True)
    spread = x - mean_state
    picks = (obs_index[:, :, :, None] == jnp.arange(states)).astype(jnp.float32)
    operator = jnp.sum(picks * obs_weight[:, :, :, None], axis=2)
    predicted = jnp.einsum("ros,rsk->rko", operator, x, precision=HIGHEST)
    mean_obs = jnp.mean(predicted, axis=1, keepdims=True)
    obs_spread = predicted - mean_obs
    active_obs = jnp.arange(obs_value.shape[1])[None, :] < obs_count[:, None]
    weighted = obs_spread * (active_obs.astype(jnp.float32) / obs_var)[:, None, :]
    gram_sum = jnp.einsum("rko,rjo->rkj", weighted, obs_spread, precision=HIGHEST)
    identity = jnp.eye(members, dtype=jnp.float32)
    scaled = identity + gram_sum / (members - 1)
    frobenius = jnp.sqrt(jnp.sum(scaled * scaled, axis=(1, 2), keepdims=True))
    iterate = scaled / frobenius
    inverse_root = jnp.broadcast_to(identity, scaled.shape)
    dot = functools.partial(jnp.einsum, "rij,rjk->rik", precision=HIGHEST)
    for _ in range(NEWTON):
        factor = 1.5 * identity - 0.5 * dot(inverse_root, iterate)
        iterate = dot(iterate, factor)
        inverse_root = dot(factor, inverse_root)
    transform = inverse_root / jnp.sqrt(frobenius)
    innovation = jnp.einsum(
        "rko,ro->rk", weighted, obs_value - mean_obs[:, 0], precision=HIGHEST
    )
    halfway = jnp.einsum("rkj,rj->rk", transform, innovation, precision=HIGHEST)
    mean_weights = jnp.einsum("rkj,rj->rk", transform, halfway, precision=HIGHEST) / (members - 1)
    increment = jnp.einsum("rk,rsk->rs", mean_weights, spread, precision=HIGHEST)[:, :, None]
    moved = jnp.einsum("rjk,rsj->rsk", transform, spread, precision=HIGHEST)
    return mean_state + increment + moved, increment


def call(kernel, out_shape, specs, scratch=(), cost=None, place=VMEM):
    many = isinstance(out_shape, tuple)
    return pl.pallas_call(
        kernel,
        out_shape=out_shape,
        in_specs=specs,
        out_specs=tuple(place for _ in out_shape) if many else place,
        scratch_shapes=scratch,
        cost_estimate=cost,
        compiler_params=pltpu.CompilerParams(vmem_limit_bytes=GRANT),
    )


def swapped_blocks(blocks, axis):
    count = len(blocks)
    if count <= 4:
        routes = [[(i, i ^ s) for i in range(count)] for s in range(count)]
        moved = []
        for s in range(1, count):
            moved.append(lax.ppermute(blocks[s], axis, routes[s]))
        return [kept(block) for block in [blocks[0], *moved]]
    order = lax.axis_index(axis) ^ jnp.arange(count)
    moved = lax.all_to_all(jnp.stack(blocks)[order], axis, split_axis=0, concat_axis=0, tiled=True)
    return [kept(block) for block in moved[order]]


def exchanged(blocks, axes, count):
    dense = blocks.reshape(count, -1, 1, LANES)
    return lax.all_to_all(dense, axes, split_axis=0, concat_axis=0, tiled=True).reshape(blocks.shape)


def f32(*shape):
    return jax.ShapeDtypeStruct(shape, jnp.float32)


def near(*shape):
    return pltpu.VMEM(shape, jnp.float32)


def far(array):
    return pltpu.with_memory_space_constraint(array, pltpu.HBM)


def kept(array):
    return pltpu.with_memory_space_constraint(array, pltpu.VMEM)


def shards(
    sample_surface_elevation,
    sample_zonal_current,
    sample_meridional_current,
    zonal_edge_layer_courant,
    meridional_edge_layer_courant,
    obs_index,
    obs_weight,
    obs_value,
    obs_var,
    obs_count,
    fine_ctrl,
):
    groups = lax.axis_size("member")
    strips = lax.axis_size("region")
    owners = ("member", "region")
    mem, rows, columns = sample_surface_elevation.shape
    count = groups * strips
    width = columns // count
    members = groups * mem
    assert rows == 1 and 2 * mem == LANES and width == 2 * TILE and STEPS * 2 == TILE
    assert columns % (2 * LANES) == 0 and strips % REG_DEV == 0 and REG_DEV == 2
    assert all(size > 1 and size & (size - 1) == 0 for size in (groups, strips))
    assert 3 * groups <= HALF // 2
    flat = (mem * columns // LANES, LANES)
    states = 3 * width * strips // REG_DEV
    small = states <= members
    later = [fine_ctrl]
    if small:
        later += [obs_index.transpose(0, 2, 1), obs_weight.transpose(0, 2, 1), obs_value, obs_var]
    pair, single, edge, live, ctrl, *seen = call(
        functools.partial(turn_kernel, mem, len(later)),
        (
            near(columns + TILE, LANES),
            near(columns + TILE, LANES),
            near(2, TILE, LANES),
            pltpu.VMEM((REG_DEV, TILE, LANES), jnp.int32),
            *(pltpu.VMEM(array.shape, array.dtype) for array in later),
        ),
        [HBM] * (6 + len(later)),
        scratch=[
            *[pltpu.VMEM(flat, jnp.float32)] * 3,
            *[pltpu.VMEM((1, columns), jnp.float32)] * 2,
            pltpu.SMEM((REG_DEV,), jnp.int32),
            pltpu.SemaphoreType.DMA((6 + len(later),)),
        ],
    )(
        far(sample_surface_elevation.reshape(flat)),
        far(sample_zonal_current.reshape(flat)),
        far(sample_meridional_current.reshape(flat)),
        far(zonal_edge_layer_courant),
        far(meridional_edge_layer_courant),
        far(obs_count),
        *(far(array) for array in later),
    )
    from_west = passed_along(edge, "fine", 1)
    from_east = from_west if lax.axis_size("fine") == 2 else passed_along(edge, "fine", -1)
    ahead = []
    if small:
        padded = -(-states // LANES) * LANES
        obs = obs_value.shape[1]
        info, pull = call(
            observe_kernel,
            (near(REG_DEV, states, padded), near(REG_DEV, states, LANES)),
            [VMEM] * 5,
            cost=pl.CostEstimate(
                flops=12 * REG_DEV * padded * padded * obs, bytes_accessed=1 << 20, transcendentals=0
            ),
        )(kept(live), *(kept(array) for array in seen))
        ahead = [kept(pull)]
    layout = (groups, strips, width)
    span = width + 2 * STEPS
    out = call(
        functools.partial(blocks_kernel, *layout),
        tuple([near(3 * span * (groups // 2) + TILE, LANES)] * strips),
        [VMEM] * (4 + len(ahead)),
    )(kept(pair), kept(single), kept(from_west), kept(from_east), *ahead)
    got = swapped_blocks(out, "region")
    turned = call(
        functools.partial(forecast_kernel, *layout),
        tuple([near(states, LANES)] * groups),
        [VMEM] * strips,
        scratch=[
            pltpu.VMEM((strips, *out[0].shape), jnp.float32),
            pltpu.VMEM((groups, states, LANES), jnp.float32),
        ],
    )(*got)
    got = swapped_blocks(turned, "member")
    back_shape = near(count * BACK_ROWS, LANES)
    gathered = pltpu.VMEM((groups, states, LANES), jnp.float32)
    if small:
        back = call(
            functools.partial(region_kernel, *layout),
            back_shape,
            [VMEM] * (groups + 2),
            scratch=[
                gathered,
                pltpu.VMEM((REG_DEV, states, members), jnp.float32),
                pltpu.VMEM((REG_DEV, states, members), jnp.float32),
            ],
        )(*got, kept(info), kept(pull))
    else:
        x = call(
            functools.partial(collect_kernel, groups),
            f32(REG_DEV, states, members),
            [VMEM] * groups,
            scratch=[gathered],
        )(*got)
        analysis, increment = analyse_in_members(
            x, obs_index, obs_weight, obs_value, obs_var, obs_count
        )
        back = call(
            functools.partial(pack_kernel, *layout), back_shape, [VMEM] * 2
        )(analysis, increment)
    home = exchanged(back, owners, count)
    ana_h, ana_u, ana_v, fine_out = call(
        functools.partial(home_kernel, mem, strips, width),
        (f32(*flat), f32(*flat), f32(*flat), f32(*fine_ctrl.shape)),
        [VMEM, VMEM],
        scratch=[
            *[pltpu.VMEM(flat, jnp.float32)] * 3,
            pltpu.VMEM(fine_ctrl.shape, jnp.float32),
            pltpu.SemaphoreType.DMA((4,)),
        ],
        place=HBM,
    )(kept(home), kept(ctrl))
    shape = (mem, rows, columns)
    return (ana_h.reshape(shape), ana_u.reshape(shape), ana_v.reshape(shape), fine_out)


def solution(mesh):
    strip = P("member", "region", "fine")
    owner = ("member", "region", "fine")
    fine = P(None, "region", "fine", "member")
    return jax.shard_map(
        shards,
        mesh=mesh,
        in_specs=(
            strip,
            strip,
            strip,
            P("region", "fine"),
            P("region", "fine"),
            P(owner, None, None),
            P(owner, None, None),
            P(owner, None),
            P(owner, None),
            P(owner),
            fine,
        ),
        out_specs=(strip, strip, strip, fine),
        check_vma=False,
    )
```

```python
import functools

import jax
import jax.numpy as jnp
from jax import lax
from jax.experimental import pallas as pl
from jax.experimental.pallas import tpu as pltpu
from jax.sharding import PartitionSpec as P


REG_DEV = 2
STEPS = 4
NEWTON = 8
LANES = 128
TILE = 8
HALF = LANES // 2
GRANT = 32 << 20


HIGHEST = lax.Precision.HIGHEST
NT = (((1,), (1,)), ((), ()))
NN = (((1,), (0,)), ((), ()))
VMEM = pl.BlockSpec(memory_space=pltpu.VMEM)
SMEM = pl.BlockSpec(memory_space=pltpu.SMEM)
HBM = pl.BlockSpec(memory_space=pltpu.HBM)


def passed_along(block, axis, distance):
    count = lax.axis_size(axis)
    route = [((i - distance) % count, i) for i in range(count)]
    return lax.ppermute(block, axis, route)


def across(slot, strips, fine):
    if strips != 4 or slot not in (1, 2):
        return slot
    return slot + fine % 2 * (3 - 2 * slot)


def lane_of(shape):
    return lax.broadcasted_iota(jnp.int32, shape, 1)


def row_of(shape):
    return lax.broadcasted_iota(jnp.int32, shape, 0)


def swapped(tile):
    return pltpu.roll(tile, HALF, 1)


def low_pair(even, odd):
    return jnp.where(lane_of(even.shape) < HALF, even, swapped(odd))


def high_pair(even, odd):
    return jnp.where(lane_of(even.shape) < HALF, swapped(even), odd)


def split(value):
    high = value.astype(jnp.bfloat16)
    return high, (value - high.astype(jnp.float32)).astype(jnp.bfloat16)


def beside(value):
    return jnp.concatenate(split(value), axis=1)


def filled(value, rows):
    if value.shape[0] == rows:
        return value
    return jnp.concatenate([value, jnp.zeros((rows - value.shape[0], value.shape[1]), value.dtype)], axis=0)


def stacked(value):
    both = filled(jnp.concatenate(split(value), axis=1), value.shape[1])
    return jnp.concatenate([both, both], axis=0)


def times(left, right):
    out = lax.dot_general(left, right, NN, preferred_element_type=jnp.float32)
    half = out.shape[1] // 2
    return out[:, :half] + out[:, half:]


def squared(value, columns):
    high, low = split(value)
    both = jnp.concatenate([high, low], axis=0)
    wide = jnp.concatenate([filled(high, columns), filled(low, columns)], axis=0)
    out = lax.dot_general(both, wide, NT, preferred_element_type=jnp.float32)
    out = out[:, :columns] + out[:, columns:]
    half = out.shape[0] // 2
    return out[:half] + out[half:]


def applied_to(left, value):
    columns = left.shape[1]
    wide = beside(left)
    high, low = (filled(part, columns) for part in split(value))
    dot = functools.partial(
        lax.dot_general, dimension_numbers=NN, preferred_element_type=jnp.float32
    )
    return dot(wide, jnp.concatenate([high, high], axis=0)) + dot(wide[:, :columns], low)


BACK_ROWS = 3 * TILE + 1


def turn_kernel(mem, later, *refs):
    sources, refs = refs[: 6 + later], refs[6 + later :]
    pair_ref, single_ref, edge_ref, live_ref = refs[:4]
    targets, sems = refs[4 + later : -1] + refs[4 : 4 + later], refs[-1]
    copies = [
        pltpu.make_async_copy(source, target, sems.at[i])
        for i, (source, target) in enumerate(zip(sources, targets))
    ]
    for copy in copies:
        copy.start()
    h_ref, u_ref, v_ref, zonal_ref, merid_ref, count_ref = targets[:6]
    tiles = h_ref.shape[0] // mem
    columns = tiles * LANES
    zero = jnp.zeros((TILE, LANES), jnp.float32)
    for ref in (pair_ref, single_ref):
        ref[0:TILE, :] = zero
        ref[columns : columns + TILE, :] = zero
    for copy in copies[:5]:
        copy.wait()
    for t in range(tiles):
        rows = pl.ds(t, mem, stride=tiles)
        lanes = slice(t * LANES, (t + 1) * LANES)
        pair = jnp.concatenate([h_ref[rows, :], u_ref[rows, :]], axis=0)
        zonal = jnp.broadcast_to(zonal_ref[:, lanes], (mem // 2, LANES))
        merid = jnp.broadcast_to(merid_ref[:, lanes], (mem // 2, LANES))
        single = jnp.concatenate([v_ref[rows, :], zonal, merid], axis=0)
        place = slice(STEPS + t * LANES, STEPS + (t + 1) * LANES)
        pair_ref[place, :] = pair.T
        single_ref[place, :] = single.T
    early = row_of((TILE, LANES)) < STEPS
    for i, ref in enumerate((pair_ref, single_ref)):
        edge_ref[i] = jnp.where(early, ref[columns : columns + TILE, :], ref[0:TILE, :])
    for copy in copies[5:]:
        copy.wait()
    for q in range(REG_DEV):
        live_ref[q] = jnp.full(live_ref.shape[1:], count_ref[q], jnp.int32)


def blocks_kernel(groups, strips, width, pair_ref, single_ref, west_ref, east_ref, *refs):
    send_refs = refs[-strips:]
    me, fine = lax.axis_index("region"), lax.axis_index("fine")
    shape = (TILE, LANES)
    early = row_of(shape) < STEPS
    part = lane_of(shape) % (HALF // 2)
    span = 3 * TILE
    for s, send_ref in enumerate(send_refs):
        owner = me ^ across(s, strips, fine)
        first, last = early & (owner == 0), ~early & (owner == strips - 1)
        courant = jnp.zeros(shape, jnp.float32)
        for p in range(groups // 2):
            for j in range(3):
                pairs, singles = [], []
                for group in (2 * p, 2 * p + 1):
                    start = pl.multiple_of(width * (group * strips + owner) + TILE * j, TILE)
                    pair = pair_ref[pl.ds(start, TILE), :]
                    single = single_ref[pl.ds(start, TILE), :]
                    if group == 0 and j == 0:
                        pair = jnp.where(first, west_ref[0], pair)
                        single = jnp.where(first, west_ref[1], single)
                    if group == groups - 1 and j == 2:
                        pair = jnp.where(last, east_ref[0], pair)
                        single = jnp.where(last, east_ref[1], single)
                    pairs.append(pair)
                    singles.append(single)
                    courant = jnp.where(part == 3 * group + j, single, courant)
                place = 3 * span * p + TILE * j
                send_ref[place : place + TILE, :] = low_pair(*pairs)
                send_ref[place + span : place + span + TILE, :] = high_pair(*pairs)
                send_ref[place + 2 * span : place + 2 * span + TILE, :] = low_pair(*singles)
        place = 3 * span * (groups // 2)
        send_ref[place : place + TILE, :] = courant


def forecast_kernel(groups, strips, width, *refs):
    got_refs, refs = refs[:strips], refs[strips:]
    send_refs, (got_ref, turned_ref) = refs[:groups], refs[groups:]
    span = width + 2 * STEPS
    per_region = strips // REG_DEV
    cells = per_region * width
    me, fine = lax.axis_index("region"), lax.axis_index("fine")
    for s, ref in enumerate(got_refs):
        got_ref[me ^ across(s, strips, fine)] = ref[...]
    low = lane_of((TILE, LANES)) < HALF
    tail = 3 * span * (groups // 2)
    for p in range(groups // 2):

        def field(r, i):
            return got_ref[r, 3 * span * p + span * i : 3 * span * p + span * (i + 1), :]

        def courant(r, first):
            mixed = got_ref[r, tail : tail + TILE, :]
            parts = []
            for j in range(3):
                even, odd = first + 6 * p + j, first + 6 * p + 3 + j
                parts.append(
                    jnp.where(
                        low,
                        jnp.broadcast_to(mixed[:, even : even + 1], (TILE, LANES)),
                        jnp.broadcast_to(mixed[:, odd : odd + 1], (TILE, LANES)),
                    )
                )
            return jnp.concatenate(parts, axis=0)

        h = [field(r, 0) for r in range(strips)]
        u = [field(r, 1) for r in range(strips)]
        v = [field(r, 2) for r in range(strips)]
        zonal = [courant(r, HALF) for r in range(strips)]
        merid = [courant(r, HALF + HALF // 2) for r in range(strips)]
        for _ in range(STEPS):
            flux_v = [merid[r] * v[r] for r in range(strips)]
            for r in range(strips):
                flux_u = zonal[r] * u[r]
                south = flux_v[r - 1] if r else jnp.zeros_like(flux_u)
                h[r] = h[r] - (flux_u - pltpu.roll(flux_u, 1, 0) + flux_v[r] - south)
            for r in range(strips):
                north = h[r + 1] if r + 1 < strips else jnp.zeros_like(h[r])
                u[r] = u[r] - (pltpu.roll(h[r], span - 1, 0) - h[r])
                v[r] = v[r] - (north - h[r])
        for i, state in enumerate((h, u, v)):
            inner = [pltpu.roll(state[r], span - STEPS, 0)[:width] for r in range(strips)]
            for s in range(per_region):
                lower, upper = inner[s], inner[per_region + s]
                place = slice(i * cells + s * width, i * cells + (s + 1) * width)
                turned_ref[2 * p, place, :] = low_pair(lower, upper)
                turned_ref[2 * p + 1, place, :] = high_pair(lower, upper)
    mine = lax.axis_index("member")
    for s, ref in enumerate(send_refs):
        ref[...] = turned_ref[mine ^ s]


def collect(got_refs, all_ref, x_ref):
    mine = lax.axis_index("member")
    for s, ref in enumerate(got_refs):
        all_ref[mine ^ s] = ref[...]
    for p in range(len(got_refs) // 2):
        even, odd = all_ref[2 * p], all_ref[2 * p + 1]
        lanes = slice(p * LANES, (p + 1) * LANES)
        x_ref[0, :, lanes] = low_pair(even, odd)
        x_ref[1, :, lanes] = high_pair(even, odd)


def observe_kernel(live_ref, index_ref, weight_ref, value_ref, var_ref, info_ref, pull_ref):
    states, padded = info_ref.shape[1:]
    obs = index_ref.shape[2]
    for q in range(REG_DEV):
        state = row_of((states, obs))
        operator = jnp.zeros((states, obs), jnp.float32)
        for j in range(index_ref.shape[1]):
            hit = state == index_ref[q, j : j + 1, :]
            operator = operator + jnp.where(hit, weight_ref[q, j : j + 1, :], 0.0)
        live = lane_of((1, obs)) < live_ref[q, 0:1, 0:1]
        inverse = jnp.where(live, 1.0 / var_ref[q : q + 1, :], 0.0)
        scaled = operator * inverse
        info_ref[q] = lax.dot_general(
            scaled,
            filled(operator, padded),
            NT,
            precision=HIGHEST,
            preferred_element_type=jnp.float32,
        )
        pulled = jnp.sum(scaled * value_ref[q : q + 1, :], axis=1, keepdims=True)
        pull_ref[q] = jnp.broadcast_to(pulled, (states, LANES))


def analyse(members, x_ref, info_ref, pull_ref, out_ref):
    states, padded = info_ref.shape[1:]
    square = (states, padded)
    diagonal = row_of(square) == lane_of(square)
    identity = jnp.where(diagonal, 1.0, 0.0)
    regions = range(REG_DEV)
    scale = 1.0 / (members - 1)

    def as_row(column):
        return jnp.sum(jnp.where(diagonal, column, 0.0), axis=0, keepdims=True)

    def applied(matrix, row):
        return jnp.sum(matrix * row, axis=1, keepdims=True)

    x = [x_ref[q] for q in regions]
    means = [jnp.sum(x[q], axis=1, keepdims=True) / members for q in regions]
    spreads = [x[q] - means[q] for q in regions]
    covs = [squared(spreads[q], padded) for q in regions]
    gains = [times(beside(covs[q]), stacked(info_ref[q] * scale)) for q in regions]
    rights = [stacked(gains[q]) for q in regions]
    gains_2 = [times(beside(gains[q]), rights[q]) for q in regions]
    pulls, inverse_norms, iterates, inverses = [], [], [], []
    for q in regions:
        pulled = pull_ref[q][:, 0:1] - applied(info_ref[q], as_row(means[q]))
        pulls.append(jnp.sum(covs[q] * pulled, axis=0, keepdims=True))
        trace = jnp.sum(jnp.where(diagonal, gains_2[q] + 2.0 * gains[q], 0.0), keepdims=True)
        inverse_norms.append(lax.rsqrt(trace + members))
    for q in regions:
        norm = inverse_norms[q]
        first = (identity + gains[q]) * norm
        second = (identity + 2.0 * gains[q] + gains_2[q]) * (norm * norm)
        third = (second + times(beside(second), rights[q])) * norm
        inverses.append(1.5 * identity - 0.5 * first)
        iterates.append(2.25 * first - 1.5 * second + 0.25 * third)
    for _ in range(1, NEWTON - 1):
        rights = [stacked(iterates[q]) for q in regions]
        lefts = [
            jnp.concatenate([beside(iterates[q]), beside(inverses[q])], axis=0) for q in regions
        ]
        both = [times(lefts[q], rights[q]) for q in regions]
        seconds = [both[q][:states] for q in regions]
        thirds = [times(beside(seconds[q]), rights[q]) for q in regions]
        inverses = [1.5 * inverses[q] - 0.5 * both[q][states:] for q in regions]
        iterates = [
            2.25 * iterates[q] - 1.5 * seconds[q] + 0.25 * thirds[q] for q in regions
        ]
    increments = []
    for q in regions:
        moved = applied_to(inverses[q], spreads[q])
        twice = applied(inverses[q], as_row(applied(inverses[q], pulls[q])))
        factor = 1.5 * identity - 0.5 * iterates[q]
        twice = applied(factor, as_row(applied(factor, as_row(twice))))
        increment = twice * (inverse_norms[q] * scale)
        increments.append(increment)
        moved = applied_to(factor, moved * jnp.sqrt(inverse_norms[q]))
        out_ref[q] = moved + (means[q] + increment)
    return increments


def pack(groups, strips, width, ana_ref, increments, send_ref):
    per_region = strips // REG_DEV
    cells = per_region * width
    states = increments[0].shape[0]
    state = row_of((states, LANES))
    lane = lane_of((states, LANES))
    for r in range(strips):
        q, s = divmod(r, per_region)
        wanted = (lane // width) * cells + s * width + lane % width
        hit = (state == wanted) & (lane < 3 * width)
        row = jnp.sum(jnp.where(hit, increments[q], 0.0), axis=0, keepdims=True)
        for group in range(groups):
            block = group * strips + r
            lanes = slice((group // 2) * LANES, (group // 2 + 1) * LANES)
            pair = high_pair if group % 2 else low_pair
            for i in range(3):
                first = i * cells + s * width
                tile = pair(
                    ana_ref[q, first : first + TILE, lanes],
                    ana_ref[q, first + TILE : first + 2 * TILE, lanes],
                )
                send_ref[BACK_ROWS * block + TILE * i : BACK_ROWS * block + TILE * (i + 1), :] = tile
            send_ref[BACK_ROWS * (block + 1) - 1 : BACK_ROWS * (block + 1), :] = row


def region_kernel(groups, strips, width, *refs):
    got_refs, (info_ref, pull_ref, send_ref, all_ref, x_ref, ana_ref) = refs[:groups], refs[groups:]
    collect(got_refs, all_ref, x_ref)
    increments = analyse(x_ref.shape[2], x_ref, info_ref, pull_ref, ana_ref)
    pack(groups, strips, width, ana_ref, increments, send_ref)


def home_kernel(mem, strips, width, got_ref, ctrl_ref, *refs):
    targets, (h_ref, u_ref, v_ref, fine_ref, sems) = refs[:4], refs[4:]
    copies = [
        pltpu.make_async_copy(source, target, sems.at[i])
        for i, (source, target) in enumerate(zip((h_ref, u_ref, v_ref, fine_ref), targets))
    ]
    tiles = got_ref.shape[0] // BACK_ROWS * width // LANES
    per_tile = LANES // width
    for i, out_ref in enumerate((h_ref, u_ref, v_ref)):
        for t in range(0, tiles, 2):
            rows = []
            for k in range(per_tile):
                first = BACK_ROWS * (t * per_tile + k) + TILE * i
                even = got_ref[first : first + TILE, :]
                first += BACK_ROWS * per_tile
                odd = got_ref[first : first + TILE, :]
                rows += [low_pair(even, odd), high_pair(even, odd)]
            turned = jnp.concatenate(rows, axis=0).T
            out_ref[pl.ds(t, mem, stride=tiles), :] = turned[:mem]
            out_ref[pl.ds(t + 1, mem, stride=tiles), :] = turned[mem:]
        copies[i].start()
    mine = lax.axis_index("member") * strips
    per_fine = LANES // (2 * width)
    row = row_of((width, LANES))
    lane = lane_of((width, LANES))
    for t in range(ctrl_ref.shape[3] // LANES):
        rows = [
            got_ref[pl.ds(BACK_ROWS * (mine + t * per_fine + b) + BACK_ROWS - 1, 1), :]
            for b in range(per_fine)
        ]
        columns = [jnp.broadcast_to(r, (LANES, LANES)).T[:, 0:1] for r in rows]
        for i in range(3):
            total = jnp.zeros((1, LANES), jnp.float32)
            for b in range(per_fine):
                hit = ((lane // 2) % width == row) & (lane // (2 * width) == b)
                part = jnp.where(hit, columns[b][i * width : (i + 1) * width], 0.0)
                total = total + jnp.sum(part, axis=0, keepdims=True)
            lanes = slice(t * LANES, (t + 1) * LANES)
            for e in range(2):
                fine_ref[i, e, :, lanes] = ctrl_ref[i, e, :, lanes] + total
    copies[3].start()
    for copy in copies:
        copy.wait()


def collect_kernel(groups, *refs):
    collect(refs[:groups], refs[-1], refs[-2])


def pack_kernel(groups, strips, width, ana_ref, inc_ref, send_ref):
    pack(groups, strips, width, ana_ref, [inc_ref[q] for q in range(REG_DEV)], send_ref)


def analyse_in_members(x, obs_index, obs_weight, obs_value, obs_var, obs_count):
    states, members = x.shape[1:]
    mean_state = jnp.mean(x, axis=2, keepdims=True)
    spread = x - mean_state
    picks = (obs_index[:, :, :, None] == jnp.arange(states)).astype(jnp.float32)
    operator = jnp.sum(picks * obs_weight[:, :, :, None], axis=2)
    predicted = jnp.einsum("ros,rsk->rko", operator, x, precision=HIGHEST)
    mean_obs = jnp.mean(predicted, axis=1, keepdims=True)
    obs_spread = predicted - mean_obs
    active_obs = jnp.arange(obs_value.shape[1])[None, :] < obs_count[:, None]
    weighted = obs_spread * (active_obs.astype(jnp.float32) / obs_var)[:, None, :]
    gram_sum = jnp.einsum("rko,rjo->rkj", weighted, obs_spread, precision=HIGHEST)
    identity = jnp.eye(members, dtype=jnp.float32)
    scaled = identity + gram_sum / (members - 1)
    frobenius = jnp.sqrt(jnp.sum(scaled * scaled, axis=(1, 2), keepdims=True))
    iterate = scaled / frobenius
    inverse_root = jnp.broadcast_to(identity, scaled.shape)
    dot = functools.partial(jnp.einsum, "rij,rjk->rik", precision=HIGHEST)
    for _ in range(NEWTON):
        factor = 1.5 * identity - 0.5 * dot(inverse_root, iterate)
        iterate = dot(iterate, factor)
        inverse_root = dot(factor, inverse_root)
    transform = inverse_root / jnp.sqrt(frobenius)
    innovation = jnp.einsum(
        "rko,ro->rk", weighted, obs_value - mean_obs[:, 0], precision=HIGHEST
    )
    halfway = jnp.einsum("rkj,rj->rk", transform, innovation, precision=HIGHEST)
    mean_weights = jnp.einsum("rkj,rj->rk", transform, halfway, precision=HIGHEST) / (members - 1)
    increment = jnp.einsum("rk,rsk->rs", mean_weights, spread, precision=HIGHEST)[:, :, None]
    moved = jnp.einsum("rjk,rsj->rsk", transform, spread, precision=HIGHEST)
    return mean_state + increment + moved, increment


def call(kernel, out_shape, specs, scratch=(), cost=None, place=VMEM):
    many = isinstance(out_shape, tuple)
    return pl.pallas_call(
        kernel,
        out_shape=out_shape,
        in_specs=specs,
        out_specs=tuple(place for _ in out_shape) if many else place,
        scratch_shapes=scratch,
        cost_estimate=cost,
        compiler_params=pltpu.CompilerParams(vmem_limit_bytes=GRANT),
    )


def swapped_blocks(blocks, axis):
    count = len(blocks)
    if count <= 4:
        axes = (axis, "fine")
        fines = lax.axis_size("fine")
        moved = []
        for s in range(1, count):
            route = []
            for i in range(count):
                for fine in range(fines):
                    other = i ^ (across(s, count, fine) if axis == "region" else s)
                    route.append((i * fines + fine, other * fines + fine))
            moved.append(lax.ppermute(blocks[s], axes, route))
        return [kept(block) for block in [blocks[0], *moved]]
    order = lax.axis_index(axis) ^ jnp.arange(count)
    moved = lax.all_to_all(jnp.stack(blocks)[order], axis, split_axis=0, concat_axis=0, tiled=True)
    return [kept(block) for block in moved[order]]


def exchanged(blocks, axes, count):
    dense = blocks.reshape(count, -1, 1, LANES)
    return lax.all_to_all(dense, axes, split_axis=0, concat_axis=0, tiled=True).reshape(blocks.shape)


def f32(*shape):
    return jax.ShapeDtypeStruct(shape, jnp.float32)


def near(*shape):
    return pltpu.VMEM(shape, jnp.float32)


def far(array):
    return pltpu.with_memory_space_constraint(array, pltpu.HBM)


def kept(array):
    return pltpu.with_memory_space_constraint(array, pltpu.VMEM)


def shards(
    sample_surface_elevation,
    sample_zonal_current,
    sample_meridional_current,
    zonal_edge_layer_courant,
    meridional_edge_layer_courant,
    obs_index,
    obs_weight,
    obs_value,
    obs_var,
    obs_count,
    fine_ctrl,
):
    groups = lax.axis_size("member")
    strips = lax.axis_size("region")
    owners = ("member", "region")
    mem, rows, columns = sample_surface_elevation.shape
    count = groups * strips
    width = columns // count
    members = groups * mem
    assert rows == 1 and 2 * mem == LANES and width == 2 * TILE and STEPS * 2 == TILE
    assert columns % (2 * LANES) == 0 and strips % REG_DEV == 0 and REG_DEV == 2
    assert all(size > 1 and size & (size - 1) == 0 for size in (groups, strips))
    assert 3 * groups <= HALF // 2
    flat = (mem * columns // LANES, LANES)
    states = 3 * width * strips // REG_DEV
    small = states <= members
    later = [fine_ctrl]
    if small:
        later += [obs_index.transpose(0, 2, 1), obs_weight.transpose(0, 2, 1), obs_value, obs_var]
    pair, single, edge, live, ctrl, *seen = call(
        functools.partial(turn_kernel, mem, len(later)),
        (
            near(columns + TILE, LANES),
            near(columns + TILE, LANES),
            near(2, TILE, LANES),
            pltpu.VMEM((REG_DEV, TILE, LANES), jnp.int32),
            *(pltpu.VMEM(array.shape, array.dtype) for array in later),
        ),
        [HBM] * (6 + len(later)),
        scratch=[
            *[pltpu.VMEM(flat, jnp.float32)] * 3,
            *[pltpu.VMEM((1, columns), jnp.float32)] * 2,
            pltpu.SMEM((REG_DEV,), jnp.int32),
            pltpu.SemaphoreType.DMA((6 + len(later),)),
        ],
    )(
        far(sample_surface_elevation.reshape(flat)),
        far(sample_zonal_current.reshape(flat)),
        far(sample_meridional_current.reshape(flat)),
        far(zonal_edge_layer_courant),
        far(meridional_edge_layer_courant),
        far(obs_count),
        *(far(array) for array in later),
    )
    from_west = passed_along(edge, "fine", 1)
    from_east = from_west if lax.axis_size("fine") == 2 else passed_along(edge, "fine", -1)
    ahead = []
    if small:
        padded = -(-states // LANES) * LANES
        obs = obs_value.shape[1]
        info, pull = call(
            observe_kernel,
            (near(REG_DEV, states, padded), near(REG_DEV, states, LANES)),
            [VMEM] * 5,
            cost=pl.CostEstimate(
                flops=12 * REG_DEV * padded * padded * obs, bytes_accessed=1 << 20, transcendentals=0
            ),
        )(kept(live), *(kept(array) for array in seen))
        ahead = [kept(pull)]
    layout = (groups, strips, width)
    span = width + 2 * STEPS
    out = call(
        functools.partial(blocks_kernel, *layout),
        tuple([near(3 * span * (groups // 2) + TILE, LANES)] * strips),
        [VMEM] * (4 + len(ahead)),
    )(kept(pair), kept(single), kept(from_west), kept(from_east), *ahead)
    got = swapped_blocks(out, "region")
    turned = call(
        functools.partial(forecast_kernel, *layout),
        tuple([near(states, LANES)] * groups),
        [VMEM] * strips,
        scratch=[
            pltpu.VMEM((strips, *out[0].shape), jnp.float32),
            pltpu.VMEM((groups, states, LANES), jnp.float32),
        ],
    )(*got)
    got = swapped_blocks(turned, "member")
    back_shape = near(count * BACK_ROWS, LANES)
    gathered = pltpu.VMEM((groups, states, LANES), jnp.float32)
    if small:
        back = call(
            functools.partial(region_kernel, *layout),
            back_shape,
            [VMEM] * (groups + 2),
            scratch=[
                gathered,
                pltpu.VMEM((REG_DEV, states, members), jnp.float32),
                pltpu.VMEM((REG_DEV, states, members), jnp.float32),
            ],
        )(*got, kept(info), kept(pull))
    else:
        x = call(
            functools.partial(collect_kernel, groups),
            f32(REG_DEV, states, members),
            [VMEM] * groups,
            scratch=[gathered],
        )(*got)
        analysis, increment = analyse_in_members(
            x, obs_index, obs_weight, obs_value, obs_var, obs_count
        )
        back = call(
            functools.partial(pack_kernel, *layout), back_shape, [VMEM] * 2
        )(analysis, increment)
    home = exchanged(back, owners, count)
    ana_h, ana_u, ana_v, fine_out = call(
        functools.partial(home_kernel, mem, strips, width),
        (f32(*flat), f32(*flat), f32(*flat), f32(*fine_ctrl.shape)),
        [VMEM, VMEM],
        scratch=[
            *[pltpu.VMEM(flat, jnp.float32)] * 3,
            pltpu.VMEM(fine_ctrl.shape, jnp.float32),
            pltpu.SemaphoreType.DMA((4,)),
        ],
        place=HBM,
    )(kept(home), kept(ctrl))
    shape = (mem, rows, columns)
    return (ana_h.reshape(shape), ana_u.reshape(shape), ana_v.reshape(shape), fine_out)


def solution(mesh):
    strip = P("member", "region", "fine")
    owner = ("member", "region", "fine")
    fine = P(None, "region", "fine", "member")
    return jax.shard_map(
        shards,
        mesh=mesh,
        in_specs=(
            strip,
            strip,
            strip,
            P("region", "fine"),
            P("region", "fine"),
            P(owner, None, None),
            P(owner, None, None),
            P(owner, None),
            P(owner, None),
            P(owner),
            fine,
        ),
        out_specs=(strip, strip, strip, fine),
        check_vma=False,
    )
```

```python
import functools

import jax
import jax.numpy as jnp
from jax import lax
from jax.experimental import pallas as pl
from jax.experimental.pallas import tpu as pltpu
from jax.sharding import PartitionSpec as P


REG_DEV = 2
STEPS = 4
NEWTON = 8
LANES = 128
TILE = 8
HALF = LANES // 2
GRANT = 32 << 20


HIGHEST = lax.Precision.HIGHEST
NT = (((1,), (1,)), ((), ()))
NN = (((1,), (0,)), ((), ()))
VMEM = pl.BlockSpec(memory_space=pltpu.VMEM)
SMEM = pl.BlockSpec(memory_space=pltpu.SMEM)
HBM = pl.BlockSpec(memory_space=pltpu.HBM)


def passed_along(block, axis, distance):
    count = lax.axis_size(axis)
    route = [((i - distance) % count, i) for i in range(count)]
    return lax.ppermute(block, axis, route)


def lane_of(shape):
    return lax.broadcasted_iota(jnp.int32, shape, 1)


def row_of(shape):
    return lax.broadcasted_iota(jnp.int32, shape, 0)


def swapped(tile):
    return pltpu.roll(tile, HALF, 1)


def low_pair(even, odd):
    return jnp.where(lane_of(even.shape) < HALF, even, swapped(odd))


def high_pair(even, odd):
    return jnp.where(lane_of(even.shape) < HALF, swapped(even), odd)


def split(value):
    high = value.astype(jnp.bfloat16)
    return high, (value - high.astype(jnp.float32)).astype(jnp.bfloat16)


def beside(value):
    return jnp.concatenate(split(value), axis=1)


def filled(value, rows):
    if value.shape[0] == rows:
        return value
    return jnp.concatenate([value, jnp.zeros((rows - value.shape[0], value.shape[1]), value.dtype)], axis=0)


def stacked(value):
    both = filled(jnp.concatenate(split(value), axis=1), value.shape[1])
    return jnp.concatenate([both, both], axis=0)


def times(left, right):
    out = lax.dot_general(left, right, NN, preferred_element_type=jnp.float32)
    half = out.shape[1] // 2
    return out[:, :half] + out[:, half:]


def squared(value, columns):
    high, low = split(value)
    both = jnp.concatenate([high, low], axis=0)
    wide = jnp.concatenate([filled(high, columns), filled(low, columns)], axis=0)
    out = lax.dot_general(both, wide, NT, preferred_element_type=jnp.float32)
    out = out[:, :columns] + out[:, columns:]
    half = out.shape[0] // 2
    return out[:half] + out[half:]


def applied_to(left, value):
    columns = left.shape[1]
    wide = beside(left)
    high, low = (filled(part, columns) for part in split(value))
    dot = functools.partial(
        lax.dot_general, dimension_numbers=NN, preferred_element_type=jnp.float32
    )
    return dot(wide, jnp.concatenate([high, high], axis=0)) + dot(wide[:, :columns], low)


BACK_ROWS = 3 * TILE + 1


def turn_kernel(mem, later, *refs):
    sources, refs = refs[: 6 + later], refs[6 + later :]
    pair_ref, single_ref, edge_ref, live_ref = refs[:4]
    targets, sems = refs[4 + later : -1] + refs[4 : 4 + later], refs[-1]
    copies = [
        pltpu.make_async_copy(source, target, sems.at[i])
        for i, (source, target) in enumerate(zip(sources, targets))
    ]
    for copy in copies:
        copy.start()
    h_ref, u_ref, v_ref, zonal_ref, merid_ref, count_ref = targets[:6]
    tiles = h_ref.shape[0] // mem
    columns = tiles * LANES
    zero = jnp.zeros((TILE, LANES), jnp.float32)
    for ref in (pair_ref, single_ref):
        ref[0:TILE, :] = zero
        ref[columns : columns + TILE, :] = zero
    for copy in copies[:5]:
        copy.wait()
    for t in range(tiles):
        rows = pl.ds(t, mem, stride=tiles)
        lanes = slice(t * LANES, (t + 1) * LANES)
        pair = jnp.concatenate([h_ref[rows, :], u_ref[rows, :]], axis=0)
        zonal = jnp.broadcast_to(zonal_ref[:, lanes], (mem // 2, LANES))
        merid = jnp.broadcast_to(merid_ref[:, lanes], (mem // 2, LANES))
        single = jnp.concatenate([v_ref[rows, :], zonal, merid], axis=0)
        place = slice(STEPS + t * LANES, STEPS + (t + 1) * LANES)
        pair_ref[place, :] = pair.T
        single_ref[place, :] = single.T
    early = row_of((TILE, LANES)) < STEPS
    for i, ref in enumerate((pair_ref, single_ref)):
        edge_ref[i] = jnp.where(early, ref[columns : columns + TILE, :], ref[0:TILE, :])
    for copy in copies[5:]:
        copy.wait()
    for q in range(REG_DEV):
        live_ref[q] = jnp.full(live_ref.shape[1:], count_ref[q], jnp.int32)


def blocks_kernel(groups, strips, width, pair_ref, single_ref, west_ref, east_ref, *refs):
    send_refs = refs[-strips:]
    me = lax.axis_index("region")
    shape = (TILE, LANES)
    early = row_of(shape) < STEPS
    part = lane_of(shape) % (HALF // 2)
    span = 3 * TILE
    for s, send_ref in enumerate(send_refs):
        owner = me ^ s
        first, last = early & (owner == 0), ~early & (owner == strips - 1)
        courant = jnp.zeros(shape, jnp.float32)
        for p in range(groups // 2):
            for j in range(3):
                pairs, singles = [], []
                for group in (2 * p, 2 * p + 1):
                    start = pl.multiple_of(width * (group * strips + owner) + TILE * j, TILE)
                    pair = pair_ref[pl.ds(start, TILE), :]
                    single = single_ref[pl.ds(start, TILE), :]
                    if group == 0 and j == 0:
                        pair = jnp.where(first, west_ref[0], pair)
                        single = jnp.where(first, west_ref[1], single)
                    if group == groups - 1 and j == 2:
                        pair = jnp.where(last, east_ref[0], pair)
                        single = jnp.where(last, east_ref[1], single)
                    pairs.append(pair)
                    singles.append(single)
                    courant = jnp.where(part == 3 * group + j, single, courant)
                place = 3 * span * p + TILE * j
                send_ref[place : place + TILE, :] = low_pair(*pairs)
                send_ref[place + span : place + span + TILE, :] = high_pair(*pairs)
                send_ref[place + 2 * span : place + 2 * span + TILE, :] = low_pair(*singles)
        place = 3 * span * (groups // 2)
        send_ref[place : place + TILE, :] = courant


def forecast_kernel(groups, strips, width, *refs):
    got_refs, refs = refs[:strips], refs[strips:]
    send_refs, (got_ref, turned_ref) = refs[:groups], refs[groups:]
    span = width + 2 * STEPS
    per_region = strips // REG_DEV
    cells = per_region * width
    me = lax.axis_index("region")
    for s, ref in enumerate(got_refs):
        got_ref[me ^ s] = ref[...]
    low = lane_of((TILE, LANES)) < HALF
    tail = 3 * span * (groups // 2)
    for p in range(groups // 2):

        def field(r, i):
            return got_ref[r, 3 * span * p + span * i : 3 * span * p + span * (i + 1), :]

        def courant(r, first):
            mixed = got_ref[r, tail : tail + TILE, :]
            parts = []
            for j in range(3):
                even, odd = first + 6 * p + j, first + 6 * p + 3 + j
                parts.append(jnp.take_along_axis(mixed, jnp.where(low, even, odd), axis=1))
            return jnp.concatenate(parts, axis=0)

        h = [field(r, 0) for r in range(strips)]
        u = [field(r, 1) for r in range(strips)]
        v = [field(r, 2) for r in range(strips)]
        zonal = [courant(r, HALF) for r in range(strips)]
        merid = [courant(r, HALF + HALF // 2) for r in range(strips)]
        for _ in range(STEPS):
            flux_v = [merid[r] * v[r] for r in range(strips)]
            for r in range(strips):
                flux_u = zonal[r] * u[r]
                south = flux_v[r - 1] if r else jnp.zeros_like(flux_u)
                h[r] = h[r] - (flux_u - pltpu.roll(flux_u, 1, 0) + flux_v[r] - south)
            for r in range(strips):
                north = h[r + 1] if r + 1 < strips else jnp.zeros_like(h[r])
                u[r] = u[r] - (pltpu.roll(h[r], span - 1, 0) - h[r])
                v[r] = v[r] - (north - h[r])
        for i, state in enumerate((h, u, v)):
            inner = [pltpu.roll(state[r], span - STEPS, 0)[:width] for r in range(strips)]
            for s in range(per_region):
                lower, upper = inner[s], inner[per_region + s]
                place = slice(i * cells + s * width, i * cells + (s + 1) * width)
                turned_ref[2 * p, place, :] = low_pair(lower, upper)
                turned_ref[2 * p + 1, place, :] = high_pair(lower, upper)
    mine = lax.axis_index("member")
    for s, ref in enumerate(send_refs):
        ref[...] = turned_ref[mine ^ s]


def regions_of(even, odd):
    return [low_pair(even, odd), high_pair(even, odd)]


def early_kernel(even_ref, odd_ref, shift_ref, cov_ref):
    for q, tile in enumerate(regions_of(even_ref[...], odd_ref[...])):
        shift = jnp.sum(tile, axis=1, keepdims=True) / LANES
        shift_ref[q] = jnp.broadcast_to(shift, shift_ref.shape[1:])
        cov_ref[q] = squared(tile - shift, cov_ref.shape[2])


def collect(got_refs, all_ref, x_ref):
    mine = lax.axis_index("member")
    for s, ref in enumerate(got_refs):
        all_ref[mine ^ s] = ref[...]
    for p in range(len(got_refs) // 2):
        even, odd = all_ref[2 * p], all_ref[2 * p + 1]
        lanes = slice(p * LANES, (p + 1) * LANES)
        for q, tile in enumerate(regions_of(even, odd)):
            x_ref[q, :, lanes] = tile


def observe_kernel(live_ref, index_ref, weight_ref, value_ref, var_ref, info_ref, pull_ref):
    states, padded = info_ref.shape[1:]
    obs = index_ref.shape[2]
    for q in range(REG_DEV):
        state = row_of((states, obs))
        operator = jnp.zeros((states, obs), jnp.float32)
        for j in range(index_ref.shape[1]):
            hit = state == index_ref[q, j : j + 1, :]
            operator = operator + jnp.where(hit, weight_ref[q, j : j + 1, :], 0.0)
        live = lane_of((1, obs)) < live_ref[q, 0:1, 0:1]
        inverse = jnp.where(live, 1.0 / var_ref[q : q + 1, :], 0.0)
        scaled = operator * inverse
        info_ref[q] = lax.dot_general(
            scaled,
            filled(operator, padded),
            NT,
            precision=HIGHEST,
            preferred_element_type=jnp.float32,
        )
        pulled = jnp.sum(scaled * value_ref[q : q + 1, :], axis=1, keepdims=True)
        pull_ref[q] = jnp.broadcast_to(pulled, (states, LANES))


def analyse(members, rest, fill, x_ref, shift_ref, cov_ref, info_ref, pull_ref, out_ref):
    states, padded = info_ref.shape[1:]
    square = (states, padded)
    diagonal = row_of(square) == lane_of(square)
    identity = jnp.where(diagonal, 1.0, 0.0)
    regions = range(REG_DEV)
    scale = 1.0 / (members - 1)

    def as_row(column):
        return jnp.sum(jnp.where(diagonal, column, 0.0), axis=0, keepdims=True)

    def applied(matrix, row):
        return jnp.sum(matrix * row, axis=1, keepdims=True)

    shifts = [shift_ref[q][:, 0:1] for q in regions]
    later = [rest[q] - shifts[q] for q in regions]
    covs = [cov_ref[q] + squared(later[q], padded) for q in regions]
    moves = [jnp.sum(later[q], axis=1, keepdims=True) / members for q in regions]
    covs = [covs[q] - members * (moves[q] * as_row(moves[q])) for q in regions]
    means = [shifts[q] + moves[q] for q in regions]
    gains = [times(beside(covs[q]), stacked(info_ref[q] * scale)) for q in regions]
    rights = [stacked(gains[q]) for q in regions]
    gains_2 = [times(beside(gains[q]), rights[q]) for q in regions]
    fill()
    pulls, inverse_norms, iterates, inverses = [], [], [], []
    for q in regions:
        pulled = pull_ref[q][:, 0:1] - applied(info_ref[q], as_row(means[q]))
        pulls.append(jnp.sum(covs[q] * pulled, axis=0, keepdims=True))
        trace = jnp.sum(jnp.where(diagonal, gains_2[q] + 2.0 * gains[q], 0.0), keepdims=True)
        inverse_norms.append(lax.rsqrt(trace + members))
    for q in regions:
        norm = inverse_norms[q]
        first = (identity + gains[q]) * norm
        second = (identity + 2.0 * gains[q] + gains_2[q]) * (norm * norm)
        third = (second + times(beside(second), rights[q])) * norm
        inverses.append(1.5 * identity - 0.5 * first)
        iterates.append(2.25 * first - 1.5 * second + 0.25 * third)
    for _ in range(1, NEWTON - 1):
        rights = [stacked(iterates[q]) for q in regions]
        seconds = [times(beside(iterates[q]), rights[q]) for q in regions]
        inverses = [
            1.5 * inverses[q] - 0.5 * times(beside(inverses[q]), rights[q]) for q in regions
        ]
        thirds = [times(beside(seconds[q]), rights[q]) for q in regions]
        iterates = [
            2.25 * iterates[q] - 1.5 * seconds[q] + 0.25 * thirds[q] for q in regions
        ]
    increments = []
    for q in regions:
        moved = applied_to(inverses[q], x_ref[q] - means[q])
        twice = applied(inverses[q], as_row(applied(inverses[q], pulls[q])))
        factor = 1.5 * identity - 0.5 * iterates[q]
        twice = applied(factor, as_row(applied(factor, as_row(twice))))
        increment = twice * (inverse_norms[q] * scale)
        increments.append(increment)
        moved = applied_to(factor, moved * jnp.sqrt(inverse_norms[q]))
        out_ref[q] = moved + (means[q] + increment)
    return increments


def pack(groups, strips, width, ana_ref, increments, send_ref):
    per_region = strips // REG_DEV
    cells = per_region * width
    states = increments[0].shape[0]
    state = row_of((states, LANES))
    lane = lane_of((states, LANES))
    for r in range(strips):
        q, s = divmod(r, per_region)
        wanted = (lane // width) * cells + s * width + lane % width
        hit = (state == wanted) & (lane < 3 * width)
        row = jnp.sum(jnp.where(hit, increments[q], 0.0), axis=0, keepdims=True)
        for group in range(groups):
            block = group * strips + r
            lanes = slice((group // 2) * LANES, (group // 2 + 1) * LANES)
            pair = high_pair if group % 2 else low_pair
            for i in range(3):
                first = i * cells + s * width
                tile = pair(
                    ana_ref[q, first : first + TILE, lanes],
                    ana_ref[q, first + TILE : first + 2 * TILE, lanes],
                )
                send_ref[BACK_ROWS * block + TILE * i : BACK_ROWS * block + TILE * (i + 1), :] = tile
            send_ref[BACK_ROWS * (block + 1) - 1 : BACK_ROWS * (block + 1), :] = row


def region_kernel(groups, strips, width, *refs):
    got_refs, refs = refs[:groups], refs[groups:]
    shift_ref, cov_ref, info_ref, pull_ref, send_ref, all_ref, x_ref, ana_ref = refs
    pairs = [
        regions_of(got_refs[s][...], got_refs[s - 1][...]) for s in range(groups - 2, 0, -2)
    ]
    rest = [jnp.concatenate([pair[q] for pair in pairs], axis=1) for q in range(REG_DEV)]
    fill = functools.partial(collect, got_refs, all_ref, x_ref)
    increments = analyse(
        x_ref.shape[2], rest, fill, x_ref, shift_ref, cov_ref, info_ref, pull_ref, ana_ref
    )
    pack(groups, strips, width, ana_ref, increments, send_ref)


def home_kernel(mem, strips, width, got_ref, ctrl_ref, *refs):
    targets, (h_ref, u_ref, v_ref, fine_ref, sems) = refs[:4], refs[4:]
    copies = [
        pltpu.make_async_copy(source, target, sems.at[i])
        for i, (source, target) in enumerate(zip((h_ref, u_ref, v_ref, fine_ref), targets))
    ]
    tiles = got_ref.shape[0] // BACK_ROWS * width // LANES
    per_tile = LANES // width
    for i, out_ref in enumerate((h_ref, u_ref, v_ref)):
        for t in range(0, tiles, 2):
            rows = []
            for k in range(per_tile):
                first = BACK_ROWS * (t * per_tile + k) + TILE * i
                even = got_ref[first : first + TILE, :]
                first += BACK_ROWS * per_tile
                odd = got_ref[first : first + TILE, :]
                rows += [low_pair(even, odd), high_pair(even, odd)]
            turned = jnp.concatenate(rows, axis=0).T
            out_ref[pl.ds(t, mem, stride=tiles), :] = turned[:mem]
            out_ref[pl.ds(t + 1, mem, stride=tiles), :] = turned[mem:]
        copies[i].start()
    mine = lax.axis_index("member") * strips
    per_fine = LANES // (2 * width)
    row = row_of((width, LANES))
    lane = lane_of((width, LANES))
    for t in range(ctrl_ref.shape[3] // LANES):
        rows = [
            got_ref[pl.ds(BACK_ROWS * (mine + t * per_fine + b) + BACK_ROWS - 1, 1), :]
            for b in range(per_fine)
        ]
        columns = [jnp.broadcast_to(r, (LANES, LANES)).T[:, 0:1] for r in rows]
        for i in range(3):
            total = jnp.zeros((1, LANES), jnp.float32)
            for b in range(per_fine):
                hit = ((lane // 2) % width == row) & (lane // (2 * width) == b)
                part = jnp.where(hit, columns[b][i * width : (i + 1) * width], 0.0)
                total = total + jnp.sum(part, axis=0, keepdims=True)
            lanes = slice(t * LANES, (t + 1) * LANES)
            for e in range(2):
                fine_ref[i, e, :, lanes] = ctrl_ref[i, e, :, lanes] + total
    copies[3].start()
    for copy in copies:
        copy.wait()


def collect_kernel(groups, *refs):
    collect(refs[:groups], refs[-1], refs[-2])


def pack_kernel(groups, strips, width, ana_ref, inc_ref, send_ref):
    pack(groups, strips, width, ana_ref, [inc_ref[q] for q in range(REG_DEV)], send_ref)


def analyse_in_members(x, obs_index, obs_weight, obs_value, obs_var, obs_count):
    states, members = x.shape[1:]
    mean_state = jnp.mean(x, axis=2, keepdims=True)
    spread = x - mean_state
    picks = (obs_index[:, :, :, None] == jnp.arange(states)).astype(jnp.float32)
    operator = jnp.sum(picks * obs_weight[:, :, :, None], axis=2)
    predicted = jnp.einsum("ros,rsk->rko", operator, x, precision=HIGHEST)
    mean_obs = jnp.mean(predicted, axis=1, keepdims=True)
    obs_spread = predicted - mean_obs
    active_obs = jnp.arange(obs_value.shape[1])[None, :] < obs_count[:, None]
    weighted = obs_spread * (active_obs.astype(jnp.float32) / obs_var)[:, None, :]
    gram_sum = jnp.einsum("rko,rjo->rkj", weighted, obs_spread, precision=HIGHEST)
    identity = jnp.eye(members, dtype=jnp.float32)
    scaled = identity + gram_sum / (members - 1)
    frobenius = jnp.sqrt(jnp.sum(scaled * scaled, axis=(1, 2), keepdims=True))
    iterate = scaled / frobenius
    inverse_root = jnp.broadcast_to(identity, scaled.shape)
    dot = functools.partial(jnp.einsum, "rij,rjk->rik", precision=HIGHEST)
    for _ in range(NEWTON):
        factor = 1.5 * identity - 0.5 * dot(inverse_root, iterate)
        iterate = dot(iterate, factor)
        inverse_root = dot(factor, inverse_root)
    transform = inverse_root / jnp.sqrt(frobenius)
    innovation = jnp.einsum(
        "rko,ro->rk", weighted, obs_value - mean_obs[:, 0], precision=HIGHEST
    )
    halfway = jnp.einsum("rkj,rj->rk", transform, innovation, precision=HIGHEST)
    mean_weights = jnp.einsum("rkj,rj->rk", transform, halfway, precision=HIGHEST) / (members - 1)
    increment = jnp.einsum("rk,rsk->rs", mean_weights, spread, precision=HIGHEST)[:, :, None]
    moved = jnp.einsum("rjk,rsj->rsk", transform, spread, precision=HIGHEST)
    return mean_state + increment + moved, increment


def call(kernel, out_shape, specs, scratch=(), cost=None, place=VMEM):
    many = isinstance(out_shape, tuple)
    return pl.pallas_call(
        kernel,
        out_shape=out_shape,
        in_specs=specs,
        out_specs=tuple(place for _ in out_shape) if many else place,
        scratch_shapes=scratch,
        cost_estimate=cost,
        compiler_params=pltpu.CompilerParams(vmem_limit_bytes=GRANT),
    )


def swapped_blocks(blocks, axis):
    count = len(blocks)
    if count <= 4:
        routes = [[(i, i ^ s) for i in range(count)] for s in range(count)]
        moved = []
        for s in range(1, count):
            moved.append(lax.ppermute(blocks[s], axis, routes[s]))
        return [kept(block) for block in [blocks[0], *moved]]
    order = lax.axis_index(axis) ^ jnp.arange(count)
    moved = lax.all_to_all(jnp.stack(blocks)[order], axis, split_axis=0, concat_axis=0, tiled=True)
    return [kept(block) for block in moved[order]]


def exchanged(blocks, axes, count):
    dense = blocks.reshape(count, -1, 1, LANES)
    return lax.all_to_all(dense, axes, split_axis=0, concat_axis=0, tiled=True).reshape(blocks.shape)


def f32(*shape):
    return jax.ShapeDtypeStruct(shape, jnp.float32)


def near(*shape):
    return pltpu.VMEM(shape, jnp.float32)


def far(array):
    return pltpu.with_memory_space_constraint(array, pltpu.HBM)


def kept(array):
    return pltpu.with_memory_space_constraint(array, pltpu.VMEM)


def shards(
    sample_surface_elevation,
    sample_zonal_current,
    sample_meridional_current,
    zonal_edge_layer_courant,
    meridional_edge_layer_courant,
    obs_index,
    obs_weight,
    obs_value,
    obs_var,
    obs_count,
    fine_ctrl,
):
    groups = lax.axis_size("member")
    strips = lax.axis_size("region")
    owners = ("member", "region")
    mem, rows, columns = sample_surface_elevation.shape
    count = groups * strips
    width = columns // count
    members = groups * mem
    assert rows == 1 and 2 * mem == LANES and width == 2 * TILE and STEPS * 2 == TILE
    assert columns % (2 * LANES) == 0 and strips % REG_DEV == 0 and REG_DEV == 2
    assert all(size > 1 and size & (size - 1) == 0 for size in (groups, strips))
    assert 3 * groups <= HALF // 2
    flat = (mem * columns // LANES, LANES)
    states = 3 * width * strips // REG_DEV
    small = states <= members and groups > 2
    later = [fine_ctrl]
    if small:
        later += [obs_index.transpose(0, 2, 1), obs_weight.transpose(0, 2, 1), obs_value, obs_var]
    pair, single, edge, live, ctrl, *seen = call(
        functools.partial(turn_kernel, mem, len(later)),
        (
            near(columns + TILE, LANES),
            near(columns + TILE, LANES),
            near(2, TILE, LANES),
            pltpu.VMEM((REG_DEV, TILE, LANES), jnp.int32),
            *(pltpu.VMEM(array.shape, array.dtype) for array in later),
        ),
        [HBM] * (6 + len(later)),
        scratch=[
            *[pltpu.VMEM(flat, jnp.float32)] * 3,
            *[pltpu.VMEM((1, columns), jnp.float32)] * 2,
            pltpu.SMEM((REG_DEV,), jnp.int32),
            pltpu.SemaphoreType.DMA((6 + len(later),)),
        ],
    )(
        far(sample_surface_elevation.reshape(flat)),
        far(sample_zonal_current.reshape(flat)),
        far(sample_meridional_current.reshape(flat)),
        far(zonal_edge_layer_courant),
        far(meridional_edge_layer_courant),
        far(obs_count),
        *(far(array) for array in later),
    )
    from_west = passed_along(edge, "fine", 1)
    from_east = from_west if lax.axis_size("fine") == 2 else passed_along(edge, "fine", -1)
    ahead = []
    if small:
        padded = -(-states // LANES) * LANES
        obs = obs_value.shape[1]
        info, pull = call(
            observe_kernel,
            (near(REG_DEV, states, padded), near(REG_DEV, states, LANES)),
            [VMEM] * 5,
            cost=pl.CostEstimate(
                flops=12 * REG_DEV * padded * padded * obs, bytes_accessed=1 << 20, transcendentals=0
            ),
        )(kept(live), *(kept(array) for array in seen))
        ahead = [kept(pull)]
    layout = (groups, strips, width)
    span = width + 2 * STEPS
    out = call(
        functools.partial(blocks_kernel, *layout),
        tuple([near(3 * span * (groups // 2) + TILE, LANES)] * strips),
        [VMEM] * (4 + len(ahead)),
    )(kept(pair), kept(single), kept(from_west), kept(from_east), *ahead)
    got = swapped_blocks(out, "region")
    turned = call(
        functools.partial(forecast_kernel, *layout),
        tuple([near(states, LANES)] * groups),
        [VMEM] * strips,
        scratch=[
            pltpu.VMEM((strips, *out[0].shape), jnp.float32),
            pltpu.VMEM((groups, states, LANES), jnp.float32),
        ],
    )(*got)
    got = swapped_blocks(turned, "member")
    back_shape = near(count * BACK_ROWS, LANES)
    gathered = pltpu.VMEM((groups, states, LANES), jnp.float32)
    if small:
        shift, cov = call(
            early_kernel,
            (near(REG_DEV, states, LANES), near(REG_DEV, states, padded)),
            [VMEM] * 2,
            cost=pl.CostEstimate(
                flops=8 * REG_DEV * padded * padded * LANES, bytes_accessed=1 << 18, transcendentals=0
            ),
        )(got[0], got[-1])
        back = call(
            functools.partial(region_kernel, *layout),
            back_shape,
            [VMEM] * (groups + 4),
            scratch=[
                gathered,
                pltpu.VMEM((REG_DEV, states, members), jnp.float32),
                pltpu.VMEM((REG_DEV, states, members), jnp.float32),
            ],
        )(*got, kept(shift), kept(cov), kept(info), kept(pull))
    else:
        x = call(
            functools.partial(collect_kernel, groups),
            f32(REG_DEV, states, members),
            [VMEM] * groups,
            scratch=[gathered],
        )(*got)
        analysis, increment = analyse_in_members(
            x, obs_index, obs_weight, obs_value, obs_var, obs_count
        )
        back = call(
            functools.partial(pack_kernel, *layout), back_shape, [VMEM] * 2
        )(analysis, increment)
    home = exchanged(back, owners, count)
    ana_h, ana_u, ana_v, fine_out = call(
        functools.partial(home_kernel, mem, strips, width),
        (f32(*flat), f32(*flat), f32(*flat), f32(*fine_ctrl.shape)),
        [VMEM, VMEM],
        scratch=[
            *[pltpu.VMEM(flat, jnp.float32)] * 3,
            pltpu.VMEM(fine_ctrl.shape, jnp.float32),
            pltpu.SemaphoreType.DMA((4,)),
        ],
        place=HBM,
    )(kept(home), kept(ctrl))
    shape = (mem, rows, columns)
    return (ana_h.reshape(shape), ana_u.reshape(shape), ana_v.reshape(shape), fine_out)


def solution(mesh):
    strip = P("member", "region", "fine")
    owner = ("member", "region", "fine")
    fine = P(None, "region", "fine", "member")
    return jax.shard_map(
        shards,
        mesh=mesh,
        in_specs=(
            strip,
            strip,
            strip,
            P("region", "fine"),
            P("region", "fine"),
            P(owner, None, None),
            P(owner, None, None),
            P(owner, None),
            P(owner, None),
            P(owner),
            fine,
        ),
        out_specs=(strip, strip, strip, fine),
        check_vma=False,
    )
```

```python
import functools

import jax
import jax.numpy as jnp
from jax import lax
from jax.experimental import pallas as pl
from jax.experimental.pallas import tpu as pltpu
from jax.sharding import PartitionSpec as P


REG_DEV = 2
STEPS = 4
NEWTON = 8
LANES = 128
TILE = 8
HALF = LANES // 2
GRANT = 32 << 20


HIGHEST = lax.Precision.HIGHEST
NT = (((1,), (1,)), ((), ()))
NN = (((1,), (0,)), ((), ()))
VMEM = pl.BlockSpec(memory_space=pltpu.VMEM)
SMEM = pl.BlockSpec(memory_space=pltpu.SMEM)
HBM = pl.BlockSpec(memory_space=pltpu.HBM)


def passed_along(block, axis, distance):
    count = lax.axis_size(axis)
    route = [((i - distance) % count, i) for i in range(count)]
    return lax.ppermute(block, axis, route)


def lane_of(shape):
    return lax.broadcasted_iota(jnp.int32, shape, 1)


def row_of(shape):
    return lax.broadcasted_iota(jnp.int32, shape, 0)


def swapped(tile):
    return pltpu.roll(tile, HALF, 1)


def low_pair(even, odd):
    return jnp.where(lane_of(even.shape) < HALF, even, swapped(odd))


def high_pair(even, odd):
    return jnp.where(lane_of(even.shape) < HALF, swapped(even), odd)


def split(value):
    high = value.astype(jnp.bfloat16)
    return high, (value - high.astype(jnp.float32)).astype(jnp.bfloat16)


def beside(value):
    return jnp.concatenate(split(value), axis=1)


def filled(value, rows):
    if value.shape[0] == rows:
        return value
    return jnp.concatenate([value, jnp.zeros((rows - value.shape[0], value.shape[1]), value.dtype)], axis=0)


def stacked(value):
    both = filled(jnp.concatenate(split(value), axis=1), value.shape[1])
    return jnp.concatenate([both, both], axis=0)


def times(left, right):
    out = lax.dot_general(left, right, NN, preferred_element_type=jnp.float32)
    half = out.shape[1] // 2
    return out[:, :half] + out[:, half:]


def squared(value, columns):
    high, low = split(value)
    both = jnp.concatenate([high, low], axis=0)
    wide = jnp.concatenate([filled(high, columns), filled(low, columns)], axis=0)
    out = lax.dot_general(both, wide, NT, preferred_element_type=jnp.float32)
    out = out[:, :columns] + out[:, columns:]
    half = out.shape[0] // 2
    return out[:half] + out[half:]


def applied_to(left, value):
    columns = left.shape[1]
    wide = beside(left)
    high, low = (filled(part, columns) for part in split(value))
    dot = functools.partial(
        lax.dot_general, dimension_numbers=NN, preferred_element_type=jnp.float32
    )
    return dot(wide, jnp.concatenate([high, high], axis=0)) + dot(wide[:, :columns], low)


BACK_ROWS = 3 * TILE + 1


def edge_kernel(mem, *refs):
    sources, edge_ref, targets, sems = refs[:5], refs[5], refs[6:-1], refs[-1]
    copies = [
        pltpu.make_async_copy(source, target, sems.at[i])
        for i, (source, target) in enumerate(zip(sources, targets))
    ]
    for copy in copies:
        copy.start()
    for copy in copies:
        copy.wait()
    fields, courants = targets[:3], targets[3:]
    tiles = fields[0].shape[0] // mem
    end = (tiles - 1) * LANES

    def outermost(first, last):
        return jnp.where(lane_of(first.shape) < HALF, first, last)

    h, u, v = (
        outermost(ref[pl.ds(0, mem, stride=tiles), :], ref[pl.ds(tiles - 1, mem, stride=tiles), :])
        for ref in fields
    )
    zonal, merid = (
        jnp.broadcast_to(outermost(ref[:, :LANES], ref[:, end:]), (mem // 2, LANES))
        for ref in courants
    )
    late = row_of((TILE, LANES)) >= STEPS
    for i, parts in enumerate(((h, u), (v, zonal, merid))):
        turned = jnp.concatenate(parts, axis=0).T
        both = jnp.where(late, turned[LANES - TILE :], turned[:TILE])
        edge_ref[i] = pltpu.roll(both, STEPS, 0)


def blocks_kernel(groups, strips, width, mem, *refs):
    h_ref, u_ref, v_ref, zonal_ref, merid_ref = refs[:5]
    send_refs, (pair_ref, single_ref) = refs[5 : 5 + strips], refs[5 + strips :]
    tiles = h_ref.shape[0] // mem
    columns = tiles * LANES
    shape = (TILE, LANES)
    zero = jnp.zeros(shape, jnp.float32)
    for ref in (pair_ref, single_ref):
        ref[0:TILE, :] = zero
        ref[columns : columns + TILE, :] = zero
    for t in range(tiles):
        rows = pl.ds(t, mem, stride=tiles)
        lanes = slice(t * LANES, (t + 1) * LANES)
        pair = jnp.concatenate([h_ref[rows, :], u_ref[rows, :]], axis=0)
        zonal = jnp.broadcast_to(zonal_ref[:, lanes], (mem // 2, LANES))
        merid = jnp.broadcast_to(merid_ref[:, lanes], (mem // 2, LANES))
        single = jnp.concatenate([v_ref[rows, :], zonal, merid], axis=0)
        place = slice(STEPS + t * LANES, STEPS + (t + 1) * LANES)
        pair_ref[place, :] = pair.T
        single_ref[place, :] = single.T
    me = lax.axis_index("region")
    part = lane_of(shape) % (HALF // 2)
    span = 3 * TILE
    for s, send_ref in enumerate(send_refs):
        owner = me ^ s
        courant = zero
        for p in range(groups // 2):
            for j in range(3):
                pairs, singles = [], []
                for group in (2 * p, 2 * p + 1):
                    start = pl.multiple_of(width * (group * strips + owner) + TILE * j, TILE)
                    pairs.append(pair_ref[pl.ds(start, TILE), :])
                    singles.append(single_ref[pl.ds(start, TILE), :])
                    courant = jnp.where(part == 3 * group + j, singles[-1], courant)
                place = 3 * span * p + TILE * j
                send_ref[place : place + TILE, :] = low_pair(*pairs)
                send_ref[place + span : place + span + TILE, :] = high_pair(*pairs)
                send_ref[place + 2 * span : place + 2 * span + TILE, :] = low_pair(*singles)
        place = 3 * span * (groups // 2)
        send_ref[place : place + TILE, :] = courant


def wrap_kernel(groups, strips, west_ref, east_ref, *refs):
    block_refs, send_refs = refs[:strips], refs[-strips:]
    me = lax.axis_index("region")
    shape = (TILE, LANES)
    early = row_of(shape) < STEPS
    low = lane_of(shape) < HALF
    part = lane_of(shape) % (HALF // 2)
    span = 3 * TILE
    end = 3 * span * (groups // 2)
    west = (west_ref[0], swapped(west_ref[0]), west_ref[1])
    east = (swapped(east_ref[0]), east_ref[0], swapped(east_ref[1]))
    for s in range(strips):
        first, last = early & (me ^ s == 0), ~early & (me ^ s == strips - 1)
        for i in range(3):
            for place, mask, value in (
                (span * i, first & low, west[i]),
                (end - 3 * span + span * i + 2 * TILE, last & ~low, east[i]),
            ):
                tile = block_refs[s][place : place + TILE, :]
                send_refs[s][place : place + TILE, :] = jnp.where(mask, value, tile)
        tile = block_refs[s][end : end + TILE, :]
        tile = jnp.where(first & ~low & (part == 0), west_ref[1], tile)
        tile = jnp.where(last & ~low & (part == 3 * groups - 1), east_ref[1], tile)
        send_refs[s][end : end + TILE, :] = tile


def forecast_kernel(groups, strips, width, *refs):
    got_refs, refs = refs[:strips], refs[strips:]
    send_refs, (got_ref, turned_ref) = refs[:groups], refs[groups:]
    span = width + 2 * STEPS
    per_region = strips // REG_DEV
    cells = per_region * width
    me = lax.axis_index("region")
    for s, ref in enumerate(got_refs):
        got_ref[me ^ s] = ref[...]
    low = lane_of((TILE, LANES)) < HALF
    tail = 3 * span * (groups // 2)
    for p in range(groups // 2):

        def field(r, i):
            return got_ref[r, 3 * span * p + span * i : 3 * span * p + span * (i + 1), :]

        def courant(r, first):
            mixed = got_ref[r, tail : tail + TILE, :]
            parts = []
            for j in range(3):
                even, odd = first + 6 * p + j, first + 6 * p + 3 + j
                parts.append(jnp.take_along_axis(mixed, jnp.where(low, even, odd), axis=1))
            return jnp.concatenate(parts, axis=0)

        h = [field(r, 0) for r in range(strips)]
        u = [field(r, 1) for r in range(strips)]
        v = [field(r, 2) for r in range(strips)]
        zonal = [courant(r, HALF) for r in range(strips)]
        merid = [courant(r, HALF + HALF // 2) for r in range(strips)]
        for _ in range(STEPS):
            flux_v = [merid[r] * v[r] for r in range(strips)]
            for r in range(strips):
                flux_u = zonal[r] * u[r]
                south = flux_v[r - 1] if r else jnp.zeros_like(flux_u)
                h[r] = h[r] - (flux_u - pltpu.roll(flux_u, 1, 0) + flux_v[r] - south)
            for r in range(strips):
                north = h[r + 1] if r + 1 < strips else jnp.zeros_like(h[r])
                u[r] = u[r] - (pltpu.roll(h[r], span - 1, 0) - h[r])
                v[r] = v[r] - (north - h[r])
        for i, state in enumerate((h, u, v)):
            inner = [pltpu.roll(state[r], span - STEPS, 0)[:width] for r in range(strips)]
            for s in range(per_region):
                lower, upper = inner[s], inner[per_region + s]
                place = slice(i * cells + s * width, i * cells + (s + 1) * width)
                turned_ref[2 * p, place, :] = low_pair(lower, upper)
                turned_ref[2 * p + 1, place, :] = high_pair(lower, upper)
    mine = lax.axis_index("member")
    for s, ref in enumerate(send_refs):
        ref[...] = turned_ref[mine ^ s]


def regions_of(even, odd):
    return [low_pair(even, odd), high_pair(even, odd)]


def early_kernel(even_ref, odd_ref, shift_ref, cov_ref):
    for q, tile in enumerate(regions_of(even_ref[...], odd_ref[...])):
        shift = jnp.sum(tile, axis=1, keepdims=True) / LANES
        shift_ref[q] = jnp.broadcast_to(shift, shift_ref.shape[1:])
        cov_ref[q] = squared(tile - shift, cov_ref.shape[2])


def collect(got_refs, all_ref, x_ref):
    mine = lax.axis_index("member")
    for s, ref in enumerate(got_refs):
        all_ref[mine ^ s] = ref[...]
    for p in range(len(got_refs) // 2):
        even, odd = all_ref[2 * p], all_ref[2 * p + 1]
        lanes = slice(p * LANES, (p + 1) * LANES)
        for q, tile in enumerate(regions_of(even, odd)):
            x_ref[q, :, lanes] = tile


def observe_kernel(count_ref, index_ref, weight_ref, value_ref, var_ref, ctrl_ref, *refs):
    info_ref, pull_ref, near_ref = refs
    near_ref[...] = ctrl_ref[...]
    states, padded = info_ref.shape[1:]
    obs = index_ref.shape[2]
    for q in range(REG_DEV):
        state = row_of((states, obs))
        operator = jnp.zeros((states, obs), jnp.float32)
        for j in range(index_ref.shape[1]):
            hit = state == index_ref[q, j : j + 1, :]
            operator = operator + jnp.where(hit, weight_ref[q, j : j + 1, :], 0.0)
        live = lane_of((1, obs)) < count_ref[q]
        inverse = jnp.where(live, 1.0 / var_ref[q : q + 1, :], 0.0)
        scaled = operator * inverse
        info_ref[q] = lax.dot_general(
            scaled,
            filled(operator, padded),
            NT,
            precision=HIGHEST,
            preferred_element_type=jnp.float32,
        )
        pulled = jnp.sum(scaled * value_ref[q : q + 1, :], axis=1, keepdims=True)
        pull_ref[q] = jnp.broadcast_to(pulled, (states, LANES))


def analyse(members, rest, fill, x_ref, shift_ref, cov_ref, info_ref, pull_ref, out_ref):
    states, padded = info_ref.shape[1:]
    square = (states, padded)
    diagonal = row_of(square) == lane_of(square)
    identity = jnp.where(diagonal, 1.0, 0.0)
    regions = range(REG_DEV)
    scale = 1.0 / (members - 1)

    def as_row(column):
        return jnp.sum(jnp.where(diagonal, column, 0.0), axis=0, keepdims=True)

    def applied(matrix, row):
        return jnp.sum(matrix * row, axis=1, keepdims=True)

    shifts = [shift_ref[q][:, 0:1] for q in regions]
    later = [rest[q] - shifts[q] for q in regions]
    covs = [cov_ref[q] + squared(later[q], padded) for q in regions]
    moves = [jnp.sum(later[q], axis=1, keepdims=True) / members for q in regions]
    covs = [covs[q] - members * (moves[q] * as_row(moves[q])) for q in regions]
    means = [shifts[q] + moves[q] for q in regions]
    gains = [times(beside(covs[q]), stacked(info_ref[q] * scale)) for q in regions]
    rights = [stacked(gains[q]) for q in regions]
    gains_2 = [times(beside(gains[q]), rights[q]) for q in regions]
    fill()
    pulls, inverse_norms, iterates, inverses = [], [], [], []
    for q in regions:
        pulled = pull_ref[q][:, 0:1] - applied(info_ref[q], as_row(means[q]))
        pulls.append(jnp.sum(covs[q] * pulled, axis=0, keepdims=True))
        trace = jnp.sum(jnp.where(diagonal, gains_2[q] + 2.0 * gains[q], 0.0), keepdims=True)
        inverse_norms.append(lax.rsqrt(trace + members))
    for q in regions:
        norm = inverse_norms[q]
        first = (identity + gains[q]) * norm
        second = (identity + 2.0 * gains[q] + gains_2[q]) * (norm * norm)
        third = (second + times(beside(second), rights[q])) * norm
        inverses.append(1.5 * identity - 0.5 * first)
        iterates.append(2.25 * first - 1.5 * second + 0.25 * third)
    for _ in range(1, NEWTON - 1):
        rights = [stacked(iterates[q]) for q in regions]
        seconds = [times(beside(iterates[q]), rights[q]) for q in regions]
        inverses = [
            1.5 * inverses[q] - 0.5 * times(beside(inverses[q]), rights[q]) for q in regions
        ]
        thirds = [times(beside(seconds[q]), rights[q]) for q in regions]
        iterates = [
            2.25 * iterates[q] - 1.5 * seconds[q] + 0.25 * thirds[q] for q in regions
        ]
    increments = []
    for q in regions:
        moved = applied_to(inverses[q], x_ref[q] - means[q])
        twice = applied(inverses[q], as_row(applied(inverses[q], pulls[q])))
        factor = 1.5 * identity - 0.5 * iterates[q]
        twice = applied(factor, as_row(applied(factor, as_row(twice))))
        increment = twice * (inverse_norms[q] * scale)
        increments.append(increment)
        moved = applied_to(factor, moved * jnp.sqrt(inverse_norms[q]))
        out_ref[q] = moved + (means[q] + increment)
    return increments


def pack(groups, strips, width, ana_ref, increments, send_ref):
    per_region = strips // REG_DEV
    cells = per_region * width
    states = increments[0].shape[0]
    state = row_of((states, LANES))
    lane = lane_of((states, LANES))
    for r in range(strips):
        q, s = divmod(r, per_region)
        wanted = (lane // width) * cells + s * width + lane % width
        hit = (state == wanted) & (lane < 3 * width)
        row = jnp.sum(jnp.where(hit, increments[q], 0.0), axis=0, keepdims=True)
        for group in range(groups):
            block = group * strips + r
            lanes = slice((group // 2) * LANES, (group // 2 + 1) * LANES)
            pair = high_pair if group % 2 else low_pair
            for i in range(3):
                first = i * cells + s * width
                tile = pair(
                    ana_ref[q, first : first + TILE, lanes],
                    ana_ref[q, first + TILE : first + 2 * TILE, lanes],
                )
                send_ref[BACK_ROWS * block + TILE * i : BACK_ROWS * block + TILE * (i + 1), :] = tile
            send_ref[BACK_ROWS * (block + 1) - 1 : BACK_ROWS * (block + 1), :] = row


def region_kernel(groups, strips, width, *refs):
    got_refs, refs = refs[:groups], refs[groups:]
    shift_ref, cov_ref, info_ref, pull_ref, send_ref, all_ref, x_ref, ana_ref = refs
    pairs = [
        regions_of(got_refs[s][...], got_refs[s - 1][...]) for s in range(groups - 2, 0, -2)
    ]
    rest = [jnp.concatenate([pair[q] for pair in pairs], axis=1) for q in range(REG_DEV)]
    fill = functools.partial(collect, got_refs, all_ref, x_ref)
    increments = analyse(
        x_ref.shape[2], rest, fill, x_ref, shift_ref, cov_ref, info_ref, pull_ref, ana_ref
    )
    pack(groups, strips, width, ana_ref, increments, send_ref)


def home_kernel(mem, strips, width, got_ref, ctrl_ref, *refs):
    targets, (h_ref, u_ref, v_ref, fine_ref, sems) = refs[:4], refs[4:]
    copies = [
        pltpu.make_async_copy(source, target, sems.at[i])
        for i, (source, target) in enumerate(zip((h_ref, u_ref, v_ref, fine_ref), targets))
    ]
    tiles = got_ref.shape[0] // BACK_ROWS * width // LANES
    per_tile = LANES // width
    for i, out_ref in enumerate((h_ref, u_ref, v_ref)):
        for t in range(0, tiles, 2):
            rows = []
            for k in range(per_tile):
                first = BACK_ROWS * (t * per_tile + k) + TILE * i
                even = got_ref[first : first + TILE, :]
                first += BACK_ROWS * per_tile
                odd = got_ref[first : first + TILE, :]
                rows += [low_pair(even, odd), high_pair(even, odd)]
            turned = jnp.concatenate(rows, axis=0).T
            out_ref[pl.ds(t, mem, stride=tiles), :] = turned[:mem]
            out_ref[pl.ds(t + 1, mem, stride=tiles), :] = turned[mem:]
        copies[i].start()
    mine = lax.axis_index("member") * strips
    per_fine = LANES // (2 * width)
    row = row_of((width, LANES))
    lane = lane_of((width, LANES))
    for t in range(ctrl_ref.shape[3] // LANES):
        rows = [
            got_ref[pl.ds(BACK_ROWS * (mine + t * per_fine + b) + BACK_ROWS - 1, 1), :]
            for b in range(per_fine)
        ]
        columns = [jnp.broadcast_to(r, (LANES, LANES)).T[:, 0:1] for r in rows]
        for i in range(3):
            total = jnp.zeros((1, LANES), jnp.float32)
            for b in range(per_fine):
                hit = ((lane // 2) % width == row) & (lane // (2 * width) == b)
                part = jnp.where(hit, columns[b][i * width : (i + 1) * width], 0.0)
                total = total + jnp.sum(part, axis=0, keepdims=True)
            lanes = slice(t * LANES, (t + 1) * LANES)
            for e in range(2):
                fine_ref[i, e, :, lanes] = ctrl_ref[i, e, :, lanes] + total
    copies[3].start()
    for copy in copies:
        copy.wait()


def collect_kernel(groups, *refs):
    collect(refs[:groups], refs[-1], refs[-2])


def pack_kernel(groups, strips, width, ana_ref, inc_ref, send_ref):
    pack(groups, strips, width, ana_ref, [inc_ref[q] for q in range(REG_DEV)], send_ref)


def analyse_in_members(x, obs_index, obs_weight, obs_value, obs_var, obs_count):
    states, members = x.shape[1:]
    mean_state = jnp.mean(x, axis=2, keepdims=True)
    spread = x - mean_state
    picks = (obs_index[:, :, :, None] == jnp.arange(states)).astype(jnp.float32)
    operator = jnp.sum(picks * obs_weight[:, :, :, None], axis=2)
    predicted = jnp.einsum("ros,rsk->rko", operator, x, precision=HIGHEST)
    mean_obs = jnp.mean(predicted, axis=1, keepdims=True)
    obs_spread = predicted - mean_obs
    active_obs = jnp.arange(obs_value.shape[1])[None, :] < obs_count[:, None]
    weighted = obs_spread * (active_obs.astype(jnp.float32) / obs_var)[:, None, :]
    gram_sum = jnp.einsum("rko,rjo->rkj", weighted, obs_spread, precision=HIGHEST)
    identity = jnp.eye(members, dtype=jnp.float32)
    scaled = identity + gram_sum / (members - 1)
    frobenius = jnp.sqrt(jnp.sum(scaled * scaled, axis=(1, 2), keepdims=True))
    iterate = scaled / frobenius
    inverse_root = jnp.broadcast_to(identity, scaled.shape)
    dot = functools.partial(jnp.einsum, "rij,rjk->rik", precision=HIGHEST)
    for _ in range(NEWTON):
        factor = 1.5 * identity - 0.5 * dot(inverse_root, iterate)
        iterate = dot(iterate, factor)
        inverse_root = dot(factor, inverse_root)
    transform = inverse_root / jnp.sqrt(frobenius)
    innovation = jnp.einsum(
        "rko,ro->rk", weighted, obs_value - mean_obs[:, 0], precision=HIGHEST
    )
    halfway = jnp.einsum("rkj,rj->rk", transform, innovation, precision=HIGHEST)
    mean_weights = jnp.einsum("rkj,rj->rk", transform, halfway, precision=HIGHEST) / (members - 1)
    increment = jnp.einsum("rk,rsk->rs", mean_weights, spread, precision=HIGHEST)[:, :, None]
    moved = jnp.einsum("rjk,rsj->rsk", transform, spread, precision=HIGHEST)
    return mean_state + increment + moved, increment


def call(kernel, out_shape, specs, scratch=(), cost=None, place=VMEM, aliases=None):
    many = isinstance(out_shape, tuple)
    return pl.pallas_call(
        kernel,
        out_shape=out_shape,
        in_specs=specs,
        out_specs=tuple(place for _ in out_shape) if many else place,
        scratch_shapes=scratch,
        cost_estimate=cost,
        input_output_aliases=aliases or {},
        compiler_params=pltpu.CompilerParams(vmem_limit_bytes=GRANT),
    )


def swapped_blocks(blocks, axis):
    count = len(blocks)
    if count <= 4:
        routes = [[(i, i ^ s) for i in range(count)] for s in range(count)]
        moved = []
        for s in range(1, count):
            moved.append(lax.ppermute(blocks[s], axis, routes[s]))
        return [kept(block) for block in [blocks[0], *moved]]
    order = lax.axis_index(axis) ^ jnp.arange(count)
    moved = lax.all_to_all(jnp.stack(blocks)[order], axis, split_axis=0, concat_axis=0, tiled=True)
    return [kept(block) for block in moved[order]]


def exchanged(blocks, axes, count):
    dense = blocks.reshape(count, -1, 1, LANES)
    return lax.all_to_all(dense, axes, split_axis=0, concat_axis=0, tiled=True).reshape(blocks.shape)


def f32(*shape):
    return jax.ShapeDtypeStruct(shape, jnp.float32)


def near(*shape):
    return pltpu.VMEM(shape, jnp.float32)


def far(array):
    return pltpu.with_memory_space_constraint(array, pltpu.HBM)


def kept(array):
    return pltpu.with_memory_space_constraint(array, pltpu.VMEM)


def shards(
    sample_surface_elevation,
    sample_zonal_current,
    sample_meridional_current,
    zonal_edge_layer_courant,
    meridional_edge_layer_courant,
    obs_index,
    obs_weight,
    obs_value,
    obs_var,
    obs_count,
    fine_ctrl,
):
    groups = lax.axis_size("member")
    strips = lax.axis_size("region")
    owners = ("member", "region")
    mem, rows, columns = sample_surface_elevation.shape
    count = groups * strips
    width = columns // count
    members = groups * mem
    assert rows == 1 and 2 * mem == LANES and width == 2 * TILE and STEPS * 2 == TILE
    assert columns % (2 * LANES) == 0 and strips % REG_DEV == 0 and REG_DEV == 2
    assert all(size > 1 and size & (size - 1) == 0 for size in (groups, strips))
    assert 3 * groups <= HALF // 2
    flat = (mem * columns // LANES, LANES)
    states = 3 * width * strips // REG_DEV
    small = states <= members and groups > 2
    inputs = [
        sample_surface_elevation.reshape(flat),
        sample_zonal_current.reshape(flat),
        sample_meridional_current.reshape(flat),
        zonal_edge_layer_courant,
        meridional_edge_layer_courant,
    ]
    edge, *taken = call(
        functools.partial(edge_kernel, mem),
        (near(2, TILE, LANES), *(near(*array.shape) for array in inputs)),
        [HBM] * len(inputs),
        scratch=[pltpu.SemaphoreType.DMA((len(inputs),))],
    )(*(far(array) for array in inputs))
    from_west = passed_along(edge, "fine", 1)
    from_east = from_west if lax.axis_size("fine") == 2 else passed_along(edge, "fine", -1)
    ctrl = fine_ctrl
    if small:
        padded = -(-states // LANES) * LANES
        obs = obs_value.shape[1]
        info, pull, ctrl = call(
            observe_kernel,
            (
                near(REG_DEV, states, padded),
                near(REG_DEV, states, LANES),
                near(*fine_ctrl.shape),
            ),
            [SMEM] + [VMEM] * 5,
            cost=pl.CostEstimate(
                flops=12 * REG_DEV * padded * padded * obs, bytes_accessed=1 << 20, transcendentals=0
            ),
        )(
            far(obs_count),
            far(obs_index.transpose(0, 2, 1)),
            far(obs_weight.transpose(0, 2, 1)),
            far(obs_value),
            far(obs_var),
            far(fine_ctrl),
        )
    layout = (groups, strips, width)
    span = width + 2 * STEPS
    blocks = tuple([near(3 * span * (groups // 2) + TILE, LANES)] * strips)
    out = call(
        functools.partial(blocks_kernel, *layout, mem),
        blocks,
        [VMEM] * 5,
        scratch=[pltpu.VMEM((columns + TILE, LANES), jnp.float32)] * 2,
        cost=pl.CostEstimate(flops=1 << 20, bytes_accessed=1 << 20, transcendentals=0),
    )(*(kept(array) for array in taken))
    out = call(
        functools.partial(wrap_kernel, groups, strips),
        blocks,
        [VMEM] * (2 + strips),
        aliases={2 + s: s for s in range(strips)},
    )(kept(from_west), kept(from_east), *(kept(block) for block in out))
    got = swapped_blocks(out, "region")
    turned = call(
        functools.partial(forecast_kernel, *layout),
        tuple([near(states, LANES)] * groups),
        [VMEM] * strips,
        scratch=[
            pltpu.VMEM((strips, *out[0].shape), jnp.float32),
            pltpu.VMEM((groups, states, LANES), jnp.float32),
        ],
    )(*got)
    got = swapped_blocks(turned, "member")
    back_shape = near(count * BACK_ROWS, LANES)
    gathered = pltpu.VMEM((groups, states, LANES), jnp.float32)
    if small:
        shift, cov = call(
            early_kernel,
            (near(REG_DEV, states, LANES), near(REG_DEV, states, padded)),
            [VMEM] * 2,
            cost=pl.CostEstimate(
                flops=8 * REG_DEV * padded * padded * LANES, bytes_accessed=1 << 18, transcendentals=0
            ),
        )(got[0], got[-1])
        back = call(
            functools.partial(region_kernel, *layout),
            back_shape,
            [VMEM] * (groups + 4),
            scratch=[
                gathered,
                pltpu.VMEM((REG_DEV, states, members), jnp.float32),
                pltpu.VMEM((REG_DEV, states, members), jnp.float32),
            ],
        )(*got, kept(shift), kept(cov), kept(info), kept(pull))
    else:
        x = call(
            functools.partial(collect_kernel, groups),
            f32(REG_DEV, states, members),
            [VMEM] * groups,
            scratch=[gathered],
        )(*got)
        analysis, increment = analyse_in_members(
            x, obs_index, obs_weight, obs_value, obs_var, obs_count
        )
        back = call(
            functools.partial(pack_kernel, *layout), back_shape, [VMEM] * 2
        )(analysis, increment)
    home = exchanged(back, owners, count)
    ana_h, ana_u, ana_v, fine_out = call(
        functools.partial(home_kernel, mem, strips, width),
        (f32(*flat), f32(*flat), f32(*flat), f32(*fine_ctrl.shape)),
        [VMEM, VMEM],
        scratch=[
            *[pltpu.VMEM(flat, jnp.float32)] * 3,
            pltpu.VMEM(fine_ctrl.shape, jnp.float32),
            pltpu.SemaphoreType.DMA((4,)),
        ],
        place=HBM,
    )(kept(home), kept(ctrl))
    shape = (mem, rows, columns)
    return (ana_h.reshape(shape), ana_u.reshape(shape), ana_v.reshape(shape), fine_out)


def solution(mesh):
    strip = P("member", "region", "fine")
    owner = ("member", "region", "fine")
    fine = P(None, "region", "fine", "member")
    return jax.shard_map(
        shards,
        mesh=mesh,
        in_specs=(
            strip,
            strip,
            strip,
            P("region", "fine"),
            P("region", "fine"),
            P(owner, None, None),
            P(owner, None, None),
            P(owner, None),
            P(owner, None),
            P(owner),
            fine,
        ),
        out_specs=(strip, strip, strip, fine),
        check_vma=False,
    )
```
